32 devices in a mesh: fsdp: 4 (over y, core), ctx: 8 (over z, x).
Axes of the slice: x: 2, y: 2, z: 4, core: 2. Of those that a mesh axis runs over, the one named last changes fastest.
Arguments:
- inputs: bfloat16 [4, 1024, 768], P('fsdp', 'ctx'), may hold values from -6 to 6
- lengths: int32 [4], P('fsdp'), may hold values from 512 to 1024, as said below
- ln1_gain: bfloat16 [768], P('fsdp'), may hold values from 0.25 to 1.75
- ln1_bias: bfloat16 [768], P('fsdp'), may hold values from -1.75 to 1.75
- qkv_weight: bfloat16 [768, 2304], P('fsdp'), may hold values from -0.3125 to 0.3125
- qv_bias: bfloat16 [1536], P('fsdp'), may hold values from -1.75 to 1.75
- out_weight: bfloat16 [768, 768], P('fsdp'), may hold values from -0.625 to 0.625
- out_bias: bfloat16 [768], P('fsdp'), may hold values from -1.75 to 1.75
- ln2_gain: bfloat16 [768], P('fsdp'), may hold values from 0.25 to 1.75
- ln2_bias: bfloat16 [768], P('fsdp'), may hold values from -1.75 to 1.75
- fc_weight: bfloat16 [768, 3072], P('fsdp'), may hold values from -0.21875 to 0.21875
- fc_bias: bfloat16 [3072], P('fsdp'), may hold values from -1.75 to 1.75
- proj_weight: bfloat16 [3072, 768], P('fsdp'), may hold values from -0.109375 to 0.109375
- proj_bias: bfloat16 [768], P('fsdp'), may hold values from -1.75 to 1.75
- cotangent: bfloat16 [4, 1024, 768], P('fsdp', 'ctx'), may hold values from -6 to 6
Outputs:
- outputs: bfloat16 [4, 1024, 768], P('fsdp', 'ctx')
- input_grad: bfloat16 [4, 1024, 768], P('fsdp', 'ctx')
- grad_ln1_gain: float32 [768], P('fsdp')
- grad_ln1_bias: float32 [768], P('fsdp')
- grad_qkv_weight: float32 [768, 2304], P('fsdp')
- grad_qv_bias: float32 [1536], P('fsdp')
- grad_out_weight: float32 [768, 768], P('fsdp')
- grad_out_bias: float32 [768], P('fsdp')
- grad_ln2_gain: float32 [768], P('fsdp')
- grad_ln2_bias: float32 [768], P('fsdp')
- grad_fc_weight: float32 [768, 3072], P('fsdp')
- grad_fc_bias: float32 [3072], P('fsdp')
- grad_proj_weight: float32 [3072, 768], P('fsdp')
- grad_proj_bias: float32 [768], P('fsdp')
The draws below stay inside these ranges and needn't reach their ends.
Inputs may be any that keep to these rules, and one draw needn't show every extreme that they name: Sequence s holds tokens at its first lengths[s] positions and padding after them; in every draw some sequence fills its whole slot of 1024.
All inputs are finite; a program needn't handle non-finite values.
Results may differ from the reference program's by a relative error of at most 0.02.
Values may be sent and summed in bfloat16 or wider, within the bound.
No kernel may reach another device: no remote copies, remote signals or barrier semaphores. Data moves between devices by JAX's collectives and lax.ppermute only.
A program may use at most 128 MiB of HBM per device.

```python
import math
import jax
import jax.numpy as jnp
from jax import lax

D = 768
HEADS = 12
HD = 64
FF = 3072
SLOT = 1024
SEQUENCES = 4


def draw_lengths(key, part):
    first_key, second_key = jax.random.split(jax.random.fold_in(key, 11))
    lengths_drawn = jax.random.randint(first_key, (SEQUENCES,), SLOT // 2, SLOT + 1)
    picked_index = jax.random.randint(second_key, (), 0, SEQUENCES)
    return jnp.where(lax_free_iota(SEQUENCES) == picked_index, SLOT, lengths_drawn).astype(jnp.int32)


def lax_free_iota(total_count):
    return jnp.arange(total_count, dtype=jnp.int32)


def levels(stream_key, dims, cuts, least, largest):
    factor_of, own = 1.0, jax.random.fold_in(stream_key, 6)
    for dim, parts in cuts:
        heights = jnp.exp(jax.random.uniform(jax.random.fold_in(own, dim), (parts,), jnp.float32, least / len(cuts), largest / len(cuts)))
        factor_of = factor_of * jnp.repeat(heights, dims[dim] // parts).reshape([-1 if axis == dim else 1 for axis in range(len(dims))])
    return factor_of


def noise(key, dims, spread, limit, pieces=(), kind=jnp.bfloat16):
    drawn = jax.random.normal(key, dims, jnp.float32) * spread
    if len(pieces) > 0:
        drawn = levels(key, dims, pieces, -0.22, 0.18) * drawn
    return jnp.clip(drawn, min=-limit, max=limit).astype(kind)


def setup_inputs(seed: int = 0) -> dict:
    key_of = jax.random.split(jax.random.key(seed), 16)
    inputs = noise(key_of[0], (SEQUENCES, SLOT, D), 1.0, 6.0, ((0, 4), (1, 8)))
    lengths = draw_lengths(jax.random.fold_in(key_of[15], 71), 0)
    ln1_gain = jnp.clip(1.0 + 0.15 * jax.random.normal(key_of[2], (D,), jnp.float32), 0.25, 1.75).astype(jnp.bfloat16)
    ln1_bias = noise(key_of[3], (D,), 0.3, 1.75, ((0, 4),))
    qkv_weight = noise(key_of[4], (D, 3 * D), (D // 2) ** -0.5, 0.3125, ((0, 4),))
    qv_bias = noise(key_of[5], (2 * D,), 0.3, 1.75, ((0, 4),))
    out_weight = noise(key_of[6], (D, D), (D // 8) ** -0.5, 0.625, ((0, 4),))
    out_bias = noise(key_of[7], (D,), 0.3, 1.75, ((0, 4),))
    ln2_gain = jnp.clip(1.0 + 0.15 * jax.random.normal(key_of[8], (D,), jnp.float32), 0.25, 1.75).astype(jnp.bfloat16)
    ln2_bias = noise(key_of[9], (D,), 0.3, 1.75, ((0, 4),))
    fc_weight = noise(key_of[10], (D, FF), D ** -0.5, 0.21875, ((0, 4),))
    fc_bias = noise(key_of[11], (FF,), 0.3, 1.75, ((0, 4),))
    proj_weight = noise(key_of[12], (FF, D), FF ** -0.5, 0.109375, ((0, 4),))
    proj_bias = noise(key_of[13], (D,), 0.3, 1.75, ((0, 4),))
    cotangent = noise(key_of[14], (SEQUENCES, SLOT, D), 1.0, 6.0, ((0, 4), (1, 8)))
    return {"inputs": inputs, "lengths": lengths, "ln1_gain": ln1_gain, "ln1_bias": ln1_bias, "qkv_weight": qkv_weight, "qv_bias": qv_bias, "out_weight": out_weight, "out_bias": out_bias, "ln2_gain": ln2_gain, "ln2_bias": ln2_bias, "fc_weight": fc_weight, "fc_bias": fc_bias, "proj_weight": proj_weight, "proj_bias": proj_bias, "cotangent": cotangent}


EPSILON = 1e-05
NEGATIVE = -1e+30
GELU_COEF = 0.7978845608028654

@jax.custom_vjp
def low(v):
    return lax.optimization_barrier(v.astype(jnp.bfloat16)).astype(jnp.float32)

@jax.custom_vjp
def low_back(v):
    return v

def low_keep(v):
    return (low(v), None)

def low_pass(kept, grad):
    return (grad,)

def back_keep(v):
    return (v, None)

def back_low(kept, grad):
    return (low(grad),)
low.defvjp(low_keep, low_pass)
low_back.defvjp(back_keep, back_low)

def gelu_tanh(values):
    return 0.5 * values * (1.0 + jnp.tanh(GELU_COEF * (values + 0.044715 * values * values * values)))

def layer_norm(values, ln_gain, ln_shift):
    centred = values - lax.optimization_barrier(jnp.mean(values, axis=-1, keepdims=True))
    variance = lax.optimization_barrier(jnp.mean(centred * centred, axis=-1, keepdims=True))
    return centred * lax.rsqrt(variance + EPSILON) * ln_gain + ln_shift

def matmul(left_side, right_side):
    return jnp.dot(left_side, right_side, precision=lax.Precision.HIGHEST, preferred_element_type=jnp.float32)

def one_sequence(params, tokens, length):
    ln1_gain, ln1_bias, qkv_weight, qv_bias, out_weight, out_bias, ln2_gain, ln2_bias, fc_weight, fc_bias, proj_weight, proj_bias = params
    places = lax.iota(jnp.int32, SLOT)
    valid_keys = places < length
    normed = low(layer_norm(tokens, ln1_gain, ln1_bias))
    full_bias = jnp.concatenate([qv_bias[:D], jnp.zeros((D,), jnp.float32), qv_bias[D:]])
    projected = low(low_back(matmul(normed, qkv_weight) + full_bias))
    queries = projected[:, :D].reshape(SLOT, HEADS, HD)
    keys_all = projected[:, D:2 * D].reshape(SLOT, HEADS, HD)
    values_all = projected[:, 2 * D:].reshape(SLOT, HEADS, HD)
    query_rows = math.gcd(SLOT, 512)

    def attend(block_start):
        query_block = lax.dynamic_slice_in_dim(queries, block_start, query_rows, 0)
        query_places = block_start + lax.iota(jnp.int32, query_rows)
        scores = jnp.einsum('qhd,khd->hqk', query_block, keys_all, precision=lax.Precision.HIGHEST) * 0.125
        scores = low_back(scores)
        allowed = (places[None, :] <= query_places[:, None]) & valid_keys[None, :]
        scores = jnp.where(allowed[None], scores, NEGATIVE)
        row_top = lax.optimization_barrier(jnp.max(scores, axis=-1, keepdims=True))
        weights = jnp.exp(scores - row_top)
        row_total = lax.optimization_barrier(jnp.sum(weights, axis=-1))
        attended = jnp.einsum('hqk,khd->qhd', low(weights), values_all, precision=lax.Precision.HIGHEST)
        return attended / jnp.transpose(row_total)[:, :, None]
    starts = lax.iota(jnp.int32, SLOT // query_rows) * query_rows
    attended = lax.map(jax.checkpoint(attend), starts).reshape(SLOT, D)
    attended = low(low_back(attended))
    branch = low_back(matmul(attended, out_weight) + out_bias)
    residual = tokens + branch
    normed_two = low(layer_norm(residual, ln2_gain, ln2_bias))
    hidden = low_back(matmul(normed_two, fc_weight) + fc_bias)
    active = low(gelu_tanh(hidden))
    result = low_back(matmul(active, proj_weight) + proj_bias)
    return jnp.where(valid_keys[:, None], residual + result, 0.0)

def forward(params, inputs_all, lengths):

    def per_sequence(scan_carry, sequence_item):
        return (scan_carry, one_sequence(params, sequence_item[0], sequence_item[1]))
    return lax.scan(per_sequence, jnp.zeros((), jnp.float32), (inputs_all, lengths))[1]

def reference(inputs, lengths, ln1_gain, ln1_bias, qkv_weight, qv_bias, out_weight, out_bias, ln2_gain, ln2_bias, fc_weight, fc_bias, proj_weight, proj_bias, cotangent):
    params = tuple([weight_array.astype(jnp.float32) for weight_array in (ln1_gain, ln1_bias, qkv_weight, qv_bias, out_weight, out_bias, ln2_gain, ln2_bias, fc_weight, fc_bias, proj_weight, proj_bias)])
    outputs, pullback = jax.vjp(lambda weight_set, token_set: forward(weight_set, token_set, lengths), params, inputs.astype(jnp.float32))
    weight_grads, input_grad = pullback(cotangent.astype(jnp.float32))
    return (outputs.astype(jnp.bfloat16), input_grad.astype(jnp.bfloat16), weight_grads[0], weight_grads[1], weight_grads[2], weight_grads[3], weight_grads[4], weight_grads[5], weight_grads[6], weight_grads[7], weight_grads[8], weight_grads[9], weight_grads[10], weight_grads[11])
```

```python
import jax
import jax.numpy as jnp
from jax import lax
from jax.experimental import pallas as pl
from jax.experimental.pallas import tpu as pltpu
from jax.sharding import PartitionSpec as P

HD = 64
EPSILON = 1e-05
NEGATIVE = -1e30
GELU_COEF = 0.7978845608028654
CUBE = 0.044715
F32 = jnp.float32
BF16 = jnp.bfloat16
WAYS = 4
PIECES = 8


def f_xor(x, k):
    n = lax.axis_size("fsdp")
    return lax.ppermute(x, "fsdp", [(i, i ^ k) for i in range(n)])


def c_xor(x, k):
    n = lax.axis_size("ctx")
    return lax.ppermute(x, "ctx", [(i, i ^ k) for i in range(n)])


def swap_layout(x):
    group = lax.axis_size("ctx")
    members = group // WAYS
    perm = []
    for f in range(WAYS):
        for c in range(group):
            j, m = divmod(c, members)
            perm.append((f * group + c, j * group + f * members + m))
    return lax.ppermute(x, ("fsdp", "ctx"), perm)


def gather_f(x):
    far = f_xor(x, 2)
    near = f_xor(x, 1)
    return [x, near, far, f_xor(far, 1)]


def scatter_f(kept_own, kept_far, sent):
    got = f_xor(sent, 1)
    far = (kept_far + got[1].astype(F32)).astype(BF16)
    return kept_own, got, f_xor(far, 2)


def reduce_c(slots):
    group = lax.axis_size("ctx")
    value = slots
    for bit in range(3):
        half = value.shape[0] // 2
        got = c_xor(value[half:], 1 << bit)
        value = (value[:half].astype(F32) + got.astype(F32)).astype(BF16)
    value = value[0]
    bit = 3
    while (1 << bit) < group:
        value = (value.astype(F32) + c_xor(value, 1 << bit).astype(F32)).astype(BF16)
        bit += 1
    return value


def gather_c(value):
    value = value[None]
    for bit in (2, 1, 0):
        value = jnp.concatenate([value, c_xor(value, 1 << bit)], axis=0)
    return value


def sum_all(rows):
    for k in (1, 2):
        rows = rows + f_xor(rows, k)
    k = 1
    while k < lax.axis_size("ctx"):
        rows = rows + c_xor(rows, k)
        k *= 2
    return rows


def call(kernel, outs, args, scratch=(), flops=0, name=None):
    vmem = pl.BlockSpec(memory_space=pltpu.VMEM)
    moved = sum(a.size * a.dtype.itemsize for a in args) + sum(
        o.size * o.dtype.itemsize for o in outs
    )
    return pl.pallas_call(
        kernel,
        out_shape=tuple(outs),
        in_specs=[pl.BlockSpec(memory_space=pltpu.SMEM)] + [vmem] * (len(args) - 1),
        out_specs=tuple([vmem] * len(outs)),
        scratch_shapes=list(scratch),
        cost_estimate=pl.CostEstimate(flops=flops, bytes_accessed=moved, transcendentals=0),
        compiler_params=pltpu.CompilerParams(vmem_limit_bytes=48 * 1024 * 1024),
        name=name,
    )(*args)


def shape(dims, dtype):
    return jax.ShapeDtypeStruct(dims, dtype)


def dot(a, b, contract):
    return lax.dot_general(a, b, ((contract[0:1], contract[1:2]), ((), ())), preferred_element_type=F32)


def block_rows(index, size):
    return pl.ds(pl.multiple_of(index * size, size), size)


def normalise(values):
    centred = values - jnp.mean(values, axis=-1, keepdims=True)
    inverse = lax.rsqrt(jnp.mean(centred * centred, axis=-1, keepdims=True) + EPSILON)
    return centred * inverse, inverse


def norm_back(upstream, scaled, inverse, gain):
    weighted = upstream * gain
    return inverse * (
        weighted
        - jnp.mean(weighted, axis=-1, keepdims=True)
        - scaled * jnp.mean(weighted * scaled, axis=-1, keepdims=True)
    )


def valid_rows(sc, chunk, rows):
    place = (chunk * sc[3] + sc[2]) * rows + lax.broadcasted_iota(jnp.int32, (rows, 1), 0)
    return place < sc[4]


def emit_partials(sc, rows, value_ref, own_ref, far_ref, sent_ref):
    f = sc[0]
    own_ref[...] = value_ref[block_rows(f, rows), :]
    far_ref[...] = value_ref[block_rows(f ^ 2, rows), :]
    sent_ref[0] = value_ref[block_rows(f ^ 1, rows), :].astype(BF16)
    sent_ref[1] = value_ref[block_rows(f ^ 3, rows), :].astype(BF16)


def cot_kernel(sc, c0, c1, c2, c3, proj, g_out, pulled, bias_row):
    rows = c0.shape[0]
    for k, ref in enumerate((c0, c1, c2, c3)):
        j = sc[0] ^ k
        kept = jnp.where(valid_rows(sc, j, rows), ref[...].astype(F32), 0.0)
        if k == 0:
            bias_row[...] = jnp.sum(kept, axis=0, keepdims=True)
        low = kept.astype(BF16)
        g_out[block_rows(j, rows), :] = low
        pulled[block_rows(j, rows), :] = dot(low, proj[...], (1, 1))


def qkv_kernel(sc, x0, x1, x2, x3, w0, w1, w2, w3, table, bias, normed, full, q, kv):
    rows, wrows = x0.shape[0], w0.shape[0]
    for k, ref in enumerate((w0, w1, w2, w3)):
        full[block_rows(sc[0] ^ k, wrows), :] = ref[...]
    for k, ref in enumerate((x0, x1, x2, x3)):
        place = block_rows(sc[0] ^ k, rows)
        scaled, _ = normalise(ref[...].astype(F32))
        low = (scaled * table[0:1, :] + table[1:2, :]).astype(BF16)
        normed[place, :] = low
        got = (dot(low, full[...], (1, 0)) + bias[...]).astype(BF16)
        width = q.shape[1]
        q[place, :] = got[:, :width] * jnp.asarray(0.125, BF16)
        kv[place, :] = got[:, width:]


def split3(value):
    high = value.astype(BF16)
    rest = value - high.astype(F32)
    mid = rest.astype(BF16)
    low = (rest - mid.astype(F32)).astype(BF16)
    return high, mid, low


def lanes(columns, rows, width, dtype):
    lane = lax.broadcasted_iota(jnp.int32, (rows, width), 1)
    out = jnp.zeros((rows, width), F32)
    for i, column in enumerate(columns):
        out = jnp.where(lane == i, column.astype(F32), out)
    return out.astype(dtype)


def joined(ref, base, count, h):
    total = None
    for part in range(3):
        column = base + part * count + h
        piece = ref[:, column : column + 1].astype(F32)
        total = piece if total is None else total + piece
    return total


def threshold(sc, other):
    return jnp.where(other == sc[2], 0, jnp.where(other < sc[2], 1 << 20, -(1 << 20)))


def attend(sc, step, first, last, refs):
    if first:
        q, kv = refs[:2]
        state_in = None
        rest = refs[2:]
    else:
        q, kv, acc_in, stat_in = refs[:4]
        rest = refs[4:]
    if last:
        out_w, attended, low, q_ext, own, far, sent, scratch = rest
    else:
        acc_out, stat_out = rest
    total, width = q.shape
    rows = total // WAYS
    heads = width // HD
    limit = threshold(sc, sc[2] ^ step)
    ahead = lax.broadcasted_iota(jnp.int32, (rows, rows), 1) - lax.broadcasted_iota(
        jnp.int32, (rows, rows), 0
    )
    allowed = ahead <= limit
    for jq in range(WAYS):
        place = slice(jq * rows, (jq + 1) * rows)
        parts, tops, sums = [], [], []
        for h in range(heads):
            cols = slice(h * HD, (h + 1) * HD)
            vcols = slice(width + h * HD, width + (h + 1) * HD)
            qh = q[place, cols]
            diag = jnp.where(allowed, dot(qh, kv[place, cols], (1, 1)), NEGATIVE)
            top = jnp.max(diag, axis=-1, keepdims=True)
            if jq > 0:
                before = dot(qh, kv[: jq * rows, cols], (1, 1))
                top = jnp.maximum(top, jnp.max(before, axis=-1, keepdims=True))
            if not first:
                old = stat_in[place, h : h + 1]
                top = jnp.maximum(top, old)
            weight = jnp.exp(diag - top)
            count = jnp.sum(weight, axis=-1, keepdims=True)
            acc = dot(weight.astype(BF16), kv[place, vcols], (1, 0))
            if jq > 0:
                weight = jnp.exp(before - top)
                count = count + jnp.sum(weight, axis=-1, keepdims=True)
                acc = acc + dot(weight.astype(BF16), kv[: jq * rows, vcols], (1, 0))
            if not first:
                shrink = jnp.exp(old - top)
                count = count + shrink * stat_in[place, heads + h : heads + h + 1]
                acc = acc + shrink * acc_in[place, cols]
            if last:
                acc = acc / count
                tops.append(top + jnp.log(count))
            else:
                tops.append(top)
                sums.append(count)
            parts.append(acc)
        joined_parts = jnp.concatenate(parts, axis=1)
        if last:
            attended[place, :] = joined_parts
            low_part = joined_parts.astype(BF16)
            low[place, :] = low_part
            scratch[place, :] = dot(low_part, out_w[...], (1, 0))
            split = [split3(t) for t in tops]
            columns = [split[h][part] for part in range(3) for h in range(heads)]
            q_ext[place, :width] = q[place, :]
            q_ext[place, width:] = lanes(columns, rows, q_ext.shape[1] - width, BF16)
        else:
            acc_out[place, :] = joined_parts
            stat_out[place, :] = lanes(tops + sums, rows, stat_out.shape[1], F32)
    if last:
        emit_partials(sc, rows, scratch, own, far, sent)


def second_norm_kernel(sc, own, got, far, x, table, residual, normed):
    value = (
        x[...].astype(F32)
        + own[...]
        + got[0].astype(F32)
        + far[...].astype(F32)
        + table[2:3, :]
    )
    residual[...] = value
    scaled, _ = normalise(value)
    normed[...] = (scaled * table[3:4, :] + table[4:5, :]).astype(BF16)


def feed_kernel(
    sc, n0, n1, n2, n3, w0, w1, w2, w3, bias, pulled,
    normed, full, active, g_hidden, bias_row, own, far, sent, scratch,
):
    rows, wrows = n0.shape[0], w0.shape[0]
    for k, ref in enumerate((w0, w1, w2, w3)):
        full[block_rows(sc[0] ^ k, wrows), :] = ref[...]
    total = jnp.zeros_like(bias_row)
    for k, ref in enumerate((n0, n1, n2, n3)):
        place = block_rows(sc[0] ^ k, rows)
        normed[place, :] = ref[...]
        hidden = dot(ref[...], full[...], (1, 0)) + bias[...]
        square = hidden * hidden
        bend = jnp.tanh(GELU_COEF * (hidden + CUBE * hidden * square))
        active[place, :] = (0.5 * hidden * (1.0 + bend)).astype(BF16)
        slope = 0.5 * (1.0 + bend) + 0.5 * hidden * (1.0 - bend * bend) * (
            GELU_COEF * (1.0 + 3.0 * CUBE * square)
        )
        low = (pulled[place, :] * slope).astype(BF16)
        g_hidden[place, :] = low
        total = total + jnp.sum(low.astype(F32), axis=0, keepdims=True)
        scratch[place, :] = dot(low, full[...], (1, 1))
    bias_row[...] = total
    emit_partials(sc, rows, scratch, own, far, sent)


def result_kernel(sc, active, proj, own, far, sent, scratch):
    rows = active.shape[0] // WAYS
    scratch[...] = dot(active[...], proj[...], (1, 0))
    emit_partials(sc, rows, scratch, own, far, sent)


def reverse(r):
    return ((r & 1) << 2) | (r & 2) | (r >> 2)


def slot_of(sc, piece):
    return reverse((sc[1] ^ piece) & 7)


def feed_grad_kernel(sc, active, g_out, normed, g_hidden, slots):
    step_rows, step_cols = slots.shape[2], slots.shape[3]
    quarter = step_rows // WAYS
    for a in range(WAYS):
        wide = dot(active[:, a * step_rows : (a + 1) * step_rows], g_out[...], (0, 0)).astype(BF16)
        for b in range(2):
            slots[slot_of(sc, a * 2 + b), 0] = wide[:, b * step_cols : (b + 1) * step_cols]
    for fp in range(WAYS):
        wide = dot(normed[:, fp * step_rows : (fp + 1) * step_rows], g_hidden[...], (0, 0)).astype(BF16)
        for a in range(WAYS):
            for b in range(2):
                slots[slot_of(sc, a * 2 + b), 1, block_rows(sc[0] ^ fp, quarter), :] = wide[
                    a * quarter : (a + 1) * quarter, b * step_cols : (b + 1) * step_cols
                ]


def second_back_kernel(sc, own, got, far, residual, cot, table, g_residual, g_branch, rows_out):
    upstream = own[...] + got[0].astype(F32) + far[...].astype(F32)
    scaled, inverse = normalise(residual[...])
    through = norm_back(upstream, scaled, inverse, table[3:4, :])
    g_out = jnp.where(valid_rows(sc, sc[0], cot.shape[0]), cot[...].astype(F32), 0.0)
    value = g_out + through
    g_residual[...] = value
    low = value.astype(BF16)
    g_branch[...] = low
    rows_out[0:1, :] = jnp.sum(upstream * scaled, axis=0, keepdims=True)
    rows_out[1:2, :] = jnp.sum(upstream, axis=0, keepdims=True)
    rows_out[2:3, :] = jnp.sum(low.astype(F32), axis=0, keepdims=True)


def pull_kernel(sc, b0, b1, b2, b3, out_w, attended, g_branch, do_ext):
    rows = b0.shape[0]
    width = attended.shape[1]
    heads = width // HD
    for k, ref in enumerate((b0, b1, b2, b3)):
        place = block_rows(sc[0] ^ k, rows)
        g_branch[place, :] = ref[...]
        low = dot(ref[...], out_w[...], (1, 1)).astype(BF16)
        product = low.astype(F32) * attended[place, :]
        split = [
            split3(jnp.sum(product[:, h * HD : (h + 1) * HD], axis=-1, keepdims=True))
            for h in range(heads)
        ]
        columns = [split[h][part] for part in range(3) for h in range(heads)]
        do_ext[place, :width] = low
        do_ext[place, width:] = lanes(columns, rows, do_ext.shape[1] - width, BF16)


def out_grad_kernel(sc, low, g_branch, slots):
    step_rows, step_cols = slots.shape[1], slots.shape[2]
    wide = dot(low[...], g_branch[...], (0, 0)).astype(BF16)
    for a in range(WAYS):
        for b in range(2):
            slots[slot_of(sc, a * 2 + b)] = wide[
                a * step_rows : (a + 1) * step_rows, b * step_cols : (b + 1) * step_cols
            ]


def pair_back(q, do, kv, allowed, want_q, want_kv, g_q, g_kv, start):
    total = kv.shape[0]
    width = kv.shape[1] // 2
    rows = total // WAYS
    heads = width // HD
    if start and want_kv:
        g_kv[...] = jnp.zeros_like(g_kv)
    for jq in range(WAYS):
        place = slice(jq * rows, (jq + 1) * rows)
        tail_q = q[place, width:].astype(F32)
        tail_do = do[place, width:].astype(F32)
        for h in range(heads):
            cols = slice(h * HD, (h + 1) * HD)
            vcols = slice(width + h * HD, width + (h + 1) * HD)
            qh = q[place, cols]
            doh = do[place, cols]
            pick = lambda t: (
                t[:, h : h + 1] + t[:, heads + h : heads + h + 1]
            ) + t[:, 2 * heads + h : 2 * heads + h + 1]
            lse, delta = pick(tail_q), pick(tail_do)
            grad = None
            for diag in ((True, False) if jq > 0 else (True,)):
                keys = place if diag else slice(0, jq * rows)
                scores = dot(qh, kv[keys, cols], (1, 1))
                weight = jnp.exp(scores - lse)
                if diag:
                    weight = jnp.where(allowed, weight, 0.0)
                pulled = dot(doh, kv[keys, vcols], (1, 1))
                low = (weight * (pulled - delta)).astype(BF16)
                if want_q:
                    more = dot(low, kv[keys, cols], (1, 0))
                    grad = more if grad is None else grad + more
                if want_kv:
                    g_kv[keys, cols] += dot(low, qh, (0, 0))
                    g_kv[keys, vcols] += dot(weight.astype(BF16), doh, (0, 0))
            if want_q:
                if start:
                    g_q[place, cols] = grad
                else:
                    g_q[place, cols] += grad


def back_first(sc, q, do, kv, g_q, g_kv):
    rows = kv.shape[0] // WAYS
    ahead = lax.broadcasted_iota(jnp.int32, (rows, rows), 1) - lax.broadcasted_iota(
        jnp.int32, (rows, rows), 0
    )
    pair_back(q, do, kv, ahead <= 0, True, True, g_q, g_kv, True)


def back_step(sc, step, last, refs):
    q, do, kv, q_other, do_other, kv_other, q_in, kv_in = refs[:8]
    if last:
        full, g_proj, own, far, sent, g_q, g_kv, scratch = refs[8:]
    else:
        g_q, g_kv = refs[8:]
    total = kv.shape[0]
    width = kv.shape[1] // 2
    rows = total // WAYS
    other = sc[2] ^ step
    ahead = jnp.zeros((rows, rows), jnp.int32)
    g_q[...] = q_in[...]
    g_kv[...] = kv_in[...]
    pair_back(q, do, kv_other, ahead <= jnp.where(other < sc[2], 1, -1), True, False, g_q, g_kv, False)
    pair_back(q_other, do_other, kv, ahead <= jnp.where(sc[2] < other, 1, -1), False, True, g_q, g_kv, False)
    if last:
        g_proj[:, :width] = (g_q[...] * 0.125).astype(BF16)
        g_proj[:, width:] = g_kv[...].astype(BF16)
        scratch[...] = dot(g_proj[...], full[...], (1, 1))
        emit_partials(sc, rows, scratch, own, far, sent)


def qkv_grad_kernel(sc, normed, g_proj, slots, sums):
    step = slots.shape[2]
    wrows = step * PIECES
    for fp in range(WAYS):
        wide = dot(normed[:, fp * wrows : (fp + 1) * wrows], g_proj[...], (0, 0)).astype(BF16)
        for piece in range(PIECES):
            slots[slot_of(sc, piece), sc[0] ^ fp] = wide[piece * step : (piece + 1) * step, :]
    sums[...] = jnp.sum(g_proj[...].astype(F32), axis=0, keepdims=True)


def first_back_kernel(sc, own, got, far, x, table, g_residual, input_grad, rows_out):
    upstream = own[...] + got[0].astype(F32) + far[...].astype(F32)
    scaled, inverse = normalise(x[...].astype(F32))
    through = norm_back(upstream, scaled, inverse, table[0:1, :])
    input_grad[...] = (g_residual[...] + through).astype(BF16)
    rows_out[0:1, :] = jnp.sum(upstream * scaled, axis=0, keepdims=True)
    rows_out[1:2, :] = jnp.sum(upstream, axis=0, keepdims=True)


def output_kernel(sc, own, got, far, residual, table, out):
    value = (
        residual[...] + own[...] + got[0].astype(F32) + far[...].astype(F32) + table[5:6, :]
    )
    out[...] = jnp.where(valid_rows(sc, sc[0], out.shape[0]), value, 0.0).astype(BF16)


def feed_final_kernel(sc, pieces, proj_out, fc_out):
    step_rows, step_cols = pieces.shape[2], pieces.shape[3]
    quarter = step_rows // WAYS
    for r in range(PIECES):
        piece = (sc[1] ^ reverse(r)) & 7
        a, b = piece >> 1, piece & 1
        cols = block_rows(b, step_cols)
        proj_out[block_rows(a, step_rows), cols] = pieces[r, 0].astype(F32)
        for k in range(WAYS):
            wide = block_rows((sc[0] ^ k) * 2 + b, step_cols)
            fc_out[block_rows(a, quarter), wide] = pieces[
                r, 1, k * quarter : (k + 1) * quarter, :
            ].astype(F32)


def out_final_kernel(sc, pieces, out):
    step_rows, step_cols = pieces.shape[1], pieces.shape[2]
    for r in range(PIECES):
        piece = (sc[1] ^ reverse(r)) & 7
        out[block_rows(piece >> 1, step_rows), block_rows(piece & 1, step_cols)] = pieces[r].astype(F32)


def qkv_final_kernel(sc, pieces, out):
    step, width = pieces.shape[2], pieces.shape[3] // 3
    for r in range(PIECES):
        place = block_rows((sc[1] ^ reverse(r)) & 7, step)
        for fp in range(WAYS):
            piece = pieces[r, sc[0] ^ fp].astype(F32)
            for part in range(3):
                base = part * WAYS * width + fp * width
                out[place, base : base + width] = piece[:, part * width : (part + 1) * width]


def body(
    inputs, lengths, ln1_gain, ln1_bias, qkv_weight, qv_bias, out_weight, out_bias,
    ln2_gain, ln2_bias, fc_weight, fc_bias, proj_weight, proj_bias, cotangent,
):
    group = lax.axis_size("ctx")
    members = group // WAYS
    assert lax.axis_size("fsdp") == WAYS and inputs.shape[0] == 1
    assert group % PIECES == 0 and group & (group - 1) == 0
    f, c = lax.axis_index("fsdp"), lax.axis_index("ctx")
    rows, width = inputs.shape[1:]
    head_width = width // WAYS
    hidden_width = fc_bias.shape[0]
    total = rows * WAYS
    f_order = f ^ jnp.arange(WAYS)

    x_own = swap_layout(inputs[0])
    cot_own = swap_layout(cotangent[0])
    length_digits = jnp.stack([lengths[0] >> 6, lengths[0] & 63]).astype(BF16)
    small = jnp.concatenate(
        [ln1_gain, ln1_bias, out_bias, ln2_gain, ln2_bias, proj_bias, qv_bias, length_digits]
    )
    small_all = jnp.stack([small, f_xor(small, 1), f_xor(small, 2), f_xor(small, 3)])
    small_all = jnp.take(small_all, f_order, axis=0).astype(F32)
    table = jnp.transpose(
        small_all[:, : 6 * head_width].reshape(WAYS, 6, head_width), (1, 0, 2)
    ).reshape(6, width)
    qv_full = small_all[:, 6 * head_width : 8 * head_width].reshape(2 * WAYS, head_width)
    qkv_bias = jnp.concatenate(
        [qv_full[f], jnp.zeros((head_width,), F32), qv_full[WAYS + f]]
    ).reshape(1, 3 * head_width)
    digits = small_all[c // members, 8 * head_width :].astype(jnp.int32)
    sc = jnp.stack(
        [f, c, c % members, jnp.asarray(members), digits[0] * 64 + digits[1]]
    ).astype(jnp.int32)

    qkv_blocks = qkv_weight.reshape(head_width, 3, WAYS, head_width)
    fc_blocks = fc_weight.reshape(head_width, WAYS, hidden_width)

    def columns(blocks, axis, k):
        return lax.dynamic_index_in_dim(blocks, f ^ k, axis, keepdims=False).reshape(
            head_width, -1
        )

    w_qkv = [columns(qkv_blocks, 2, k) for k in range(WAYS)]
    w_fc = [columns(fc_blocks, 1, k) for k in range(WAYS)]
    w_qkv = [w_qkv[0]] + [f_xor(w_qkv[k], k) for k in range(1, WAYS)]
    x_all = gather_f(x_own)
    normed_one, qkv_full, q, kv = call(
        qkv_kernel,
        [
            shape((total, width), BF16),
            shape((width, 3 * head_width), BF16),
            shape((total, head_width), BF16),
            shape((total, 2 * head_width), BF16),
        ],
        [sc, *x_all, *w_qkv, table, qkv_bias],
        flops=2 * total * width * 3 * head_width,
        name="qkv",
    )
    kv_other = [kv] + [c_xor(kv, r) for r in range(1, members)]
    w_fc = [w_fc[0]] + [f_xor(w_fc[k], k) for k in range(1, WAYS)]
    cot_all = gather_f(cot_own)
    g_out, pulled, proj_row = call(
        cot_kernel,
        [shape((total, width), BF16), shape((total, hidden_width), F32), shape((1, width), F32)],
        [sc, *cot_all, proj_weight],
        flops=2 * total * width * hidden_width,
        name="cot",
    )

    partials = [shape((rows, width), F32), shape((rows, width), F32), shape((2, rows, width), BF16)]
    state = []
    for r in range(members):
        first, last = r == 0, r == members - 1
        if last:
            outs = [
                shape((total, head_width), F32),
                shape((total, head_width), BF16),
                shape((total, head_width + 64), BF16),
                *partials,
            ]
            scratch = [pltpu.VMEM((total, width), F32)]
            extra = [out_weight]
        else:
            outs = [shape((total, head_width), F32), shape((total, 128), F32)]
            scratch, extra = [], []

        def kernel(sc_ref, *refs, r=r, first=first, last=last):
            attend(sc_ref, r, first, last, refs)

        state = call(
            kernel,
            outs,
            [sc, q, kv_other[r], *state, *extra],
            scratch,
            flops=4 * total * total * head_width,
            name=f"attend{min(r, 1)}",
        )
    attended, attended_low, q_ext, *branch = state
    q_other = [q_ext] + [c_xor(q_ext, r) for r in range(1, members)]
    branch = scatter_f(*branch)
    residual, normed_two = call(
        second_norm_kernel,
        [shape((rows, width), F32), shape((rows, width), BF16)],
        [sc, *branch, x_own, table],
        name="norm2",
    )
    normed_two_all = gather_f(normed_two)
    normed_two_full, fc_full, active, g_hidden, fc_row, *g_two = call(
        feed_kernel,
        [
            shape((total, width), BF16),
            shape((width, hidden_width), BF16),
            shape((total, hidden_width), BF16),
            shape((total, hidden_width), BF16),
            shape((1, hidden_width), F32),
            *partials,
        ],
        [sc, *normed_two_all, *w_fc, fc_bias.astype(F32).reshape(1, -1), pulled],
        [pltpu.VMEM((total, width), F32)],
        flops=4 * total * width * hidden_width,
        name="feed",
    )
    g_two = scatter_f(*g_two)
    g_residual, g_branch, two_rows = call(
        second_back_kernel,
        [shape((rows, width), F32), shape((rows, width), BF16), shape((3, width), F32)],
        [sc, *g_two, residual, cot_own, table],
        name="norm2_back",
    )
    g_branch_all = gather_f(g_branch)
    g_branch_full, do_ext = call(
        pull_kernel,
        [shape((total, width), BF16), shape((total, head_width + 64), BF16)],
        [sc, *g_branch_all, out_weight, attended],
        flops=2 * total * width * head_width,
        name="pull",
    )
    do_other = [do_ext] + [c_xor(do_ext, r) for r in range(1, members)]
    grads = call(
        back_first,
        [shape((total, head_width), F32), shape((total, 2 * head_width), F32)],
        [sc, q_ext, do_ext, kv],
        flops=10 * total * total * head_width,
        name="back0",
    )
    for r in range(1, members):
        last = r == members - 1
        outs = [shape((total, head_width), F32), shape((total, 2 * head_width), F32)]
        if last:
            scratch = [pltpu.VMEM(o.shape, F32) for o in outs] + [pltpu.VMEM((total, width), F32)]
            outs = [shape((total, 3 * head_width), BF16), *partials]
            extra = [qkv_full]
        else:
            scratch, extra = [], []

        def kernel(sc_ref, *refs, r=r, last=last):
            back_step(sc_ref, r, last, refs)

        grads = call(
            kernel,
            outs,
            [sc, q_ext, do_ext, kv, q_other[r], do_other[r], kv_other[r], *grads, *extra],
            scratch,
            flops=14 * total * total * head_width,
            name="back1",
        )
    g_proj, *g_one = grads
    g_one = scatter_f(*g_one)
    step = head_width // PIECES
    qkv_slots, qkv_sums = call(
        qkv_grad_kernel,
        [shape((PIECES, WAYS, step, 3 * head_width), BF16), shape((1, 3 * head_width), F32)],
        [sc, normed_one, g_proj],
        flops=2 * total * width * 3 * head_width,
        name="qkv_grad",
    )
    input_grad, one_rows = call(
        first_back_kernel,
        [shape((rows, width), BF16), shape((2, width), F32)],
        [sc, *g_one, x_own, table, g_residual],
        name="norm1_back",
    )
    input_grad = swap_layout(input_grad)[None]

    result = call(
        result_kernel,
        partials,
        [sc, active, proj_weight],
        [pltpu.VMEM((total, width), F32)],
        flops=2 * total * width * hidden_width,
        name="result",
    )
    result = scatter_f(*result)
    (outputs,) = call(
        output_kernel, [shape((rows, width), BF16)], [sc, *result, residual, table], name="output"
    )
    outputs = swap_layout(outputs)[None]

    (feed_slots,) = call(
        feed_grad_kernel,
        [shape((PIECES, 2, head_width, width // 2), BF16)],
        [sc, active, g_out, normed_two_full, g_hidden],
        flops=4 * total * width * hidden_width,
        name="feed_grad",
    )
    quarter = head_width // WAYS
    feed_piece = reduce_c(feed_slots)
    fc_piece = feed_piece[1].reshape(WAYS, quarter, width // 2)
    fc_piece = jnp.stack([fc_piece[0]] + [f_xor(fc_piece[k], k) for k in range(1, WAYS)])
    feed_piece = jnp.stack([feed_piece[0], fc_piece.reshape(head_width, width // 2)])
    grad_proj, grad_fc = call(
        feed_final_kernel,
        [shape((hidden_width, width), F32), shape((head_width, WAYS * hidden_width), F32)],
        [sc, gather_c(feed_piece)],
        name="feed_final",
    )
    (out_slots,) = call(
        out_grad_kernel,
        [shape((PIECES, quarter, width // 2), BF16)],
        [sc, attended_low, g_branch_full],
        flops=2 * total * width * head_width,
        name="out_grad",
    )
    (grad_out,) = call(
        out_final_kernel,
        [shape((head_width, width), F32)],
        [sc, gather_c(reduce_c(out_slots))],
        name="out_final",
    )
    qkv_piece = reduce_c(qkv_slots)
    qkv_piece = jnp.stack([qkv_piece[0]] + [f_xor(qkv_piece[k], k) for k in range(1, WAYS)])
    (grad_qkv,) = call(
        qkv_final_kernel,
        [shape((head_width, 3 * width), F32)],
        [sc, gather_c(qkv_piece)],
        name="qkv_final",
    )

    here = (jnp.arange(WAYS) == f)[:, None]
    q_row = jnp.where(here, qkv_sums[:, :head_width], 0.0).reshape(1, width)
    v_row = jnp.where(here, qkv_sums[:, 2 * head_width :], 0.0).reshape(1, width)
    fc_rows = jnp.where(here, fc_row, 0.0)
    early = sum_all(jnp.concatenate([two_rows, proj_row, fc_rows], axis=0))
    late = sum_all(jnp.concatenate([one_rows, q_row, v_row], axis=0))

    def mine(row):
        return lax.dynamic_slice_in_dim(row, f * head_width, head_width, 0)

    grad_qv = lax.dynamic_slice_in_dim(
        jnp.concatenate([late[2], late[3]]), f * 2 * head_width, 2 * head_width, 0
    )
    grad_fc_bias = lax.dynamic_index_in_dim(early[4:], f, 0, keepdims=False)
    return (
        outputs,
        input_grad,
        mine(late[0]),
        mine(late[1]),
        grad_qkv,
        grad_qv,
        grad_out,
        mine(early[2]),
        mine(early[0]),
        mine(early[1]),
        grad_fc,
        grad_fc_bias,
        grad_proj,
        mine(early[3]),
    )


def solution(mesh):
    tokens, rows, vector = P("fsdp", "ctx", None), P("fsdp", None), P("fsdp")
    in_specs = (
        tokens, vector, vector, vector, rows, vector, rows, vector,
        vector, vector, rows, vector, rows, vector, tokens,
    )
    out_specs = (
        tokens, tokens, vector, vector, rows, vector, rows, vector,
        vector, vector, rows, vector, rows, vector,
    )
    return jax.shard_map(body, mesh=mesh, in_specs=in_specs, out_specs=out_specs, check_vma=False)
```

```python
import functools

import jax
import jax.numpy as jnp
from jax import lax
from jax.experimental import pallas as pl
from jax.experimental.pallas import tpu as pltpu
from jax.sharding import PartitionSpec as P

HD = 64
EPSILON = 1e-05
NEGATIVE = -1e30
GELU_COEF = 0.7978845608028654
CUBE = 0.044715
F32 = jnp.float32
BF16 = jnp.bfloat16
WAYS = 4
PIECES = 8
VMEM_LIMIT = 24 * 1024 * 1024


def f_xor(x, k):
    n = lax.axis_size("fsdp")
    return lax.ppermute(x, "fsdp", [(i, i ^ k) for i in range(n)])


def c_xor(x, k):
    n = lax.axis_size("ctx")
    return lax.ppermute(x, "ctx", [(i, i ^ k) for i in range(n)])


def swap_layout(x):
    group = lax.axis_size("ctx")
    members = group // WAYS
    perm = []
    for f in range(WAYS):
        for c in range(group):
            j, m = divmod(c, members)
            perm.append((f * group + c, j * group + f * members + m))
    return lax.ppermute(x, ("fsdp", "ctx"), perm)


def after(value, *others):
    return lax.optimization_barrier((value, *others))[0]


def gather_f(x, until=lambda far: far):
    far = f_xor(x, 2)
    near = f_xor(x, 1)
    return [x, near, far, f_xor(until(far), 1)]


class Order:
    def __init__(self, scalars):
        self.scalars = scalars
        self.token = None

    def tie(self, value):
        if self.token is None:
            return value
        return lax.optimization_barrier((value, self.token))[0]

    def mark(self, value):
        self.token = value
        return value

    def call(self, kernel, outs, args, scratch=(), flops=0, name=None, direct=False, late=()):
        scalars = after(self.tie(self.scalars), *late)
        got = call(kernel, outs, [scalars, *args], scratch, flops, name, direct)
        self.mark(min(got, key=lambda value: value.size))
        return got

    def scatter_f(self, kept_own, kept_far, sent):
        return kept_own, kept_far, f_xor(sent, 1)

    def scatter_f_far(self, state, late=()):
        kept_own, kept_far, got = state
        (far,) = self.call(
            far_kernel, [shape(kept_own.shape, BF16)], [kept_far, got], name="far", late=late
        )
        return kept_own, got, f_xor(far, 2)


X, Z1, Z2 = 0, 1, 2


class Chain:
    def __init__(self, order, bits, name, keep, send, vec=None):
        self.order, self.bits, self.name = order, bits, name
        self.stage = 0
        self.keep = keep
        self.vec = vec
        self.got = c_xor(send, 1 << bits[0])

    def fold(self, splits=1):
        self.stage += 1
        name = self.name + "_fold"
        dims = self.keep.shape
        if self.stage < 3:
            half = (dims[0] // 2, *dims[1:])
            if self.vec is None:
                self.keep, send = self.order.call(
                    fold_kernel, [shape(half, BF16)] * 2, [self.keep, self.got], name=name
                )
            else:
                both = (half[0] + self.vec.shape[0], half[1])
                self.keep, self.vec, send = self.order.call(
                    fold_both_kernel,
                    [shape(half, BF16), shape(self.vec.shape, BF16), shape(both, BF16)],
                    [self.keep, self.vec, self.got],
                    name=name,
                )
            self.got = c_xor(send, 1 << self.bits[self.stage])
            return None
        extra = lax.axis_size("ctx") > PIECES
        if self.vec is not None:
            value, self.vec = self.order.call(
                last_both_kernel,
                [shape(dims, BF16), shape(self.vec.shape, BF16)],
                [self.keep, self.vec, self.got],
                name=name,
            )
            self.vec = self.others(self.vec)
            return self.others(value)
        rows = dims[-2]
        parts = 1 if extra else splits
        pieces = self.order.call(
            last_fold_kernel,
            [shape((rows // parts, dims[-1]), BF16)] * parts,
            [self.keep.reshape(rows, dims[-1]), self.got.reshape(rows, dims[-1])],
            name=name,
        )
        if extra:
            value = self.others(pieces[0])
            step = rows // splits
            pieces = [value[i * step : (i + 1) * step] for i in range(splits)]
        return pieces[0] if splits == 1 else list(pieces)

    def others(self, value):
        bit = 3
        while (1 << bit) < lax.axis_size("ctx"):
            value = (value.astype(F32) + c_xor(value, 1 << bit).astype(F32)).astype(BF16)
            bit += 1
        return value

    def start_gather(self, value):
        self.value = value[None]
        self.got = c_xor(self.value, 1 << self.bits[2])
        self.stage = 2

    def grow(self):
        self.stage -= 1
        self.value = self.order.mark(
            jnp.concatenate([self.order.tie(self.value), self.got], axis=0)
        )
        self.got = c_xor(self.value, 1 << self.bits[self.stage])


def call(kernel, outs, args, scratch=(), flops=0, name=None, direct=False):
    vmem = pl.BlockSpec(memory_space=pltpu.VMEM)
    moved = sum(a.size * a.dtype.itemsize for a in args) + sum(
        o.size * o.dtype.itemsize for o in outs
    )
    return pl.pallas_call(
        kernel,
        out_shape=tuple(outs),
        in_specs=[pl.BlockSpec(memory_space=pltpu.SMEM)] + [vmem] * (len(args) - 1),
        out_specs=tuple([pl.BlockSpec() if direct else vmem] * len(outs)),
        scratch_shapes=list(scratch),
        cost_estimate=pl.CostEstimate(flops=flops, bytes_accessed=moved, transcendentals=0),
        compiler_params=pltpu.CompilerParams(vmem_limit_bytes=VMEM_LIMIT),
        name=name,
    )(*args)


def shape(dims, dtype):
    return jax.ShapeDtypeStruct(dims, dtype)


def dot(a, b, contract):
    return lax.dot_general(a, b, ((contract[0:1], contract[1:2]), ((), ())), preferred_element_type=F32)


def block_rows(index, size):
    return pl.ds(pl.multiple_of(index * size, size), size)


def normalise(values):
    centred = values - jnp.mean(values, axis=-1, keepdims=True)
    inverse = lax.rsqrt(jnp.mean(centred * centred, axis=-1, keepdims=True) + EPSILON)
    return centred * inverse, inverse


def norm_back(upstream, scaled, inverse, gain):
    weighted = upstream * gain
    return inverse * (
        weighted
        - jnp.mean(weighted, axis=-1, keepdims=True)
        - scaled * jnp.mean(weighted * scaled, axis=-1, keepdims=True)
    )


def valid_rows(sc, table, chunk, rows):
    place = (chunk * sc[3] + sc[2]) * rows + lax.broadcasted_iota(jnp.int32, (rows, 1), 0)
    return place.astype(F32) < table[6:7, 0:1]


def emit_partials(sc, rows, value_ref, own_ref, far_ref, sent_ref):
    f = sc[0]
    own_ref[...] = value_ref[block_rows(f, rows), :]
    far_ref[...] = value_ref[block_rows(f ^ 2, rows), :]
    sent_ref[0] = value_ref[block_rows(f ^ 1, rows), :].astype(BF16)
    sent_ref[1] = value_ref[block_rows(f ^ 3, rows), :].astype(BF16)


def far_kernel(sc, kept, got, out):
    out[...] = (kept[...] + got[1].astype(F32)).astype(BF16)


def fold_kernel(sc, keep, got, kept, sent):
    half = keep.shape[0] // 2
    sent[...] = (keep[half:].astype(F32) + got[half:].astype(F32)).astype(BF16)
    kept[...] = (keep[:half].astype(F32) + got[:half].astype(F32)).astype(BF16)


def fold_both_kernel(sc, keep, vec, got, kept, vec_out, sent):
    count = keep.shape[0]
    half = count // 2
    both = (vec[...].astype(F32) + got[count:].astype(F32)).astype(BF16)
    sent[half:] = both
    vec_out[...] = both
    sent[:half] = (keep[half:].astype(F32) + got[half:count].astype(F32)).astype(BF16)
    kept[...] = (keep[:half].astype(F32) + got[:half].astype(F32)).astype(BF16)


def last_fold_kernel(sc, keep, got, *outs):
    rows = outs[0].shape[0]
    for i, out in enumerate(outs):
        place = slice(i * rows, (i + 1) * rows)
        out[...] = (keep[place].astype(F32) + got[place].astype(F32)).astype(BF16)


def last_both_kernel(sc, keep, vec, got, kept, vec_out):
    count = keep.shape[0]
    vec_out[...] = (vec[...].astype(F32) + got[count:].astype(F32)).astype(BF16)
    kept[...] = (keep[...].astype(F32) + got[:count].astype(F32)).astype(BF16)


def exchange_kernel(sc, near, far, vec, own, s1, s2, s3):
    rows = own.shape[0]
    own[...] = near[:rows]
    for sent, ref, base in ((s2, far, 0), (s3, far, rows), (s1, near, rows)):
        sent[:rows] = ref[base : base + rows]
        sent[rows:] = vec[...]


VECTOR_ROWS = 12


def vector_place(row, block, width):
    at = row * WAYS + block
    return slice(at // 3, at // 3 + 1), slice((at % 3) * width, (at % 3 + 1) * width)


def join_kernel(sc, own, vec, r1, r2, r3, near, far, mine, qv, fc, scratch):
    rows, width = own.shape[0], own.shape[1] // 3
    near[:rows] = own[...]
    near[rows:] = r1[:rows]
    far[:rows] = r2[:rows]
    far[rows:] = r3[:rows]
    scratch[...] = (
        vec[...].astype(F32)
        + r1[rows:].astype(F32)
        + r2[rows:].astype(F32)
        + r3[rows:].astype(F32)
    )
    for block in range(WAYS):

        @pl.when(sc[0] == block)
        def _(block=block):
            for row in range(6):
                mine[row : row + 1, :] = scratch[vector_place(row, block, width)]
            for i in range(2):
                at = 2 * block + i
                qv[:, i * width : (i + 1) * width] = scratch[
                    vector_place(6 + at // WAYS, at % WAYS, width)
                ]
            for i in range(WAYS):
                fc[:, i * width : (i + 1) * width] = scratch[vector_place(8 + block, i, width)]


def small_kernel(sc, g1, b1, bo, g2, b2, bp, qv, out):
    width = out.shape[1]
    out[...] = jnp.zeros_like(out)
    for i, ref in enumerate((g1, b1, bo, g2, b2, bp)):
        out[i : i + 1, :] = ref[...].reshape(1, width)
    out[6:7, :] = qv[0:width].reshape(1, width)
    out[7:8, :] = qv[width : 2 * width].reshape(1, width)
    length = sc[4]
    out[8:9, :] = jnp.full((1, width), length >> 6, jnp.int32).astype(BF16)
    out[9:10, :] = jnp.full((1, width), length & 63, jnp.int32).astype(BF16)


def table_kernel(sc, s0, s1, s2, s3, table, bias):
    width = s0.shape[1]
    table[7:8, :] = jnp.zeros((1, table.shape[1]), F32)
    bias[...] = jnp.zeros_like(bias)
    odd = (sc[0] & 1) == 1
    for k, ref in enumerate((s0, s1, s2, s3)):
        values = ref[...].astype(F32)
        j = sc[0] ^ k
        pair = jnp.where(odd, values[7:8], values[6:7])
        for block in range(WAYS):

            @pl.when(j == block)
            def _(values=values, block=block):
                table[0:6, block * width : (block + 1) * width] = values[0:6]

        @pl.when(j == (sc[0] >> 1))
        def _(pair=pair):
            bias[:, :width] = pair

        @pl.when(j == 2 + (sc[0] >> 1))
        def _(pair=pair):
            bias[:, 2 * width :] = pair

        @pl.when(j == sc[5])
        def _(values=values):
            row = values[8:9] * 64.0 + values[9:10]
            for block in range(WAYS):
                table[6:7, block * width : (block + 1) * width] = row


def qkv_columns_kernel(sc, weight, w0, w1, w2, w3):
    width = w0.shape[1] // 3
    for k, ref in ((2, w2), (3, w3), (1, w1), (0, w0)):
        for block in range(WAYS):

            @pl.when((sc[0] ^ k) == block)
            def _(ref=ref, block=block):
                for part in range(3):
                    base = part * WAYS * width + block * width
                    ref[:, part * width : (part + 1) * width] = weight[:, base : base + width]


def fc_columns_kernel(sc, weight, w0, w1, w2, w3):
    for k, ref in ((2, w2), (3, w3), (1, w1), (0, w0)):
        ref[...] = weight[:, block_rows(sc[0] ^ k, ref.shape[1])]


def cot_kernel(sc, c0, c1, c2, c3, proj, table, g_out, pulled, bias_row):
    rows = c0.shape[0]
    for k, ref in enumerate((c0, c1, c2, c3)):
        j = sc[0] ^ k
        kept = jnp.where(valid_rows(sc, table, j, rows), ref[...].astype(F32), 0.0)
        if k == 0:
            bias_row[...] = jnp.sum(kept, axis=0, keepdims=True)
        low = kept.astype(BF16)
        g_out[block_rows(j, rows), :] = low
        pulled[block_rows(j, rows), :] = dot(low, proj[...], (1, 1))


def qkv_kernel(sc, x0, x1, x2, x3, w0, w1, w2, w3, table, bias, normed, scales, full, q, kv):
    rows, wrows = x0.shape[0], w0.shape[0]
    for k, ref in enumerate((w0, w1, w2, w3)):
        full[block_rows(sc[0] ^ k, wrows), :] = ref[...]
    for k, ref in enumerate((x0, x1, x2, x3)):
        place = block_rows(sc[0] ^ k, rows)
        scaled, _ = normalise(ref[...].astype(F32))
        low = (scaled * table[0:1, :] + table[1:2, :]).astype(BF16)
        normed[place, :] = low
        scales[place, :] = scaled.astype(BF16)
        got = (dot(low, full[...], (1, 0)) + bias[...]).astype(BF16)
        width = q.shape[1]
        q[place, :] = got[:, :width] * jnp.asarray(0.125, BF16)
        kv[place, :] = got[:, width:]


def split3(value):
    high = value.astype(BF16)
    rest = value - high.astype(F32)
    mid = rest.astype(BF16)
    low = (rest - mid.astype(F32)).astype(BF16)
    return high, mid, low


def lanes(columns, rows, width, dtype):
    lane = lax.broadcasted_iota(jnp.int32, (rows, width), 1)
    out = jnp.zeros((rows, width), F32)
    for i, column in enumerate(columns):
        out = jnp.where(lane == i, column.astype(F32), out)
    return out.astype(dtype)


def joined(ref, base, count, h):
    total = None
    for part in range(3):
        column = base + part * count + h
        piece = ref[:, column : column + 1].astype(F32)
        total = piece if total is None else total + piece
    return total


def threshold(sc, other):
    return jnp.where(other == sc[2], 0, jnp.where(other < sc[2], 1 << 20, -(1 << 20)))


def attend(sc, step, first, last, refs):
    if first:
        q, kv = refs[:2]
        state_in = None
        rest = refs[2:]
    else:
        q, kv, acc_in, stat_in = refs[:4]
        rest = refs[4:]
    if last:
        out_w, attended, low, q_ext, own, far, sent, scratch = rest
    else:
        acc_out, stat_out = rest
    total, width = q.shape
    rows = total // WAYS
    heads = width // HD
    limit = threshold(sc, sc[2] ^ step)
    ahead = lax.broadcasted_iota(jnp.int32, (rows, rows), 1) - lax.broadcasted_iota(
        jnp.int32, (rows, rows), 0
    )
    allowed = ahead <= limit
    for jq in range(WAYS):
        place = slice(jq * rows, (jq + 1) * rows)
        parts, tops, sums = [], [], []
        for h in range(heads):
            cols = slice(h * HD, (h + 1) * HD)
            vcols = slice(width + h * HD, width + (h + 1) * HD)
            qh = q[place, cols]
            diag = jnp.where(allowed, dot(qh, kv[place, cols], (1, 1)), NEGATIVE)
            top = jnp.max(diag, axis=-1, keepdims=True)
            if jq > 0:
                before = dot(qh, kv[: jq * rows, cols], (1, 1))
                top = jnp.maximum(top, jnp.max(before, axis=-1, keepdims=True))
            if not first:
                old = stat_in[place, h : h + 1]
                top = jnp.maximum(top, old)
            weight = jnp.exp(diag - top)
            count = jnp.sum(weight, axis=-1, keepdims=True)
            acc = dot(weight.astype(BF16), kv[place, vcols], (1, 0))
            if jq > 0:
                weight = jnp.exp(before - top)
                count = count + jnp.sum(weight, axis=-1, keepdims=True)
                acc = acc + dot(weight.astype(BF16), kv[: jq * rows, vcols], (1, 0))
            if not first:
                shrink = jnp.exp(old - top)
                count = count + shrink * stat_in[place, heads + h : heads + h + 1]
                acc = acc + shrink * acc_in[place, cols]
            if last:
                acc = acc / count
                tops.append(top + jnp.log(count))
            else:
                tops.append(top)
                sums.append(count)
            parts.append(acc)
        joined_parts = jnp.concatenate(parts, axis=1)
        if last:
            attended[place, :] = joined_parts
            low_part = joined_parts.astype(BF16)
            low[place, :] = low_part
            scratch[place, :] = dot(low_part, out_w[...], (1, 0))
            split = [split3(t) for t in tops]
            columns = [split[h][part] for part in range(3) for h in range(heads)]
            q_ext[place, :width] = q[place, :]
            q_ext[place, width:] = lanes(columns, rows, q_ext.shape[1] - width, BF16)
        else:
            acc_out[place, :] = joined_parts
            stat_out[place, :] = lanes(tops + sums, rows, stat_out.shape[1], F32)
    if last:
        emit_partials(sc, rows, scratch, own, far, sent)


def second_norm_kernel(sc, own, got, far, x, table, residual, normed):
    value = (
        x[...].astype(F32)
        + own[...]
        + got[0].astype(F32)
        + far[...].astype(F32)
        + table[2:3, :]
    )
    residual[...] = value
    scaled, _ = normalise(value)
    normed[...] = (scaled * table[3:4, :] + table[4:5, :]).astype(BF16)


def feed_kernel(
    sc, n0, n1, n2, n3, w0, w1, w2, w3, bias, pulled,
    normed, full, active, g_hidden, bias_rows, own, far, sent, scratch,
):
    rows, wrows = n0.shape[0], w0.shape[0]
    for k, ref in enumerate((w0, w1, w2, w3)):
        full[block_rows(sc[0] ^ k, wrows), :] = ref[...]
    total = jnp.zeros((1, bias_rows.shape[1]), F32)
    for k, ref in enumerate((n0, n1, n2, n3)):
        place = block_rows(sc[0] ^ k, rows)
        normed[place, :] = ref[...]
        hidden = dot(ref[...], full[...], (1, 0)) + bias[...]
        square = hidden * hidden
        bend = jnp.tanh(GELU_COEF * (hidden + CUBE * hidden * square))
        active[place, :] = (0.5 * hidden * (1.0 + bend)).astype(BF16)
        slope = 0.5 * (1.0 + bend) + 0.5 * hidden * (1.0 - bend * bend) * (
            GELU_COEF * (1.0 + 3.0 * CUBE * square)
        )
        low = (pulled[place, :] * slope).astype(BF16)
        g_hidden[place, :] = low
        total = total + jnp.sum(low.astype(F32), axis=0, keepdims=True)
        scratch[place, :] = dot(low, full[...], (1, 1))
    bias_rows[...] = jnp.where(
        lax.broadcasted_iota(jnp.int32, bias_rows.shape, 0) == sc[0], total, 0.0
    )
    emit_partials(sc, rows, scratch, own, far, sent)


def result_kernel(sc, active, proj, own, far, sent, scratch):
    rows = active.shape[0] // WAYS
    scratch[...] = dot(active[...], proj[...], (1, 0))
    emit_partials(sc, rows, scratch, own, far, sent)


def piece_of(sc, bits, slot):
    r = 0
    for i, bit in enumerate(bits):
        r |= ((slot >> (2 - i)) & 1) << bit
    return (sc[1] ^ r) & 7


def place_halves(keep, send):
    half = keep.shape[0]
    return [(slot, keep if slot < half else send, slot % half) for slot in range(2 * half)]


def tile_grad_kernel(bits, sc, active, g_out, keep, send, scratch):
    step_rows, step_cols = keep.shape[1], keep.shape[2]
    scratch[...] = dot(active[...], g_out[...], (0, 0)).astype(BF16)
    for slot, ref, at in place_halves(keep, send):
        piece = piece_of(sc, bits, slot)
        ref[at] = scratch[block_rows(piece >> 1, step_rows), block_rows(piece & 1, step_cols)]


def fc_grad_kernel(bits, sc, normed, g_hidden, keep, send, scratch):
    step_rows, step_cols = keep.shape[1], keep.shape[2]
    quarter = step_rows // WAYS
    scratch[...] = dot(normed[...], g_hidden[...], (0, 0)).astype(BF16)
    for slot, ref, at in place_halves(keep, send):
        piece = piece_of(sc, bits, slot)
        for k in range(WAYS):
            start = (sc[0] ^ k) * WAYS + (piece >> 1)
            ref[at, k * quarter : (k + 1) * quarter, :] = scratch[
                block_rows(start, quarter), block_rows(piece & 1, step_cols)
            ]


def second_back_kernel(sc, own, got, far, residual, cot, table, g_residual, g_branch, rows_out):
    upstream = own[...] + got[0].astype(F32) + far[...].astype(F32)
    scaled, inverse = normalise(residual[...])
    through = norm_back(upstream, scaled, inverse, table[3:4, :])
    g_out = jnp.where(valid_rows(sc, table, sc[0], cot.shape[0]), cot[...].astype(F32), 0.0)
    value = g_out + through
    g_residual[...] = value
    low = value.astype(BF16)
    g_branch[...] = low
    rows_out[0:1, :] = jnp.sum(upstream * scaled, axis=0, keepdims=True)
    rows_out[1:2, :] = jnp.sum(upstream, axis=0, keepdims=True)
    rows_out[2:3, :] = jnp.sum(low.astype(F32), axis=0, keepdims=True)


def pull_kernel(sc, b0, b1, b2, b3, out_w, attended, g_branch, do_ext):
    rows = b0.shape[0]
    width = attended.shape[1]
    heads = width // HD
    for k, ref in enumerate((b0, b1, b2, b3)):
        place = block_rows(sc[0] ^ k, rows)
        g_branch[place, :] = ref[...]
        low = dot(ref[...], out_w[...], (1, 1)).astype(BF16)
        product = low.astype(F32) * attended[place, :]
        split = [
            split3(jnp.sum(product[:, h * HD : (h + 1) * HD], axis=-1, keepdims=True))
            for h in range(heads)
        ]
        columns = [split[h][part] for part in range(3) for h in range(heads)]
        do_ext[place, :width] = low
        do_ext[place, width:] = lanes(columns, rows, do_ext.shape[1] - width, BF16)


def pair_back(q, do, kv, allowed, want_q, want_kv, g_q, g_kv, start):
    total = kv.shape[0]
    width = kv.shape[1] // 2
    rows = total // WAYS
    heads = width // HD
    if start and want_kv:
        g_kv[...] = jnp.zeros_like(g_kv)
    for jq in range(WAYS):
        place = slice(jq * rows, (jq + 1) * rows)
        tail_q = q[place, width:].astype(F32)
        tail_do = do[place, width:].astype(F32)
        for h in range(heads):
            cols = slice(h * HD, (h + 1) * HD)
            vcols = slice(width + h * HD, width + (h + 1) * HD)
            qh = q[place, cols]
            doh = do[place, cols]
            pick = lambda t: (
                t[:, h : h + 1] + t[:, heads + h : heads + h + 1]
            ) + t[:, 2 * heads + h : 2 * heads + h + 1]
            lse, delta = pick(tail_q), pick(tail_do)
            grad = None
            for diag in ((True, False) if jq > 0 else (True,)):
                keys = place if diag else slice(0, jq * rows)
                scores = dot(qh, kv[keys, cols], (1, 1))
                weight = jnp.exp(scores - lse)
                if diag:
                    weight = jnp.where(allowed, weight, 0.0)
                pulled = dot(doh, kv[keys, vcols], (1, 1))
                low = (weight * (pulled - delta)).astype(BF16)
                if want_q:
                    more = dot(low, kv[keys, cols], (1, 0))
                    grad = more if grad is None else grad + more
                if want_kv:
                    g_kv[keys, cols] += dot(low, qh, (0, 0))
                    g_kv[keys, vcols] += dot(weight.astype(BF16), doh, (0, 0))
            if want_q:
                if start:
                    g_q[place, cols] = grad
                else:
                    g_q[place, cols] += grad


def back_first(sc, q, do, kv, g_q, g_kv):
    rows = kv.shape[0] // WAYS
    ahead = lax.broadcasted_iota(jnp.int32, (rows, rows), 1) - lax.broadcasted_iota(
        jnp.int32, (rows, rows), 0
    )
    pair_back(q, do, kv, ahead <= 0, True, True, g_q, g_kv, True)


def back_step(sc, step, last, refs):
    q, do, kv, q_other, do_other, kv_other, q_in, kv_in = refs[:8]
    if last:
        full, scales, g_proj, own, far, sent, sums, g_q, g_kv, scratch = refs[8:]
    else:
        g_q, g_kv = refs[8:]
    total = kv.shape[0]
    width = kv.shape[1] // 2
    rows = total // WAYS
    other = sc[2] ^ step
    ahead = jnp.zeros((rows, rows), jnp.int32)
    g_q[...] = q_in[...]
    g_kv[...] = kv_in[...]
    pair_back(q, do, kv_other, ahead <= jnp.where(other < sc[2], 1, -1), True, False, g_q, g_kv, False)
    pair_back(q_other, do_other, kv, ahead <= jnp.where(sc[2] < other, 1, -1), False, True, g_q, g_kv, False)
    if last:
        g_proj[:, :width] = (g_q[...] * 0.125).astype(BF16)
        g_proj[:, width:] = g_kv[...].astype(BF16)
        scratch[...] = dot(g_proj[...], full[...], (1, 1))
        emit_partials(sc, rows, scratch, own, far, sent)
        sums[0:1, :] = jnp.sum(scratch[...] * scales[...].astype(F32), axis=0, keepdims=True)
        sums[1:2, :] = jnp.sum(scratch[...], axis=0, keepdims=True)


def qkv_grad_kernel(
    near_bits, far_bits, sc, normed, g_proj, two, proj, fc, one, nk, ns, vec, wk, ws, scratch, rows_out
):
    step = nk.shape[0] // PIECES
    width = nk.shape[1] // 3
    scratch[...] = dot(normed[...], g_proj[...], (0, 0))
    for base, bits, keep, send in ((2, far_bits, wk, ws), (0, near_bits, nk, ns)):
        for slot in range(PIECES):
            ref, at = (keep, slot) if slot < PIECES // 2 else (send, slot - PIECES // 2)
            piece = piece_of(sc, bits, slot)
            for i in range(2):
                start = (sc[0] ^ (base + i)) * PIECES + piece
                ref[(2 * at + i) * step : (2 * at + i + 1) * step, :] = scratch[
                    block_rows(start, step), :
                ].astype(BF16)
    rows_out[0:2, :] = one[...]
    rows_out[2:3, :] = two[2:3, :]
    rows_out[3:5, :] = two[0:2, :]
    rows_out[5:6, :] = proj[...]
    rows_out[6:8, :] = jnp.zeros_like(rows_out[6:8, :])
    rows_out[8:12, :] = fc[...]
    total = jnp.sum(g_proj[...].astype(F32), axis=0, keepdims=True)
    for block in range(WAYS):

        @pl.when(sc[0] == block)
        def _(block=block):
            place = slice(block * width, (block + 1) * width)
            rows_out[6:7, place] = total[:, :width]
            rows_out[7:8, place] = total[:, 2 * width :]

    for row in range(VECTOR_ROWS):
        for block in range(WAYS):
            vec[vector_place(row, block, width)] = rows_out[
                row : row + 1, block * width : (block + 1) * width
            ].astype(BF16)
    ns[nk.shape[0] :, :] = vec[...]


def first_back_kernel(sc, own, got, far, x, table, g_residual, input_grad):
    upstream = own[...] + got[0].astype(F32) + far[...].astype(F32)
    scaled, inverse = normalise(x[...].astype(F32))
    through = norm_back(upstream, scaled, inverse, table[0:1, :])
    input_grad[...] = (g_residual[...] + through).astype(BF16)


def output_kernel(sc, own, got, far, residual, table, out):
    value = (
        residual[...] + own[...] + got[0].astype(F32) + far[...].astype(F32) + table[5:6, :]
    )
    out[...] = jnp.where(valid_rows(sc, table, sc[0], out.shape[0]), value, 0.0).astype(BF16)


def slots_in(near, far):
    half = near.shape[0]
    return [(slot, near if slot < half else far, slot % half) for slot in range(2 * half)]


def tiles_final_kernel(bits, sc, near, far, proj_out, out_out):
    step_cols = near.shape[2]
    for slot, ref, at in slots_in(near, far):
        piece = piece_of(sc, bits, slot)
        base = 0
        for out in (proj_out, out_out):
            rows = out.shape[0] // WAYS
            out[block_rows(piece >> 1, rows), block_rows(piece & 1, step_cols)] = ref[
                at, base : base + rows
            ].astype(F32)
            base += rows


def fc_final_kernel(bits, sc, near, far, out):
    quarter, step_cols = near.shape[1] // WAYS, near.shape[2]
    for slot, ref, at in slots_in(near, far):
        piece = piece_of(sc, bits, slot)
        for k in range(WAYS):
            wide = block_rows((sc[0] ^ k) * 2 + (piece & 1), step_cols)
            out[block_rows(piece >> 1, quarter), wide] = ref[
                at, k * quarter : (k + 1) * quarter
            ].astype(F32)


def qkv_final_kernel(near_bits, far_bits, sc, nn, nf, wn, wf, out):
    step, width = nn.shape[1] // 2, nn.shape[2] // 3
    for base, bits, near, far in ((0, near_bits, nn, nf), (2, far_bits, wn, wf)):
        for slot, ref, at in slots_in(near, far):
            place = block_rows(piece_of(sc, bits, slot), step)
            for i in range(2):
                piece = ref[at, i * step : (i + 1) * step].astype(F32)
                for block in range(WAYS):

                    @pl.when((sc[0] ^ (base + i)) == block)
                    def _(piece=piece, block=block, place=place):
                        for part in range(3):
                            start = part * WAYS * width + block * width
                            out[place, start : start + width] = piece[
                                :, part * width : (part + 1) * width
                            ]


def body(
    inputs, lengths, ln1_gain, ln1_bias, qkv_weight, qv_bias, out_weight, out_bias,
    ln2_gain, ln2_bias, fc_weight, fc_bias, proj_weight, proj_bias, cotangent,
):
    group = lax.axis_size("ctx")
    members = group // WAYS
    assert lax.axis_size("fsdp") == WAYS and inputs.shape[0] == 1
    assert group % PIECES == 0 and group & (group - 1) == 0
    f, c = lax.axis_index("fsdp"), lax.axis_index("ctx")
    rows, width = inputs.shape[1:]
    head_width = width // WAYS
    hidden_width = fc_bias.shape[0]
    total = rows * WAYS
    scalars = jnp.stack(
        [f, c, c % members, jnp.asarray(members), lengths[0], c // members]
    ).astype(jnp.int32)
    order = Order(scalars)

    x_own = swap_layout(inputs[0])
    cot_own = swap_layout(cotangent[0])
    w_qkv = order.call(
        qkv_columns_kernel,
        [shape((head_width, 3 * head_width), BF16)] * WAYS,
        [qkv_weight],
        name="qkv_columns",
    )
    far2, far3, near = f_xor(w_qkv[2], 2), f_xor(w_qkv[3], 3), f_xor(w_qkv[1], 1)
    w_qkv = [w_qkv[0], near, far2, far3]
    (small,) = order.call(
        small_kernel,
        [shape((16, head_width), BF16)],
        [ln1_gain, ln1_bias, out_bias, ln2_gain, ln2_bias, proj_bias, qv_bias],
        name="small",
    )
    small_all = [small, f_xor(small, 1), f_xor(small, 2), f_xor(small, 3)]
    x_all = gather_f(after(x_own, far2))
    cot_all = gather_f(after(cot_own, x_all[1]))
    table, qkv_bias = order.call(
        table_kernel,
        [shape((8, width), F32), shape((1, 3 * head_width), F32)],
        small_all,
        name="table",
    )
    w_fc = order.call(
        fc_columns_kernel,
        [shape((head_width, hidden_width), BF16)] * WAYS,
        [fc_weight],
        name="fc_columns",
    )
    far2, far3, near = f_xor(w_fc[2], 2), f_xor(w_fc[3], 3), f_xor(w_fc[1], 1)
    w_fc = [w_fc[0], near, far2, far3]

    normed_one, scales_one, qkv_full, q, kv = order.call(
        qkv_kernel,
        [
            shape((total, width), BF16),
            shape((total, width), BF16),
            shape((width, 3 * head_width), BF16),
            shape((total, head_width), BF16),
            shape((total, 2 * head_width), BF16),
        ],
        [*x_all, *w_qkv, table, qkv_bias],
        flops=2 * total * width * 3 * head_width,
        name="qkv",
    )
    kv_other = [kv] + [c_xor(kv, r) for r in range(1, members)]

    partials = [shape((rows, width), F32), shape((rows, width), F32), shape((2, rows, width), BF16)]
    state = []
    for r in range(members):
        first, last = r == 0, r == members - 1
        if last:
            outs = [
                shape((total, head_width), F32),
                shape((total, head_width), BF16),
                shape((total, head_width + 64), BF16),
                *partials,
            ]
            scratch = [pltpu.VMEM((total, width), F32)]
            extra = [out_weight]
        else:
            outs = [shape((total, head_width), F32), shape((total, 128), F32)]
            scratch, extra = [], []

        def kernel(sc_ref, *refs, r=r, first=first, last=last):
            attend(sc_ref, r, first, last, refs)

        state = order.call(
            kernel,
            outs,
            [q, kv_other[r], *state, *extra],
            scratch,
            flops=4 * total * total * head_width,
            name=f"attend{min(r, 1)}",
            late=[w_fc[2]] if last else [],
        )
        if r == 0:
            g_out, pulled, proj_row = order.call(
                cot_kernel,
                [
                    shape((total, width), BF16),
                    shape((total, hidden_width), F32),
                    shape((1, width), F32),
                ],
                [*cot_all, proj_weight, table],
                flops=2 * total * width * hidden_width,
                name="cot",
            )
    attended, attended_low, q_ext, *branch = state
    branch = order.scatter_f(*branch)
    q_other = [q_ext] + [c_xor(q_ext, r) for r in range(1, members)]
    branch = order.scatter_f_far(branch, late=[w_fc[1], w_fc[3]])
    residual, normed_two = order.call(
        second_norm_kernel,
        [shape((rows, width), F32), shape((rows, width), BF16)],
        [*branch, x_own, table],
        name="norm2",
    )
    normed_two_all = gather_f(normed_two)
    normed_two_full, fc_full, active, g_hidden, fc_rows, *g_two = order.call(
        feed_kernel,
        [
            shape((total, width), BF16),
            shape((width, hidden_width), BF16),
            shape((total, hidden_width), BF16),
            shape((total, hidden_width), BF16),
            shape((WAYS, hidden_width), F32),
            *partials,
        ],
        [*normed_two_all, *w_fc, fc_bias.astype(F32).reshape(1, -1), pulled],
        [pltpu.VMEM((total, width), F32)],
        flops=4 * total * width * hidden_width,
        name="feed",
    )
    g_two = order.scatter_f(*g_two)
    one, other = (X, Z1, Z2), (Z1, X, Z2)
    half = PIECES // 2
    slots = [shape((half, head_width, width // 2), BF16)] * 2
    keep, send = order.call(
        functools.partial(tile_grad_kernel, other),
        slots,
        [active, g_out],
        [pltpu.VMEM((width, width), BF16)],
        flops=2 * total * width * hidden_width,
        name="proj_grad",
    )
    proj_chain = Chain(order, other, "proj", keep, send)
    g_two = order.scatter_f_far(g_two)
    keep, send = order.call(
        functools.partial(fc_grad_kernel, one),
        slots,
        [normed_two_full, g_hidden],
        [pltpu.VMEM((width, width), BF16)],
        flops=2 * total * width * hidden_width,
        name="fc_grad",
    )
    fc_chain = Chain(order, one, "fc", keep, send)
    result = order.call(
        result_kernel,
        partials,
        [active, proj_weight],
        [pltpu.VMEM((total, width), F32)],
        flops=2 * total * width * hidden_width,
        name="result",
    )
    result = order.scatter_f(*result)
    g_residual, g_branch, two_rows = order.call(
        second_back_kernel,
        [shape((rows, width), F32), shape((rows, width), BF16), shape((3, width), F32)],
        [*g_two, residual, cot_own, table],
        name="norm2_back",
    )
    g_branch_all = gather_f(g_branch)
    g_branch_full, do_ext = order.call(
        pull_kernel,
        [shape((total, width), BF16), shape((total, head_width + 64), BF16)],
        [*g_branch_all, out_weight, attended],
        flops=2 * total * width * head_width,
        name="pull",
    )
    do_other = [do_ext] + [c_xor(do_ext, r) for r in range(1, members)]
    grads = order.call(
        back_first,
        [shape((total, head_width), F32), shape((total, 2 * head_width), F32)],
        [q_ext, do_ext, kv],
        flops=10 * total * total * head_width,
        name="back0",
    )
    proj_chain.fold()
    fc_chain.fold()
    for r in range(1, members):
        last = r == members - 1
        outs = [shape((total, head_width), F32), shape((total, 2 * head_width), F32)]
        if last:
            scratch = [pltpu.VMEM(o.shape, F32) for o in outs] + [pltpu.VMEM((total, width), F32)]
            outs = [shape((total, 3 * head_width), BF16), *partials, shape((2, width), F32)]
            extra = [qkv_full, scales_one]
        else:
            scratch, extra = [], []

        def kernel(sc_ref, *refs, r=r, last=last):
            back_step(sc_ref, r, last, refs)

        grads = order.call(
            kernel,
            outs,
            [q_ext, do_ext, kv, q_other[r], do_other[r], kv_other[r], *grads, *extra],
            scratch,
            flops=14 * total * total * head_width,
            name="back1",
        )
    g_proj, *g_one, one_rows = grads
    g_one = order.scatter_f(*g_one)
    step = head_width // PIECES
    flat = 2 * half * step
    near_keep, near_send, vec, far_keep, far_send = order.call(
        functools.partial(qkv_grad_kernel, one, other),
        [
            shape((flat, 3 * head_width), BF16),
            shape((flat + 16, 3 * head_width), BF16),
            shape((16, 3 * head_width), BF16),
            shape((flat, 3 * head_width), BF16),
            shape((flat, 3 * head_width), BF16),
        ],
        [normed_one, g_proj, two_rows, proj_row, fc_rows, one_rows],
        [pltpu.VMEM((width, 3 * head_width), F32), pltpu.VMEM((VECTOR_ROWS, width), F32)],
        flops=2 * total * width * 3 * head_width,
        name="qkv_grad",
    )
    near_chain = Chain(order, one, "qkv_near", near_keep, near_send, vec)
    far_chain = Chain(order, other, "qkv_far", far_keep, far_send)
    g_one = order.scatter_f_far(g_one)
    quarter = head_width // WAYS
    keep, send = order.call(
        functools.partial(tile_grad_kernel, other),
        [shape((half, quarter, width // 2), BF16)] * 2,
        [attended_low, g_branch_full],
        [pltpu.VMEM((head_width, width), BF16)],
        flops=2 * total * width * head_width,
        name="out_grad",
    )
    out_chain = Chain(order, other, "out", keep, send)
    proj_chain.fold()
    fc_chain.fold()
    (input_grad,) = order.call(
        first_back_kernel,
        [shape((rows, width), BF16)],
        [*g_one, x_own, table, g_residual],
        name="norm1_back",
    )
    input_grad = swap_layout(input_grad)[None]
    near_chain.fold()
    far_chain.fold()
    result = order.scatter_f_far(result)
    proj_piece = proj_chain.fold()
    fc_pieces = fc_chain.fold(WAYS)
    fc_pieces = [fc_pieces[0]] + [f_xor(fc_pieces[k], k) for k in range(1, WAYS)]
    out_chain.fold()
    near_chain.fold()
    far_chain.fold()
    fc_chain.start_gather(order.mark(jnp.concatenate([order.tie(fc_pieces[0]), *fc_pieces[1:]])))
    out_chain.fold()
    near_piece = near_chain.fold()
    far_piece = far_chain.fold()
    sent_rows = shape((step + 16, 3 * head_width), BF16)
    own, s1, s2, s3 = order.call(
        exchange_kernel,
        [shape((step, 3 * head_width), BF16)] + [sent_rows] * 3,
        [near_piece, far_piece, near_chain.vec],
        name="exchange",
    )
    r2, r3, r1 = f_xor(s2, 2), f_xor(s3, 3), f_xor(s1, 1)
    out_piece = out_chain.fold()
    proj_chain.start_gather(
        order.mark(jnp.concatenate([order.tie(proj_piece), out_piece], axis=0))
    )
    fc_chain.grow()
    near_piece, far_piece, mine, grad_qv, grad_fc_bias = order.call(
        join_kernel,
        [
            shape((2 * step, 3 * head_width), BF16),
            shape((2 * step, 3 * head_width), BF16),
            shape((6, head_width), F32),
            shape((1, 2 * head_width), F32),
            shape((1, hidden_width), F32),
        ],
        [own, near_chain.vec, r1, r2, r3],
        [pltpu.VMEM((16, 3 * head_width), F32)],
        name="join",
    )
    near_chain.start_gather(near_piece)
    far_chain.start_gather(far_piece)
    (outputs,) = order.call(
        output_kernel, [shape((rows, width), BF16)], [*result, residual, table], name="output"
    )
    outputs = swap_layout(outputs)[None]
    proj_chain.grow()
    near_chain.grow()
    far_chain.grow()
    fc_chain.grow()
    proj_chain.grow()
    near_chain.grow()
    far_chain.grow()

    def finish(kernel, dims, *chains, name):
        arrays = [a for chain in chains for a in (chain.value, chain.got)]
        bits = [chain.bits for chain in chains]
        return order.call(
            functools.partial(kernel, *bits),
            [shape(d, F32) for d in dims],
            arrays,
            name=name,
            direct=True,
        )

    (grad_fc,) = finish(
        fc_final_kernel, [(head_width, WAYS * hidden_width)], fc_chain, name="fc_final"
    )
    grad_proj, grad_out = finish(
        tiles_final_kernel, [(hidden_width, width), (head_width, width)], proj_chain, name="proj_final"
    )
    (grad_qkv,) = finish(
        qkv_final_kernel, [(head_width, 3 * width)], near_chain, far_chain, name="qkv_final"
    )
    return (
        outputs,
        input_grad,
        mine[0],
        mine[1],
        grad_qkv,
        grad_qv[0],
        grad_out,
        mine[2],
        mine[3],
        mine[4],
        grad_fc,
        grad_fc_bias[0],
        grad_proj,
        mine[5],
    )


def solution(mesh):
    tokens, rows, vector = P("fsdp", "ctx", None), P("fsdp", None), P("fsdp")
    in_specs = (
        tokens, vector, vector, vector, rows, vector, rows, vector,
        vector, vector, rows, vector, rows, vector, tokens,
    )
    out_specs = (
        tokens, tokens, vector, vector, rows, vector, rows, vector,
        vector, vector, rows, vector, rows, vector,
    )
    return jax.shard_map(body, mesh=mesh, in_specs=in_specs, out_specs=out_specs, check_vma=False)
```

```python
import functools

import jax
import jax.numpy as jnp
from jax import lax
from jax.experimental import pallas as pl
from jax.experimental.pallas import tpu as pltpu
from jax.sharding import PartitionSpec as P

HD = 64
EPSILON = 1e-05
NEGATIVE = -1e30
GELU_COEF = 0.7978845608028654
CUBE = 0.044715
F32 = jnp.float32
BF16 = jnp.bfloat16
WAYS = 4
PIECES = 8
VMEM_LIMIT = 24 * 1024 * 1024


def f_xor(x, k):
    n = lax.axis_size("fsdp")
    return lax.ppermute(x, "fsdp", [(i, i ^ k) for i in range(n)])


def c_xor(x, k):
    n = lax.axis_size("ctx")
    return lax.ppermute(x, "ctx", [(i, i ^ k) for i in range(n)])


def turned(index):
    return ((index & 1) << 1) | (index >> 1)


def swap_layout(x):
    group = lax.axis_size("ctx")
    members = group // WAYS
    perm = []
    for f in range(WAYS):
        for c in range(group):
            j, m = divmod(c, members)
            perm.append((f * group + c, turned(j) * group + turned(f) * members + m))
    return lax.ppermute(x, ("fsdp", "ctx"), perm)


def after(value, *others):
    return lax.optimization_barrier((value, *others))[0]


def gather_f(x, until=lambda far: far):
    far = f_xor(x, 2)
    near = f_xor(x, 1)
    return [x, near, far, f_xor(until(far), 1)]


class Order:
    def __init__(self, scalars):
        self.scalars = scalars
        self.token = None

    def tie(self, value):
        if self.token is None:
            return value
        return lax.optimization_barrier((value, self.token))[0]

    def mark(self, value):
        self.token = value
        return value

    def call(self, kernel, outs, args, scratch=(), flops=0, name=None, direct=False, late=()):
        scalars = after(self.tie(self.scalars), *late)
        got = call(kernel, outs, [scalars, *args], scratch, flops, name, direct)
        self.mark(min(got, key=lambda value: value.size))
        return got

    def scatter_f(self, kept_own, kept_far, sent_far, sent_own):
        return kept_own, kept_far, f_xor(sent_far, 1), f_xor(sent_own, 1)

    def scatter_f_far(self, state, late=()):
        kept_own, kept_far, got_far, got_own = state
        (far,) = self.call(
            far_kernel, [shape(kept_own.shape, BF16)], [kept_far, got_far], name="far", late=late
        )
        return kept_own, got_own, f_xor(far, 2)


X, Z1, Z2 = 0, 1, 2
ONE, OTHER = (X, Z1, Z2), (Z1, X, Z2)


def others(value):
    bit = 3
    while (1 << bit) < lax.axis_size("ctx"):
        value = (value.astype(F32) + c_xor(value, 1 << bit).astype(F32)).astype(BF16)
        bit += 1
    return value


def call(kernel, outs, args, scratch=(), flops=0, name=None, direct=False):
    vmem = pl.BlockSpec(memory_space=pltpu.VMEM)
    moved = sum(a.size * a.dtype.itemsize for a in args) + sum(
        o.size * o.dtype.itemsize for o in outs
    )
    return pl.pallas_call(
        kernel,
        out_shape=tuple(outs),
        in_specs=[pl.BlockSpec(memory_space=pltpu.SMEM)] + [vmem] * (len(args) - 1),
        out_specs=tuple([pl.BlockSpec() if direct else vmem] * len(outs)),
        scratch_shapes=list(scratch),
        cost_estimate=pl.CostEstimate(flops=flops, bytes_accessed=moved, transcendentals=0),
        compiler_params=pltpu.CompilerParams(vmem_limit_bytes=VMEM_LIMIT),
        name=name,
    )(*args)


def shape(dims, dtype):
    return jax.ShapeDtypeStruct(dims, dtype)


def dot(a, b, contract):
    return lax.dot_general(a, b, ((contract[0:1], contract[1:2]), ((), ())), preferred_element_type=F32)


def block_rows(index, size):
    return pl.ds(pl.multiple_of(index * size, size), size)


def member_rows(member, size):
    return block_rows(turned(member), size)


def normalise(values):
    centred = values - jnp.mean(values, axis=-1, keepdims=True)
    inverse = lax.rsqrt(jnp.mean(centred * centred, axis=-1, keepdims=True) + EPSILON)
    return centred * inverse, inverse


def norm_back(upstream, scaled, inverse, gain):
    weighted = upstream * gain
    return inverse * (
        weighted
        - jnp.mean(weighted, axis=-1, keepdims=True)
        - scaled * jnp.mean(weighted * scaled, axis=-1, keepdims=True)
    )


def valid_rows(sc, table, chunk, rows):
    place = (turned(chunk) * sc[3] + sc[2]) * rows + lax.broadcasted_iota(jnp.int32, (rows, 1), 0)
    return place.astype(F32) < table[6:7, 0:1]


def emit_partials(sc, rows, value_ref, own_ref, far_ref, sent_far, sent_own):
    f = sc[0]
    own_ref[...] = value_ref[member_rows(f, rows), :]
    far_ref[...] = value_ref[member_rows(f ^ 2, rows), :]
    sent_own[...] = value_ref[member_rows(f ^ 1, rows), :].astype(BF16)
    sent_far[...] = value_ref[member_rows(f ^ 3, rows), :].astype(BF16)


def far_kernel(sc, kept, got, out):
    out[...] = (kept[...] + got[...].astype(F32)).astype(BF16)


def added(a, b):
    return (a.astype(F32) + b.astype(F32)).astype(BF16)


def fold_into(keep, got, kept, sent):
    half = keep.shape[0] // 2
    sent[:half] = added(keep[half:], got[half : 2 * half])
    kept[...] = added(keep[:half], got[:half])


def mlp_fold_kernel(sc, proj, proj_got, fc, fc_got, proj_kept, proj_sent, fc_kept, fc_sent):
    fold_into(proj, proj_got, proj_kept, proj_sent)
    fold_into(fc, fc_got, fc_kept, fc_sent)


def mlp_meet_kernel(sc, proj, proj_got, fc, fc_got, kept, sent):
    for i, (keep, got) in enumerate(((proj, proj_got), (fc, fc_got))):
        kept[i] = added(keep[0], got[0])
        sent[i] = added(keep[1], got[1])


def mlp_last_kernel(sc, keep, got, proj, *pieces):
    proj[...] = added(keep[0], got[0])
    rows = pieces[0].shape[0]
    for i, piece in enumerate(pieces):
        place = slice(i * rows, (i + 1) * rows)
        piece[...] = added(keep[1, place], got[1, place])


def mlp_join_kernel(sc, proj, p0, p1, p2, p3, out):
    out[0] = proj[...]
    rows = p0.shape[0]
    for i, piece in enumerate((p0, p1, p2, p3)):
        out[1, i * rows : (i + 1) * rows] = piece[...]


def mlp_part_kernel(sc, own, got, proj, fc):
    for i, out in enumerate((proj, fc)):
        out[0] = own[i]
        out[1] = got[i]


def grow_kernel(sc, a, a_got, b, b_got, a_out, b_out):
    for own, got, out in ((a, a_got, a_out), (b, b_got, b_out)):
        count = own.shape[0]
        out[:count] = own[...]
        out[count:] = got[...]


def qkv_fold_kernel(sc, near, vec, near_got, far, far_got, near_kept, vec_out, near_sent, far_kept, far_sent):
    fold_into(near, near_got, near_kept, near_sent)
    both = added(vec[...], near_got[near.shape[0] :])
    near_sent[near.shape[0] // 2 :] = both
    vec_out[...] = both
    fold_into(far, far_got, far_kept, far_sent)


def qkv_meet_kernel(sc, near, vec, near_got, far, far_got, kept, vec_out, sent):
    rows, more = near.shape[0] // 2, far.shape[0] // 2
    kept[:rows] = added(near[:rows], near_got[:rows])
    sent[:rows] = added(near[rows:], near_got[rows : 2 * rows])
    kept[rows:] = added(far[:more], far_got[:more])
    sent[rows : rows + more] = added(far[more:], far_got[more:])
    both = added(vec[...], near_got[2 * rows :])
    sent[rows + more :] = both
    vec_out[...] = both


def qkv_last_kernel(sc, keep, vec, got, piece, vec_out):
    count = keep.shape[0]
    piece[...] = added(keep[...], got[:count])
    vec_out[...] = added(vec[...], got[count:])


def exchange_kernel(sc, piece, vec, s1, s2, s3):
    rows = s1.shape[0] - vec.shape[0]
    for k, sent in ((2, s2), (3, s3), (1, s1)):
        sent[:rows] = piece[k * rows : (k + 1) * rows]
        sent[rows:] = vec[...]


def qkv_part_kernel(sc, own, got, near, far):
    rows = near.shape[1]
    for i, ref in enumerate((own, got)):
        near[i] = ref[:rows]
        far[i] = ref[rows:]


VECTOR_ROWS = 12


def vector_place(row, block, width):
    at = row * WAYS + block
    return slice(at // 3, at // 3 + 1), slice((at % 3) * width, (at % 3 + 1) * width)


def join_kernel(sc, piece, vec, r1, r2, r3, joined, *rest):
    *mine, qv, fc, scratch = rest
    rows, width = r1.shape[0] - vec.shape[0], piece.shape[1] // 3
    joined[:rows] = piece[:rows]
    for i, got in ((1, r1), (2, r2), (3, r3)):
        joined[i * rows : (i + 1) * rows] = got[:rows]
    joined[WAYS * rows :] = piece[WAYS * rows :]
    scratch[...] = (
        vec[...].astype(F32)
        + r1[rows:].astype(F32)
        + r2[rows:].astype(F32)
        + r3[rows:].astype(F32)
    )
    for block in range(WAYS):

        @pl.when(sc[0] == block)
        def _(block=block):
            for row in range(6):
                mine[row][...] = scratch[vector_place(row, block, width)].reshape(width)
            for i in range(2):
                at = 2 * block + i
                qv[i * width : (i + 1) * width] = scratch[
                    vector_place(6 + at // WAYS, at % WAYS, width)
                ].reshape(width)
            for i in range(WAYS):
                fc[i * width : (i + 1) * width] = scratch[
                    vector_place(8 + block, i, width)
                ].reshape(width)


def small_kernel(sc, vectors, out, bias):
    width = out.shape[1]
    out[...] = jnp.zeros_like(out)
    length = sc[4]
    out[8:9, :] = jnp.full((1, width), length >> 6, jnp.int32).astype(BF16)
    out[9:10, :] = jnp.full((1, width), length & 63, jnp.int32).astype(BF16)
    for i in range(8):
        out[i : i + 1, :] = vectors[i * width : (i + 1) * width].reshape(1, width)
    bias[...] = vectors[8 * width :].reshape(bias.shape).astype(F32)


def table_kernel(sc, s0, s1, s2, s3, table, bias):
    width = s0.shape[1]
    table[7:8, :] = jnp.zeros((1, table.shape[1]), F32)
    bias[...] = jnp.zeros_like(bias)
    odd = (sc[0] & 1) == 1
    for k, ref in enumerate((s0, s1, s2, s3)):
        values = ref[...].astype(F32)
        j = sc[0] ^ k
        pair = jnp.where(odd, values[7:8], values[6:7])
        for block in range(WAYS):

            @pl.when(j == block)
            def _(values=values, block=block):
                table[0:6, block * width : (block + 1) * width] = values[0:6]

        @pl.when(j == (sc[0] >> 1))
        def _(pair=pair):
            bias[:, :width] = pair

        @pl.when(j == 2 + (sc[0] >> 1))
        def _(pair=pair):
            bias[:, 2 * width :] = pair

        @pl.when(j == sc[5])
        def _(values=values):
            row = values[8:9] * 64.0 + values[9:10]
            for block in range(WAYS):
                table[6:7, block * width : (block + 1) * width] = row


def qkv_columns_kernel(sc, weight, w0, w1, w2, w2_low, w3):
    width = w0.shape[1] // 3
    half = w2.shape[0]
    rows = {0: [(w0, 0)], 1: [(w1, 0)], 2: [(w2, 0), (w2_low, half)], 3: [(w3, 0)]}
    for k in (2, 3, 1, 0):
        for block in range(WAYS):

            @pl.when((sc[0] ^ k) == block)
            def _(k=k, block=block):
                for ref, start in rows[k]:
                    for part in range(3):
                        base = part * WAYS * width + block * width
                        ref[:, part * width : (part + 1) * width] = weight[
                            start : start + ref.shape[0], base : base + width
                        ]


def fc_columns_kernel(sc, weight, w0, w1, w2, w3):
    for k, ref in ((2, w2), (3, w3), (1, w1), (0, w0)):
        ref[...] = weight[:, block_rows(sc[0] ^ k, ref.shape[1])]


def cot_kernel(sc, c0, c1, c2, c3, proj, table, g_out, pulled, bias_row):
    rows = c0.shape[0]
    for k, ref in enumerate((c0, c1, c2, c3)):
        j = sc[0] ^ k
        kept = jnp.where(valid_rows(sc, table, j, rows), ref[...].astype(F32), 0.0)
        if k == 0:
            bias_row[...] = jnp.sum(kept, axis=0, keepdims=True)
        low = kept.astype(BF16)
        g_out[member_rows(j, rows), :] = low
        pulled[member_rows(j, rows), :] = dot(low, proj[...], (1, 1))


def qkv_kernel(sc, x0, x1, x2, x3, w0, w1, w2, w2_low, w3, table, bias, normed, scales, full, q, kv):
    rows, wrows = x0.shape[0], w0.shape[0]
    half = wrows // 2
    for k, ref in ((0, w0), (1, w1), (3, w3)):
        full[block_rows(sc[0] ^ k, wrows), :] = ref[...]
    full[block_rows((sc[0] ^ 2) * 2, half), :] = w2[...]
    full[block_rows((sc[0] ^ 2) * 2 + 1, half), :] = w2_low[...]
    for k, ref in enumerate((x0, x1, x2, x3)):
        place = member_rows(sc[0] ^ k, rows)
        scaled, _ = normalise(ref[...].astype(F32))
        low = (scaled * table[0:1, :] + table[1:2, :]).astype(BF16)
        normed[place, :] = low
        scales[place, :] = scaled.astype(BF16)
        got = (dot(low, full[...], (1, 0)) + bias[...]).astype(BF16)
        width = q.shape[1]
        q[place, :] = got[:, :width] * jnp.asarray(0.125, BF16)
        kv[place, :] = got[:, width:]


def split3(value):
    high = value.astype(BF16)
    rest = value - high.astype(F32)
    mid = rest.astype(BF16)
    low = (rest - mid.astype(F32)).astype(BF16)
    return high, mid, low


def lanes(columns, rows, width, dtype):
    lane = lax.broadcasted_iota(jnp.int32, (rows, width), 1)
    out = jnp.zeros((rows, width), F32)
    for i, column in enumerate(columns):
        out = jnp.where(lane == i, column.astype(F32), out)
    return out.astype(dtype)


def joined(ref, base, count, h):
    total = None
    for part in range(3):
        column = base + part * count + h
        piece = ref[:, column : column + 1].astype(F32)
        total = piece if total is None else total + piece
    return total


def threshold(sc, other):
    return jnp.where(other == sc[2], 0, jnp.where(other < sc[2], 1 << 20, -(1 << 20)))


def attend(sc, step, first, last, refs):
    if first:
        q, kv = refs[:2]
        state_in = None
        rest = refs[2:]
    else:
        q, kv, acc_in, stat_in = refs[:4]
        rest = refs[4:]
    if last:
        out_w, attended, low, q_ext, own, far, sent, sent_own, scratch = rest
    else:
        acc_out, stat_out = rest
    total, width = q.shape
    rows = total // WAYS
    heads = width // HD
    limit = threshold(sc, sc[2] ^ step)
    ahead = lax.broadcasted_iota(jnp.int32, (rows, rows), 1) - lax.broadcasted_iota(
        jnp.int32, (rows, rows), 0
    )
    allowed = ahead <= limit
    for jq in range(WAYS):
        place = slice(jq * rows, (jq + 1) * rows)
        parts, tops, sums = [], [], []
        for h in range(heads):
            cols = slice(h * HD, (h + 1) * HD)
            vcols = slice(width + h * HD, width + (h + 1) * HD)
            qh = q[place, cols]
            diag = jnp.where(allowed, dot(qh, kv[place, cols], (1, 1)), NEGATIVE)
            top = jnp.max(diag, axis=-1, keepdims=True)
            if jq > 0:
                before = dot(qh, kv[: jq * rows, cols], (1, 1))
                top = jnp.maximum(top, jnp.max(before, axis=-1, keepdims=True))
            if not first:
                old = stat_in[place, h : h + 1]
                top = jnp.maximum(top, old)
            weight = jnp.exp(diag - top)
            count = jnp.sum(weight, axis=-1, keepdims=True)
            acc = dot(weight.astype(BF16), kv[place, vcols], (1, 0))
            if jq > 0:
                weight = jnp.exp(before - top)
                count = count + jnp.sum(weight, axis=-1, keepdims=True)
                acc = acc + dot(weight.astype(BF16), kv[: jq * rows, vcols], (1, 0))
            if not first:
                shrink = jnp.exp(old - top)
                count = count + shrink * stat_in[place, heads + h : heads + h + 1]
                acc = acc + shrink * acc_in[place, cols]
            if last:
                acc = acc / count
                tops.append(top + jnp.log(count))
            else:
                tops.append(top)
                sums.append(count)
            parts.append(acc)
        joined_parts = jnp.concatenate(parts, axis=1)
        if last:
            attended[place, :] = joined_parts
            low_part = joined_parts.astype(BF16)
            low[place, :] = low_part
            scratch[place, :] = dot(low_part, out_w[...], (1, 0))
            split = [split3(t) for t in tops]
            columns = [split[h][part] for part in range(3) for h in range(heads)]
            q_ext[place, :width] = q[place, :]
            q_ext[place, width:] = lanes(columns, rows, q_ext.shape[1] - width, BF16)
        else:
            acc_out[place, :] = joined_parts
            stat_out[place, :] = lanes(tops + sums, rows, stat_out.shape[1], F32)
    if last:
        emit_partials(sc, rows, scratch, own, far, sent, sent_own)


def second_norm_kernel(sc, own, got, far, x, table, residual, normed):
    value = (
        x[...].astype(F32)
        + own[...]
        + got[...].astype(F32)
        + far[...].astype(F32)
        + table[2:3, :]
    )
    residual[...] = value
    scaled, _ = normalise(value)
    normed[...] = (scaled * table[3:4, :] + table[4:5, :]).astype(BF16)


def assemble_kernel(sc, w0, w1, w2, w3, full):
    for k, ref in enumerate((w0, w1, w2, w3)):
        full[block_rows(sc[0] ^ k, ref.shape[0]), :] = ref[...]


def feed_kernel(
    sc, n0, n1, n2, n3, full, bias, pulled,
    normed, active, g_hidden, bias_row, own, far, sent, sent_own, scratch,
):
    rows = n0.shape[0]
    total = jnp.zeros_like(bias_row)
    for k, ref in enumerate((n0, n1, n2, n3)):
        place = member_rows(sc[0] ^ k, rows)
        normed[place, :] = ref[...]
        hidden = dot(ref[...], full[...], (1, 0)) + bias[...]
        square = hidden * hidden
        bend = jnp.tanh(GELU_COEF * (hidden + CUBE * hidden * square))
        active[place, :] = (0.5 * hidden * (1.0 + bend)).astype(BF16)
        slope = 0.5 * (1.0 + bend) + 0.5 * hidden * (1.0 - bend * bend) * (
            GELU_COEF * (1.0 + 3.0 * CUBE * square)
        )
        low = (pulled[place, :] * slope).astype(BF16)
        g_hidden[place, :] = low
        total = total + jnp.sum(low.astype(F32), axis=0, keepdims=True)
        scratch[place, :] = dot(low, full[...], (1, 1))
    bias_row[...] = total
    emit_partials(sc, rows, scratch, own, far, sent, sent_own)


def result_kernel(sc, active, proj, own, far, sent, sent_own, scratch):
    rows = active.shape[0] // WAYS
    scratch[...] = dot(active[...], proj[...], (1, 0))
    emit_partials(sc, rows, scratch, own, far, sent, sent_own)


def piece_of(sc, bits, slot):
    r = 0
    for i, bit in enumerate(bits):
        r |= ((slot >> (2 - i)) & 1) << bit
    return (sc[1] ^ r) & 7


def place_halves(keep, send):
    half = keep.shape[0]
    return [(slot, keep if slot < half else send, slot % half) for slot in range(2 * half)]


def tile_grad_kernel(bits, sc, active, g_out, keep, send, scratch):
    step_rows, step_cols = keep.shape[1], keep.shape[2]
    scratch[...] = dot(active[...], g_out[...], (0, 0)).astype(BF16)
    for slot, ref, at in place_halves(keep, send):
        piece = piece_of(sc, bits, slot)
        ref[at] = scratch[block_rows(piece >> 1, step_rows), block_rows(piece & 1, step_cols)]


def fc_grad_kernel(bits, sc, normed, g_hidden, keep, send, scratch):
    step_rows, step_cols = keep.shape[1], keep.shape[2]
    quarter = step_rows // WAYS
    scratch[...] = dot(normed[...], g_hidden[...], (0, 0)).astype(BF16)
    for slot, ref, at in place_halves(keep, send):
        piece = piece_of(sc, bits, slot)
        for k in range(WAYS):
            start = (sc[0] ^ k) * WAYS + (piece >> 1)
            ref[at, k * quarter : (k + 1) * quarter, :] = scratch[
                block_rows(start, quarter), block_rows(piece & 1, step_cols)
            ]


def second_back_kernel(sc, own, got, far, residual, cot, table, g_residual, g_branch, rows_out):
    upstream = own[...] + got[...].astype(F32) + far[...].astype(F32)
    scaled, inverse = normalise(residual[...])
    through = norm_back(upstream, scaled, inverse, table[3:4, :])
    g_out = jnp.where(valid_rows(sc, table, sc[0], cot.shape[0]), cot[...].astype(F32), 0.0)
    value = g_out + through
    g_residual[...] = value
    low = value.astype(BF16)
    g_branch[...] = low
    rows_out[0:1, :] = jnp.sum(upstream * scaled, axis=0, keepdims=True)
    rows_out[1:2, :] = jnp.sum(upstream, axis=0, keepdims=True)
    rows_out[2:3, :] = jnp.sum(low.astype(F32), axis=0, keepdims=True)


def pull_kernel(sc, b0, b1, b2, b3, out_w, attended, g_branch, do_ext):
    rows = b0.shape[0]
    width = attended.shape[1]
    heads = width // HD
    for k, ref in enumerate((b0, b1, b2, b3)):
        place = member_rows(sc[0] ^ k, rows)
        g_branch[place, :] = ref[...]
        low = dot(ref[...], out_w[...], (1, 1)).astype(BF16)
        product = low.astype(F32) * attended[place, :]
        split = [
            split3(jnp.sum(product[:, h * HD : (h + 1) * HD], axis=-1, keepdims=True))
            for h in range(heads)
        ]
        columns = [split[h][part] for part in range(3) for h in range(heads)]
        do_ext[place, :width] = low
        do_ext[place, width:] = lanes(columns, rows, do_ext.shape[1] - width, BF16)


def pair_back(q, do, kv, allowed, g_q=None, g_kv=None, q_in=None):
    total = kv.shape[0]
    width = kv.shape[1] // 2
    rows = total // WAYS
    heads = width // HD
    for jq in range(WAYS):
        place = slice(jq * rows, (jq + 1) * rows)
        tail_q = q[place, width:].astype(F32)
        tail_do = do[place, width:].astype(F32)
        for h in range(heads):
            cols = slice(h * HD, (h + 1) * HD)
            vcols = slice(width + h * HD, width + (h + 1) * HD)
            qh = q[place, cols]
            doh = do[place, cols]
            pick = lambda t: (
                t[:, h : h + 1] + t[:, heads + h : heads + h + 1]
            ) + t[:, 2 * heads + h : 2 * heads + h + 1]
            lse, delta = pick(tail_q), pick(tail_do)
            grad = None if q_in is None else q_in[place, cols]
            for diag in ((True, False) if jq > 0 else (True,)):
                keys = place if diag else slice(0, jq * rows)
                scores = dot(qh, kv[keys, cols], (1, 1))
                weight = jnp.exp(scores - lse)
                if diag:
                    weight = jnp.where(allowed, weight, 0.0)
                pulled = dot(doh, kv[keys, vcols], (1, 1))
                low = (weight * (pulled - delta)).astype(BF16)
                if g_q is not None:
                    more = dot(low, kv[keys, cols], (1, 0))
                    grad = more if grad is None else grad + more
                if g_kv is not None:
                    g_kv[keys, cols] += dot(low, qh, (0, 0))
                    g_kv[keys, vcols] += dot(weight.astype(BF16), doh, (0, 0))
            if g_q is not None:
                g_q[place, cols] = grad


def ahead_of(rows):
    return lax.broadcasted_iota(jnp.int32, (rows, rows), 1) - lax.broadcasted_iota(
        jnp.int32, (rows, rows), 0
    )


def back_first(sc, q, do, kv, g_q, g_kv):
    g_kv[...] = jnp.zeros_like(g_kv)
    pair_back(q, do, kv, ahead_of(kv.shape[0] // WAYS) <= 0, g_q, g_kv)


def back_queries(sc, step, q, do, kv_other, q_in, g_q):
    limit = jnp.where((sc[2] ^ step) < sc[2], 1, -1)
    rows = kv_other.shape[0] // WAYS
    pair_back(q, do, kv_other, jnp.zeros((rows, rows), jnp.int32) <= limit, g_q=g_q, q_in=q_in)


def back_keys(sc, step, last, refs):
    q_other, do_other, kv, kv_in = refs[:4]
    if last:
        q_in, full, scales, g_proj, own, far, sent, sent_own, sums, g_kv, scratch = refs[4:]
    else:
        (g_kv,) = refs[4:]
    width = kv.shape[1] // 2
    rows = kv.shape[0] // WAYS
    limit = jnp.where(sc[2] < (sc[2] ^ step), 1, -1)
    g_kv[...] = kv_in[...]
    pair_back(q_other, do_other, kv, jnp.zeros((rows, rows), jnp.int32) <= limit, g_kv=g_kv)
    if last:
        g_proj[:, :width] = (q_in[...] * 0.125).astype(BF16)
        g_proj[:, width:] = g_kv[...].astype(BF16)
        scratch[...] = dot(g_proj[...], full[...], (1, 1))
        emit_partials(sc, rows, scratch, own, far, sent, sent_own)
        sums[0:1, :] = jnp.sum(scratch[...] * scales[...].astype(F32), axis=0, keepdims=True)
        sums[1:2, :] = jnp.sum(scratch[...], axis=0, keepdims=True)


def out_grad_kernel(bits, sc, attended, g_branch, slots, scratch):
    scratch[...] = dot(attended[...], g_branch[...], (0, 0)).astype(BF16)
    rows, cols = scratch.shape[0] // WAYS, scratch.shape[1] // 2
    tall, rest = 2 * rows // 3, rows // 3
    for slot in range(PIECES):
        piece = piece_of(sc, bits, slot)
        block = scratch[block_rows(piece >> 1, rows), block_rows(piece & 1, cols)]
        slots[slot, :, :cols] = block[:tall]
        slots[slot, :rest, cols:] = block[tall:, : cols // 2]
        slots[slot, rest:, cols:] = block[tall:, cols // 2 :]


def qkv_grad_kernel(
    near_bits, far_bits, sc, normed, g_proj, out, two, proj, fc, one, nk, ns, vec, wk, ws, scratch, rows_out
):
    half = PIECES // 2
    step = scratch.shape[0] // WAYS // PIECES
    width = nk.shape[1] // 3
    scratch[...] = dot(normed[...], g_proj[...], (0, 0))
    for base, bits, keep, send in ((2, far_bits, wk, ws), (0, near_bits, nk, ns)):
        size = keep.shape[0] // half
        for slot in range(PIECES):
            ref, at = (keep, slot) if slot < half else (send, slot - half)
            piece = piece_of(sc, bits, slot)
            for i in range(2):
                start = (sc[0] ^ (base + i)) * PIECES + piece
                ref[at * size + i * step : at * size + (i + 1) * step, :] = scratch[
                    block_rows(start, step), :
                ].astype(BF16)
            if base == 2:
                ref[at * size + 2 * step : (at + 1) * size, :] = out[slot]
    rows_out[0:2, :] = one[...]
    rows_out[2:3, :] = two[2:3, :]
    rows_out[3:5, :] = two[0:2, :]
    rows_out[5:6, :] = proj[...]
    rows_out[6:8, :] = jnp.zeros_like(rows_out[6:8, :])
    rows_out[8:12, :] = jnp.zeros_like(rows_out[8:12, :])
    total = jnp.sum(g_proj[...].astype(F32), axis=0, keepdims=True)
    for block in range(WAYS):

        @pl.when(sc[0] == block)
        def _(block=block):
            place = slice(block * width, (block + 1) * width)
            rows_out[6:7, place] = total[:, :width]
            rows_out[7:8, place] = total[:, 2 * width :]
            rows_out[8 + block : 9 + block, :] = fc[...]

    for row in range(VECTOR_ROWS):
        for block in range(WAYS):
            vec[vector_place(row, block, width)] = rows_out[
                row : row + 1, block * width : (block + 1) * width
            ].astype(BF16)
    ns[nk.shape[0] :, :] = vec[...]


def first_back_kernel(sc, own, got, far, x, table, g_residual, r_own, r_got, r_far, residual, out):
    upstream = own[...] + got[...].astype(F32) + far[...].astype(F32)
    scaled, inverse = normalise(x[...].astype(F32))
    through = norm_back(upstream, scaled, inverse, table[0:1, :])
    out[1] = (g_residual[...] + through).astype(BF16)
    value = (
        residual[...] + r_own[...] + r_got[...].astype(F32) + r_far[...].astype(F32) + table[5:6, :]
    )
    out[0] = jnp.where(valid_rows(sc, table, sc[0], x.shape[0]), value, 0.0).astype(BF16)


def slots_in(near, far):
    half = near.shape[0]
    return [(slot, near if slot < half else far, slot % half) for slot in range(2 * half)]


def proj_final_kernel(bits, sc, near, far, out):
    rows, cols = near.shape[1:]
    for slot, ref, at in slots_in(near, far):
        piece = piece_of(sc, bits, slot)
        out[block_rows(piece >> 1, rows), block_rows(piece & 1, cols)] = ref[at].astype(F32)


def fc_final_kernel(bits, sc, near, far, out):
    quarter, step_cols = near.shape[1] // WAYS, near.shape[2]
    for slot, ref, at in slots_in(near, far):
        piece = piece_of(sc, bits, slot)
        for k in range(WAYS):
            wide = block_rows((sc[0] ^ k) * 2 + (piece & 1), step_cols)
            out[block_rows(piece >> 1, quarter), wide] = ref[
                at, k * quarter : (k + 1) * quarter
            ].astype(F32)


def qkv_final_kernel(near_bits, far_bits, sc, nn, nf, wn, wf, out, out_out):
    step, width = nn.shape[1] // 2, nn.shape[2] // 3
    cols = out_out.shape[1] // 2
    rows = out_out.shape[0] // WAYS
    tall, rest = 2 * rows // 3, rows // 3
    for slot, ref, at in slots_in(wn, wf):
        piece = piece_of(sc, far_bits, slot)
        block = ref[at, 2 * step :].astype(F32)
        start = (piece >> 1) * rows
        left = pl.ds(pl.multiple_of((piece & 1) * cols, cols), cols)
        low = pl.ds(pl.multiple_of(start, 8), tall)
        out_out[low, left] = block[:, :cols]
        high = pl.ds(pl.multiple_of(start + tall, 8), rest)
        out_out[high, left] = jnp.concatenate([block[:rest, cols:], block[rest:, cols:]], axis=1)
    for member in range(WAYS):

        @pl.when(sc[0] == member)
        def _(member=member):
            for base, bits, near, far in ((0, near_bits, nn, nf), (2, far_bits, wn, wf)):
                for slot, ref, at in slots_in(near, far):
                    place = block_rows(piece_of(sc, bits, slot), step)
                    for i in range(2):
                        piece = ref[at, i * step : (i + 1) * step].astype(F32)
                        for part in range(3):
                            start = (part * WAYS + (member ^ (base + i))) * width
                            out[place, start : start + width] = piece[
                                :, part * width : (part + 1) * width
                            ]


def body(
    inputs, lengths, ln1_gain, ln1_bias, qkv_weight, qv_bias, out_weight, out_bias,
    ln2_gain, ln2_bias, fc_weight, fc_bias, proj_weight, proj_bias, cotangent,
):
    group = lax.axis_size("ctx")
    members = group // WAYS
    assert lax.axis_size("fsdp") == WAYS and inputs.shape[0] == 1
    assert group % PIECES == 0 and group & (group - 1) == 0
    f, c = lax.axis_index("fsdp"), lax.axis_index("ctx")
    rows, width = inputs.shape[1:]
    head_width = width // WAYS
    hidden_width = fc_bias.shape[0]
    total = rows * WAYS
    half = PIECES // 2
    scalars = jnp.stack(
        [f, c, c % members, jnp.asarray(members), lengths[0], turned(c // members)]
    ).astype(jnp.int32)
    order = Order(scalars)

    vectors = [ln1_gain, ln1_bias, out_bias, ln2_gain, ln2_bias, proj_bias, qv_bias, fc_bias]
    w_qkv = order.call(
        qkv_columns_kernel,
        [
            shape((head_width // (2 if i in (2, 3) else 1), 3 * head_width), BF16)
            for i in range(5)
        ],
        [qkv_weight],
        name="qkv_columns",
    )
    small, fc_row = order.call(
        small_kernel,
        [shape((16, head_width), BF16), shape((1, hidden_width), F32)],
        [jnp.concatenate(vectors)],
        name="small",
    )
    small_all = [small, f_xor(small, 1), f_xor(small, 2), f_xor(small, 3)]
    x_own = swap_layout(inputs[0])
    cot_own = swap_layout(after(cotangent[0], x_own))
    far2, far2_low = f_xor(w_qkv[2], 2), f_xor(w_qkv[3], 2)
    far3, near = f_xor(w_qkv[4], 3), f_xor(w_qkv[1], 1)
    w_qkv = [w_qkv[0], near, far2, far2_low, far3]
    x_far = f_xor(after(x_own, far2, far2_low, small), 2)
    x_all = [x_own, f_xor(x_own, 1), x_far, f_xor(after(x_far, far3), 1)]
    table, qkv_bias = order.call(
        table_kernel,
        [shape((8, width), F32), shape((1, 3 * head_width), F32)],
        small_all,
        flops=4 * 10**9,
        name="table",
        late=[x_own],
    )
    w_fc = order.call(
        fc_columns_kernel,
        [shape((head_width, hidden_width), BF16)] * WAYS,
        [fc_weight],
        name="fc_columns",
    )
    far2, far3, near = f_xor(w_fc[2], 2), f_xor(w_fc[3], 3), f_xor(w_fc[1], 1)
    w_fc = [w_fc[0], near, far2, far3]

    normed_one, scales_one, qkv_full, q, kv = order.call(
        qkv_kernel,
        [
            shape((total, width), BF16),
            shape((total, width), BF16),
            shape((width, 3 * head_width), BF16),
            shape((total, head_width), BF16),
            shape((total, 2 * head_width), BF16),
        ],
        [*x_all, *w_qkv, table, qkv_bias],
        flops=2 * total * width * 3 * head_width,
        name="qkv",
    )
    kv_other = [kv] + [c_xor(kv, r) for r in range(1, members)]

    partials = [shape((rows, width), F32)] * 2 + [shape((rows, width), BF16)] * 2
    state = []
    for r in range(members):
        first, last = r == 0, r == members - 1
        if r == 1:
            cot_all = gather_f(after(cot_own, state[1]))
        if last:
            outs = [
                shape((total, head_width), F32),
                shape((total, head_width), BF16),
                shape((total, head_width + 64), BF16),
                *partials,
            ]
            scratch = [pltpu.VMEM((total, width), F32)]
            extra = [out_weight]
        else:
            outs = [shape((total, head_width), F32), shape((total, 128), F32)]
            scratch, extra = [], []

        def kernel(sc_ref, *refs, r=r, first=first, last=last):
            attend(sc_ref, r, first, last, refs)

        state = order.call(
            kernel,
            outs,
            [q, kv_other[r], *state, *extra],
            scratch,
            flops=4 * total * total * head_width,
            name=f"attend{min(r, 1)}",
            late=[w_fc[2], cot_own] if last else [],
        )
    attended, attended_low, q_ext, *branch = state
    branch = order.scatter_f(*branch)
    q_other = [q_ext] + [c_xor(q_ext, r) for r in range(1, members)]
    (fc_full,) = order.call(
        assemble_kernel,
        [shape((width, hidden_width), BF16)],
        w_fc,
        name="fc_assemble",
        late=[cot_all[2]],
    )
    branch = order.scatter_f_far(branch)
    residual, normed_two = order.call(
        second_norm_kernel,
        [shape((rows, width), F32), shape((rows, width), BF16)],
        [*branch, x_own, table],
        name="norm2",
    )
    normed_two_all = gather_f(normed_two)
    g_out, pulled, proj_row = order.call(
        cot_kernel,
        [
            shape((total, width), BF16),
            shape((total, hidden_width), F32),
            shape((1, width), F32),
        ],
        [*cot_all, proj_weight, table],
        flops=2 * total * width * hidden_width,
        name="cot",
    )
    normed_two_full, active, g_hidden, fc_rows, *g_two = order.call(
        feed_kernel,
        [
            shape((total, width), BF16),
            shape((total, hidden_width), BF16),
            shape((total, hidden_width), BF16),
            shape((1, hidden_width), F32),
            *partials,
        ],
        [*normed_two_all, fc_full, fc_row, pulled],
        [pltpu.VMEM((total, width), F32)],
        flops=4 * total * width * hidden_width,
        name="feed",
        late=q_other[1:],
    )
    g_two = order.scatter_f(*g_two)
    slots = [shape((half, head_width, width // 2), BF16)] * 2
    proj_keep, send = order.call(
        functools.partial(tile_grad_kernel, OTHER),
        slots,
        [active, g_out],
        [pltpu.VMEM((width, width), BF16)],
        flops=2 * total * width * hidden_width,
        name="proj_grad",
    )
    proj_got = c_xor(send, 1 << OTHER[0])
    g_two = order.scatter_f_far(g_two)
    fc_keep, send = order.call(
        functools.partial(fc_grad_kernel, ONE),
        slots,
        [normed_two_full, g_hidden],
        [pltpu.VMEM((width, width), BF16)],
        flops=2 * total * width * hidden_width,
        name="fc_grad",
    )
    fc_got = c_xor(send, 1 << ONE[0])
    result = order.call(
        result_kernel,
        partials,
        [active, proj_weight],
        [pltpu.VMEM((total, width), F32)],
        flops=2 * total * width * hidden_width,
        name="result",
    )
    result = order.scatter_f(*result)
    g_residual, g_branch, two_rows = order.call(
        second_back_kernel,
        [shape((rows, width), F32), shape((rows, width), BF16), shape((3, width), F32)],
        [*g_two, residual, cot_own, table],
        name="norm2_back",
    )
    g_branch_all = gather_f(g_branch)
    g_branch_full, do_ext = order.call(
        pull_kernel,
        [shape((total, width), BF16), shape((total, head_width + 64), BF16)],
        [*g_branch_all, out_weight, attended],
        flops=2 * total * width * head_width,
        name="pull",
    )
    do_other = [do_ext] + [c_xor(do_ext, r) for r in range(1, members)]
    step = head_width // PIECES
    out_rows = head_width // 6
    (out_slots,) = order.call(
        functools.partial(out_grad_kernel, ONE),
        [shape((PIECES, out_rows, 3 * head_width), BF16)],
        [attended_low, g_branch_full],
        [pltpu.VMEM((head_width, width), BF16)],
        flops=2 * total * width * head_width,
        name="out_grad",
    )
    tile = (head_width, width // 2)
    proj_keep, proj_send, fc_keep, fc_send = order.call(
        mlp_fold_kernel,
        [shape((2, *tile), BF16)] * 4,
        [proj_keep, proj_got, fc_keep, fc_got],
        name="mlp_fold",
    )
    result = order.scatter_f_far(result)
    proj_got, fc_got = c_xor(proj_send, 1 << OTHER[1]), c_xor(fc_send, 1 << ONE[1])
    g_q, g_kv = order.call(
        back_first,
        [shape((total, head_width), F32), shape((total, 2 * head_width), F32)],
        [q_ext, do_ext, kv],
        flops=10 * total * total * head_width,
        name="back0",
    )
    mlp_keep, mlp_send = order.call(
        mlp_meet_kernel,
        [shape((2, *tile), BF16)] * 2,
        [proj_keep, proj_got, fc_keep, fc_got],
        name="mlp_meet",
    )
    mlp_got = c_xor(mlp_send, 1 << Z2)
    for r in range(1, members):

        def kernel(sc_ref, *refs, r=r):
            back_queries(sc_ref, r, *refs)

        (g_q,) = order.call(
            kernel,
            [shape(g_q.shape, F32)],
            [q_ext, do_ext, kv_other[r], g_q],
            flops=6 * total * total * head_width,
            name="back_q",
        )
    for r in range(1, members):
        last = r == members - 1
        outs, scratch, extra = [shape(g_kv.shape, F32)], [], []
        if last:
            scratch = [pltpu.VMEM(g_kv.shape, F32), pltpu.VMEM((total, width), F32)]
            outs = [shape((total, 3 * head_width), BF16), *partials, shape((2, width), F32)]
            extra = [g_q, qkv_full, scales_one]

        def kernel(sc_ref, *refs, r=r, last=last):
            back_keys(sc_ref, r, last, refs)

        grads = order.call(
            kernel,
            outs,
            [q_other[r], do_other[r], kv, g_kv, *extra],
            scratch,
            flops=8 * total * total * head_width,
            name="back_kv",
        )
        g_kv = grads[0]
    g_proj, *g_one, one_rows = grads
    g_one = order.scatter_f(*g_one)
    quarter = head_width // WAYS
    pieces = order.call(
        mlp_last_kernel,
        [shape(tile, BF16)] + [shape((quarter, tile[1]), BF16)] * WAYS,
        [mlp_keep, mlp_got],
        name="mlp_last",
    )
    proj_piece, *fc_pieces = [others(piece) for piece in pieces]
    fc_pieces = [fc_pieces[0]] + [f_xor(fc_pieces[k], k) for k in range(1, WAYS)]
    near_rows, far_rows, vec_rows, cols = 2 * step, 2 * step + out_rows, 16, 3 * head_width
    near_keep, near_send, vec, far_keep, far_send = order.call(
        functools.partial(qkv_grad_kernel, OTHER, ONE),
        [
            shape((half * near_rows, cols), BF16),
            shape((half * near_rows + vec_rows, cols), BF16),
            shape((vec_rows, cols), BF16),
            shape((half * far_rows, cols), BF16),
            shape((half * far_rows, cols), BF16),
        ],
        [normed_one, g_proj, out_slots, two_rows, proj_row, fc_rows, one_rows],
        [pltpu.VMEM((width, cols), F32), pltpu.VMEM((VECTOR_ROWS, width), F32)],
        flops=2 * total * width * cols,
        name="qkv_grad",
    )
    near_got, far_got = c_xor(near_send, 1 << OTHER[0]), c_xor(far_send, 1 << ONE[0])
    g_one = order.scatter_f_far(g_one)
    (mlp_own,) = order.call(
        mlp_join_kernel,
        [shape((2, *tile), BF16)],
        [proj_piece, *fc_pieces],
        name="mlp_join",
    )
    mlp_got = c_xor(mlp_own, 1 << Z2)
    near_keep, vec, near_send, far_keep, far_send = order.call(
        qkv_fold_kernel,
        [
            shape((2 * near_rows, cols), BF16),
            shape((vec_rows, cols), BF16),
            shape((2 * near_rows + vec_rows, cols), BF16),
            shape((2 * far_rows, cols), BF16),
            shape((2 * far_rows, cols), BF16),
        ],
        [near_keep, vec, near_got, far_keep, far_got],
        name="qkv_fold",
    )
    near_got, far_got = c_xor(near_send, 1 << OTHER[1]), c_xor(far_send, 1 << ONE[1])
    (both,) = order.call(
        first_back_kernel,
        [shape((2, rows, width), BF16)],
        [*g_one, x_own, table, g_residual, *result, residual],
        name="norm1_back",
    )
    both = swap_layout(both)
    keep, vec, send = order.call(
        qkv_meet_kernel,
        [
            shape((near_rows + far_rows, cols), BF16),
            shape((vec_rows, cols), BF16),
            shape((near_rows + far_rows + vec_rows, cols), BF16),
        ],
        [near_keep, vec, near_got, far_keep, far_got],
        name="qkv_meet",
    )
    got = c_xor(send, 1 << Z2)
    proj_own, fc_own = order.call(
        mlp_part_kernel, [shape((2, *tile), BF16)] * 2, [mlp_own, mlp_got], name="mlp_part"
    )
    proj_got, fc_got = c_xor(proj_own, 1 << OTHER[1]), c_xor(fc_own, 1 << ONE[1])
    proj_own, fc_own = order.call(
        grow_kernel,
        [shape((half, *tile), BF16)] * 2,
        [proj_own, proj_got, fc_own, fc_got],
        name="mlp_grow",
        late=[got],
    )
    proj_got, fc_got = c_xor(proj_own, 1 << OTHER[0]), c_xor(fc_own, 1 << ONE[0])
    piece, vec = order.call(
        qkv_last_kernel,
        [shape((near_rows + far_rows, cols), BF16), shape((vec_rows, cols), BF16)],
        [keep, vec, got],
        name="qkv_last",
    )
    piece, vec = others(piece), others(vec)
    s1, s2, s3 = order.call(
        exchange_kernel, [shape((step + vec_rows, cols), BF16)] * 3, [piece, vec], name="exchange"
    )
    r2, r3, r1 = f_xor(s2, 2), f_xor(s3, 3), f_xor(s1, 1)
    joined, *mine, grad_qv, grad_fc_bias = order.call(
        join_kernel,
        [
            shape((near_rows + far_rows, cols), BF16),
            *[shape((head_width,), F32)] * 6,
            shape((2 * head_width,), F32),
            shape((hidden_width,), F32),
        ],
        [piece, vec, r1, r2, r3],
        [pltpu.VMEM((vec_rows, cols), F32)],
        name="join",
    )
    got = c_xor(joined, 1 << Z2)
    near_own, far_own = order.call(
        qkv_part_kernel,
        [shape((2, near_rows, cols), BF16), shape((2, far_rows, cols), BF16)],
        [joined, got],
        name="qkv_part",
    )
    near_got, far_got = c_xor(near_own, 1 << OTHER[1]), c_xor(far_own, 1 << ONE[1])
    def finish(kernel, dims, arrays, name):
        return order.call(kernel, [shape(d, F32) for d in dims], arrays, name=name, direct=True)

    (grad_fc,) = finish(
        functools.partial(fc_final_kernel, ONE),
        [(head_width, WAYS * hidden_width)],
        [fc_own, fc_got],
        "fc_final",
    )
    (grad_proj,) = finish(
        functools.partial(proj_final_kernel, OTHER),
        [(hidden_width, width)],
        [proj_own, proj_got],
        "proj_final",
    )
    near_own, far_own = order.call(
        grow_kernel,
        [shape((half, near_rows, cols), BF16), shape((half, far_rows, cols), BF16)],
        [near_own, near_got, far_own, far_got],
        name="qkv_grow",
        late=[both],
    )
    near_got, far_got = c_xor(near_own, 1 << OTHER[0]), c_xor(far_own, 1 << ONE[0])

    grad_qkv, grad_out = finish(
        functools.partial(qkv_final_kernel, OTHER, ONE),
        [(head_width, 3 * width), (head_width, width)],
        [near_own, near_got, far_own, far_got],
        "qkv_final",
    )
    return (
        both[0:1],
        both[1:2],
        mine[0],
        mine[1],
        grad_qkv,
        grad_qv,
        grad_out,
        mine[2],
        mine[3],
        mine[4],
        grad_fc,
        grad_fc_bias,
        grad_proj,
        mine[5],
    )


def solution(mesh):
    tokens, rows, vector = P("fsdp", "ctx", None), P("fsdp", None), P("fsdp")
    in_specs = (
        tokens, vector, vector, vector, rows, vector, rows, vector,
        vector, vector, rows, vector, rows, vector, tokens,
    )
    out_specs = (
        tokens, tokens, vector, vector, rows, vector, rows, vector,
        vector, vector, rows, vector, rows, vector,
    )
    return jax.shard_map(body, mesh=mesh, in_specs=in_specs, out_specs=out_specs, check_vma=False)
```

```python
import functools

import jax
import jax.numpy as jnp
from jax import lax
from jax.experimental import pallas as pl
from jax.experimental.pallas import tpu as pltpu
from jax.sharding import PartitionSpec as P

HD = 64
EPSILON = 1e-05
NEGATIVE = -1e30
GELU_COEF = 0.7978845608028654
CUBE = 0.044715
F32 = jnp.float32
BF16 = jnp.bfloat16
WAYS = 4
PIECES = 8
VMEM_LIMIT = 24 * 1024 * 1024


def f_xor(x, k):
    n = lax.axis_size("fsdp")
    return lax.ppermute(x, "fsdp", [(i, i ^ k) for i in range(n)])


def c_xor(x, k):
    n = lax.axis_size("ctx")
    return lax.ppermute(x, "ctx", [(i, i ^ k) for i in range(n)])


def turned(index):
    return ((index & 1) << 1) | (index >> 1)


def swap_layout(x):
    group = lax.axis_size("ctx")
    members = group // WAYS
    perm = []
    for f in range(WAYS):
        for c in range(group):
            j, m = divmod(c, members)
            perm.append((f * group + c, turned(j) * group + turned(f) * members + m))
    return lax.ppermute(x, ("fsdp", "ctx"), perm)


def after(value, *others):
    return lax.optimization_barrier((value, *others))[0]


def gather_f(x, until=lambda far: far):
    far = f_xor(x, 2)
    near = f_xor(x, 1)
    return [x, near, far, f_xor(until(far), 1)]


class Order:
    def __init__(self, scalars):
        self.scalars = scalars
        self.token = None

    def tie(self, value):
        if self.token is None:
            return value
        return lax.optimization_barrier((value, self.token))[0]

    def mark(self, value):
        self.token = value
        return value

    def call(self, kernel, outs, args, scratch=(), flops=0, name=None, direct=False, late=()):
        scalars = after(self.tie(self.scalars), *late)
        got = call(kernel, outs, [scalars, *args], scratch, flops, name, direct)
        self.mark(min(got, key=lambda value: value.size))
        return got

    def scatter_f(self, kept_own, kept_far, sent_far, sent_own):
        return kept_own, kept_far, f_xor(sent_far, 1), f_xor(sent_own, 1)

    def scatter_f_far(self, state, late=()):
        kept_own, kept_far, got_far, got_own = state
        (far,) = self.call(
            far_kernel, [shape(kept_own.shape, BF16)], [kept_far, got_far], name="far", late=late
        )
        return kept_own, got_own, f_xor(far, 2)


X, Z1, Z2 = 0, 1, 2
ONE, OTHER = (X, Z1, Z2), (Z1, X, Z2)


def others(value):
    bit = 3
    while (1 << bit) < lax.axis_size("ctx"):
        value = (value.astype(F32) + c_xor(value, 1 << bit).astype(F32)).astype(BF16)
        bit += 1
    return value


def call(kernel, outs, args, scratch=(), flops=0, name=None, direct=False):
    vmem = pl.BlockSpec(memory_space=pltpu.VMEM)
    moved = sum(a.size * a.dtype.itemsize for a in args) + sum(
        o.size * o.dtype.itemsize for o in outs
    )
    return pl.pallas_call(
        kernel,
        out_shape=tuple(outs),
        in_specs=[pl.BlockSpec(memory_space=pltpu.SMEM)] + [vmem] * (len(args) - 1),
        out_specs=tuple([pl.BlockSpec() if direct else vmem] * len(outs)),
        scratch_shapes=list(scratch),
        cost_estimate=pl.CostEstimate(flops=flops, bytes_accessed=moved, transcendentals=0),
        compiler_params=pltpu.CompilerParams(vmem_limit_bytes=VMEM_LIMIT),
        name=name,
    )(*args)


def shape(dims, dtype):
    return jax.ShapeDtypeStruct(dims, dtype)


def dot(a, b, contract):
    return lax.dot_general(a, b, ((contract[0:1], contract[1:2]), ((), ())), preferred_element_type=F32)


def block_rows(index, size):
    return pl.ds(pl.multiple_of(index * size, size), size)


def member_rows(member, size):
    return block_rows(turned(member), size)


def normalise(values):
    centred = values - jnp.mean(values, axis=-1, keepdims=True)
    inverse = lax.rsqrt(jnp.mean(centred * centred, axis=-1, keepdims=True) + EPSILON)
    return centred * inverse, inverse


def norm_back(upstream, scaled, inverse, gain):
    weighted = upstream * gain
    return inverse * (
        weighted
        - jnp.mean(weighted, axis=-1, keepdims=True)
        - scaled * jnp.mean(weighted * scaled, axis=-1, keepdims=True)
    )


def valid_rows(sc, table, chunk, rows):
    place = (turned(chunk) * sc[3] + sc[2]) * rows + lax.broadcasted_iota(jnp.int32, (rows, 1), 0)
    return place.astype(F32) < table[6:7, 0:1]


def emit_partials(sc, rows, value_ref, own_ref, far_ref, sent_far, sent_own):
    f = sc[0]
    own_ref[...] = value_ref[member_rows(f, rows), :]
    far_ref[...] = value_ref[member_rows(f ^ 2, rows), :]
    sent_own[...] = value_ref[member_rows(f ^ 1, rows), :].astype(BF16)
    sent_far[...] = value_ref[member_rows(f ^ 3, rows), :].astype(BF16)


def far_kernel(sc, kept, got, out):
    out[...] = (kept[...] + got[...].astype(F32)).astype(BF16)


def added(a, b):
    return (a.astype(F32) + b.astype(F32)).astype(BF16)


def fold_into(keep, got, kept, sent):
    half = keep.shape[0] // 2
    sent[:half] = added(keep[half:], got[half : 2 * half])
    kept[...] = added(keep[:half], got[:half])


def mlp_fold_kernel(sc, proj, proj_got, fc, fc_got, proj_kept, proj_sent, fc_kept, fc_sent):
    fold_into(proj, proj_got, proj_kept, proj_sent)
    fold_into(fc, fc_got, fc_kept, fc_sent)


def mlp_meet_kernel(sc, proj, proj_got, fc, fc_got, kept, sent):
    for i, (keep, got) in enumerate(((proj, proj_got), (fc, fc_got))):
        kept[i] = added(keep[0], got[0])
        sent[i] = added(keep[1], got[1])


def mlp_last_kernel(sc, keep, got, proj, *pieces):
    proj[...] = added(keep[0], got[0])
    rows = pieces[0].shape[0]
    for i, piece in enumerate(pieces):
        place = slice(i * rows, (i + 1) * rows)
        piece[...] = added(keep[1, place], got[1, place])


def mlp_join_kernel(sc, p0, p1, p2, p3, out):
    rows = p0.shape[0]
    for i, piece in enumerate((p0, p1, p2, p3)):
        out[i * rows : (i + 1) * rows] = piece[...]


def mlp_part_kernel(sc, proj_own, proj_got, fc_own, fc_got, proj, fc):
    for out, own, got in ((proj, proj_own, proj_got), (fc, fc_own, fc_got)):
        out[0] = own[...]
        out[1] = got[...]


def grow_kernel(sc, a, a_got, b, b_got, a_out, b_out):
    for own, got, out in ((a, a_got, a_out), (b, b_got, b_out)):
        count = own.shape[0]
        out[:count] = own[...]
        out[count:] = got[...]


def qkv_fold_kernel(sc, near, vec, near_got, far, far_got, near_kept, vec_out, near_sent, far_kept, far_sent):
    fold_into(near, near_got, near_kept, near_sent)
    both = added(vec[...], near_got[near.shape[0] :])
    near_sent[near.shape[0] // 2 :] = both
    vec_out[...] = both
    fold_into(far, far_got, far_kept, far_sent)


def qkv_meet_kernel(sc, near, vec, near_got, far, far_got, kept, vec_out, sent):
    rows, more = near.shape[0] // 2, far.shape[0] // 2
    kept[:rows] = added(near[:rows], near_got[:rows])
    sent[:rows] = added(near[rows:], near_got[rows : 2 * rows])
    kept[rows:] = added(far[:more], far_got[:more])
    sent[rows : rows + more] = added(far[more:], far_got[more:])
    both = added(vec[...], near_got[2 * rows :])
    sent[rows + more :] = both
    vec_out[...] = both


def qkv_last_kernel(sc, keep, vec, got, piece, vec_out):
    count = keep.shape[0]
    piece[...] = added(keep[...], got[:count])
    vec_out[...] = added(vec[...], got[count:])


def exchange_kernel(sc, piece, vec, s1, s2, s3):
    rows = s1.shape[0] - vec.shape[0]
    for k, sent in ((2, s2), (3, s3), (1, s1)):
        sent[:rows] = piece[k * rows : (k + 1) * rows]
        sent[rows:] = vec[...]


def qkv_part_kernel(sc, own, got, near, far):
    rows = near.shape[1]
    for i, ref in enumerate((own, got)):
        near[i] = ref[:rows]
        far[i] = ref[rows:]


VECTOR_ROWS = 12


def vector_place(row, block, width):
    at = row * WAYS + block
    return slice(at // 3, at // 3 + 1), slice((at % 3) * width, (at % 3 + 1) * width)


def join_kernel(sc, piece, vec, r1, r2, r3, joined, *rest):
    *mine, qv, fc, scratch = rest
    rows, width = r1.shape[0] - vec.shape[0], piece.shape[1] // 3
    joined[:rows] = piece[:rows]
    for i, got in ((1, r1), (2, r2), (3, r3)):
        joined[i * rows : (i + 1) * rows] = got[:rows]
    joined[WAYS * rows :] = piece[WAYS * rows :]
    scratch[...] = (
        vec[...].astype(F32)
        + r1[rows:].astype(F32)
        + r2[rows:].astype(F32)
        + r3[rows:].astype(F32)
    )
    for block in range(WAYS):

        @pl.when(sc[0] == block)
        def _(block=block):
            for row in range(6):
                mine[row][...] = scratch[vector_place(row, block, width)].reshape(width)
            for i in range(2):
                at = 2 * block + i
                qv[i * width : (i + 1) * width] = scratch[
                    vector_place(6 + at // WAYS, at % WAYS, width)
                ].reshape(width)
            for i in range(WAYS):
                fc[i * width : (i + 1) * width] = scratch[
                    vector_place(8 + block, i, width)
                ].reshape(width)


def small_kernel(sc, vectors, out, bias):
    width = out.shape[1]
    out[...] = jnp.zeros_like(out)
    length = sc[4]
    out[8:9, :] = jnp.full((1, width), length >> 6, jnp.int32).astype(BF16)
    out[9:10, :] = jnp.full((1, width), length & 63, jnp.int32).astype(BF16)
    for i in range(8):
        out[i : i + 1, :] = vectors[i * width : (i + 1) * width].reshape(1, width)
    bias[...] = vectors[8 * width :].reshape(bias.shape).astype(F32)


def table_kernel(sc, s0, s1, s2, s3, table, bias):
    width = s0.shape[1]
    table[7:8, :] = jnp.zeros((1, table.shape[1]), F32)
    bias[...] = jnp.zeros_like(bias)
    odd = (sc[0] & 1) == 1
    for k, ref in enumerate((s0, s1, s2, s3)):
        values = ref[...].astype(F32)
        j = sc[0] ^ k
        pair = jnp.where(odd, values[7:8], values[6:7])
        for block in range(WAYS):

            @pl.when(j == block)
            def _(values=values, block=block):
                table[0:6, block * width : (block + 1) * width] = values[0:6]

        @pl.when(j == (sc[0] >> 1))
        def _(pair=pair):
            bias[:, :width] = pair

        @pl.when(j == 2 + (sc[0] >> 1))
        def _(pair=pair):
            bias[:, 2 * width :] = pair

        @pl.when(j == sc[5])
        def _(values=values):
            row = values[8:9] * 64.0 + values[9:10]
            for block in range(WAYS):
                table[6:7, block * width : (block + 1) * width] = row


def half_of(sc, rows):
    return block_rows(sc[1] & 1, rows)


def qkv_columns_kernel(sc, weight, w0, w1, w2, w3):
    width = w0.shape[1] // 3
    half = half_of(sc, w2.shape[0])
    for k, ref in ((2, w2), (3, w3), (1, w1), (0, w0)):
        for block in range(WAYS):

            @pl.when((sc[0] ^ k) == block)
            def _(k=k, ref=ref, block=block):
                for part in range(3):
                    base = part * WAYS * width + block * width
                    source = weight[half if k > 1 else slice(None), base : base + width]
                    ref[:, part * width : (part + 1) * width] = source


def fc_columns_kernel(sc, weight, w0, w1, w2, w3):
    for k, ref in ((2, w2), (3, w3), (1, w1), (0, w0)):
        ref[...] = weight[:, block_rows(sc[0] ^ k, ref.shape[1])]


def assemble(sc, near, far, full):
    for k, ref in enumerate(near):
        full[block_rows(sc[0] ^ k, ref.shape[0]), :] = ref[...]
    mine = sc[1] & 1
    for k, halves in ((2, far[:2]), (3, far[2:])):
        for i, ref in enumerate(halves):
            full[block_rows((sc[0] ^ k) * 2 + (mine ^ i), ref.shape[0]), :] = ref[...]


def fetched(w0, w1, w2, w3):
    far2, far3 = f_xor(w2, 2), f_xor(w3, 3)
    return [w0, f_xor(w1, 1), far2, c_xor(far2, 1 << X), far3, c_xor(far3, 1 << X)]


def cot_kernel(sc, c0, c1, c2, c3, proj, table, g_out, pulled, bias_row):
    rows = c0.shape[0]
    for k, ref in enumerate((c0, c1, c2, c3)):
        j = sc[0] ^ k
        kept = jnp.where(valid_rows(sc, table, j, rows), ref[...].astype(F32), 0.0)
        if k == 0:
            bias_row[...] = jnp.sum(kept, axis=0, keepdims=True)
        low = kept.astype(BF16)
        g_out[member_rows(j, rows), :] = low
        pulled[member_rows(j, rows), :] = dot(low, proj[...], (1, 1))


def qkv_kernel(sc, x0, x1, x2, x3, w0, w1, w2, w2_x, w3, w3_x, table, bias, normed, scales, full, q, kv):
    rows = x0.shape[0]
    assemble(sc, (w0, w1), (w2, w2_x, w3, w3_x), full)
    for k, ref in enumerate((x0, x1, x2, x3)):
        place = member_rows(sc[0] ^ k, rows)
        scaled, _ = normalise(ref[...].astype(F32))
        low = (scaled * table[0:1, :] + table[1:2, :]).astype(BF16)
        normed[place, :] = low
        scales[place, :] = scaled.astype(BF16)
        got = (dot(low, full[...], (1, 0)) + bias[...]).astype(BF16)
        width = q.shape[1]
        q[place, :] = got[:, :width] * jnp.asarray(0.125, BF16)
        kv[place, :] = got[:, width:]


def split3(value):
    high = value.astype(BF16)
    rest = value - high.astype(F32)
    mid = rest.astype(BF16)
    low = (rest - mid.astype(F32)).astype(BF16)
    return high, mid, low


def lanes(columns, rows, width, dtype):
    lane = lax.broadcasted_iota(jnp.int32, (rows, width), 1)
    out = jnp.zeros((rows, width), F32)
    for i, column in enumerate(columns):
        out = jnp.where(lane == i, column.astype(F32), out)
    return out.astype(dtype)


def joined(ref, base, count, h):
    total = None
    for part in range(3):
        column = base + part * count + h
        piece = ref[:, column : column + 1].astype(F32)
        total = piece if total is None else total + piece
    return total


def threshold(sc, other):
    return jnp.where(other == sc[2], 0, jnp.where(other < sc[2], 1 << 20, -(1 << 20)))


def mask_last(values, allowed, other):
    rows = allowed.shape[1]
    masked = jnp.where(allowed, values[:, values.shape[1] - rows :], other)
    if values.shape[1] == rows:
        return masked
    return jnp.concatenate([values[:, : values.shape[1] - rows], masked], axis=1)


def attend(sc, step, first, last, refs):
    if first:
        q, kv = refs[:2]
        state_in = None
        rest = refs[2:]
    else:
        q, kv, acc_in, stat_in = refs[:4]
        rest = refs[4:]
    if last:
        out_w, attended, low, q_ext, own, far, sent, sent_own, scratch = rest
    else:
        acc_out, stat_out = rest
    total, width = q.shape
    rows = total // WAYS
    heads = width // HD
    limit = threshold(sc, sc[2] ^ step)
    ahead = lax.broadcasted_iota(jnp.int32, (rows, rows), 1) - lax.broadcasted_iota(
        jnp.int32, (rows, rows), 0
    )
    allowed = ahead <= limit
    for jq in range(WAYS):
        place = slice(jq * rows, (jq + 1) * rows)
        parts, tops, sums = [], [], []
        for h in range(heads):
            cols = slice(h * HD, (h + 1) * HD)
            vcols = slice(width + h * HD, width + (h + 1) * HD)
            qh = q[place, cols]
            keys = slice(0, (jq + 1) * rows)
            scores = dot(qh, kv[keys, cols], (1, 1))
            scores = mask_last(scores, allowed, NEGATIVE)
            top = jnp.max(scores, axis=-1, keepdims=True)
            if not first:
                old = stat_in[place, h : h + 1]
                top = jnp.maximum(top, old)
            weight = jnp.exp(scores - top)
            count = jnp.sum(weight, axis=-1, keepdims=True)
            acc = dot(weight.astype(BF16), kv[keys, vcols], (1, 0))
            if not first:
                shrink = jnp.exp(old - top)
                count = count + shrink * stat_in[place, heads + h : heads + h + 1]
                acc = acc + shrink * acc_in[place, cols]
            if last:
                acc = acc / count
                tops.append(top + jnp.log(count))
            else:
                tops.append(top)
                sums.append(count)
            parts.append(acc)
        joined_parts = jnp.concatenate(parts, axis=1)
        if last:
            attended[place, :] = joined_parts
            low_part = joined_parts.astype(BF16)
            low[place, :] = low_part
            scratch[place, :] = dot(low_part, out_w[...], (1, 0))
            split = [split3(t) for t in tops]
            columns = [split[h][part] for part in range(3) for h in range(heads)]
            q_ext[place, :width] = q[place, :]
            q_ext[place, width:] = lanes(columns, rows, q_ext.shape[1] - width, BF16)
        else:
            acc_out[place, :] = joined_parts
            stat_out[place, :] = lanes(tops + sums, rows, stat_out.shape[1], F32)
    if last:
        emit_partials(sc, rows, scratch, own, far, sent, sent_own)


def second_norm_kernel(sc, own, got, far, x, table, residual, normed):
    value = (
        x[...].astype(F32)
        + own[...]
        + got[...].astype(F32)
        + far[...].astype(F32)
        + table[2:3, :]
    )
    residual[...] = value
    scaled, _ = normalise(value)
    normed[...] = (scaled * table[3:4, :] + table[4:5, :]).astype(BF16)


def assemble_kernel(sc, w0, w1, w2, w3, full):
    for k, ref in enumerate((w0, w1, w2, w3)):
        full[block_rows(sc[0] ^ k, ref.shape[0]), :] = ref[...]


def feed_kernel(
    sc, n0, n1, n2, n3, full, bias, pulled,
    normed, active, g_hidden, bias_row, own, far, sent, sent_own, scratch,
):
    rows = n0.shape[0]
    total = jnp.zeros_like(bias_row)
    for k, ref in enumerate((n0, n1, n2, n3)):
        place = member_rows(sc[0] ^ k, rows)
        normed[place, :] = ref[...]
        hidden = dot(ref[...], full[...], (1, 0)) + bias[...]
        square = hidden * hidden
        bend = jnp.tanh(GELU_COEF * (hidden + CUBE * hidden * square))
        active[place, :] = (0.5 * hidden * (1.0 + bend)).astype(BF16)
        slope = 0.5 * (1.0 + bend) + 0.5 * hidden * (1.0 - bend * bend) * (
            GELU_COEF * (1.0 + 3.0 * CUBE * square)
        )
        low = (pulled[place, :] * slope).astype(BF16)
        g_hidden[place, :] = low
        total = total + jnp.sum(low.astype(F32), axis=0, keepdims=True)
        scratch[place, :] = dot(low, full[...], (1, 1))
    bias_row[...] = total
    emit_partials(sc, rows, scratch, own, far, sent, sent_own)


def result_kernel(sc, active, proj, own, far, sent, sent_own, scratch):
    rows = active.shape[0] // WAYS
    scratch[...] = dot(active[...], proj[...], (1, 0))
    emit_partials(sc, rows, scratch, own, far, sent, sent_own)


def piece_of(sc, bits, slot):
    r = 0
    for i, bit in enumerate(bits):
        r |= ((slot >> (2 - i)) & 1) << bit
    return (sc[1] ^ r) & 7


def place_halves(keep, send):
    half = keep.shape[0]
    return [(slot, keep if slot < half else send, slot % half) for slot in range(2 * half)]


def tile_grad_kernel(bits, sc, active, g_out, keep, send, scratch):
    step_rows, step_cols = keep.shape[1], keep.shape[2]
    scratch[...] = dot(active[...], g_out[...], (0, 0)).astype(BF16)
    for slot, ref, at in place_halves(keep, send):
        piece = piece_of(sc, bits, slot)
        ref[at] = scratch[block_rows(piece >> 1, step_rows), block_rows(piece & 1, step_cols)]


def fc_grad_kernel(bits, sc, normed, g_hidden, keep, send, scratch):
    step_rows, step_cols = keep.shape[1], keep.shape[2]
    quarter = step_rows // WAYS
    scratch[...] = dot(normed[...], g_hidden[...], (0, 0)).astype(BF16)
    for slot, ref, at in place_halves(keep, send):
        piece = piece_of(sc, bits, slot)
        for k in range(WAYS):
            start = (sc[0] ^ k) * WAYS + (piece >> 1)
            ref[at, k * quarter : (k + 1) * quarter, :] = scratch[
                block_rows(start, quarter), block_rows(piece & 1, step_cols)
            ]


def second_back_kernel(sc, own, got, far, residual, cot, table, g_residual, g_branch, rows_out):
    upstream = own[...] + got[...].astype(F32) + far[...].astype(F32)
    scaled, inverse = normalise(residual[...])
    through = norm_back(upstream, scaled, inverse, table[3:4, :])
    g_out = jnp.where(valid_rows(sc, table, sc[0], cot.shape[0]), cot[...].astype(F32), 0.0)
    value = g_out + through
    g_residual[...] = value
    low = value.astype(BF16)
    g_branch[...] = low
    rows_out[0:1, :] = jnp.sum(upstream * scaled, axis=0, keepdims=True)
    rows_out[1:2, :] = jnp.sum(upstream, axis=0, keepdims=True)
    rows_out[2:3, :] = jnp.sum(low.astype(F32), axis=0, keepdims=True)


def pull_kernel(sc, b0, b1, b2, b3, out_w, attended, g_branch, do_ext):
    rows = b0.shape[0]
    width = attended.shape[1]
    heads = width // HD
    for k, ref in enumerate((b0, b1, b2, b3)):
        place = member_rows(sc[0] ^ k, rows)
        g_branch[place, :] = ref[...]
        low = dot(ref[...], out_w[...], (1, 1)).astype(BF16)
        product = low.astype(F32) * attended[place, :]
        split = [
            split3(jnp.sum(product[:, h * HD : (h + 1) * HD], axis=-1, keepdims=True))
            for h in range(heads)
        ]
        columns = [split[h][part] for part in range(3) for h in range(heads)]
        do_ext[place, :width] = low
        do_ext[place, width:] = lanes(columns, rows, do_ext.shape[1] - width, BF16)


def pair_back(q, do, kv, allowed, g_q=None, g_kv=None, q_in=None):
    total = kv.shape[0]
    width = kv.shape[1] // 2
    rows = total // WAYS
    heads = width // HD
    for jq in range(WAYS):
        place = slice(jq * rows, (jq + 1) * rows)
        tail_q = q[place, width:].astype(F32)
        tail_do = do[place, width:].astype(F32)
        for h in range(heads):
            cols = slice(h * HD, (h + 1) * HD)
            vcols = slice(width + h * HD, width + (h + 1) * HD)
            qh = q[place, cols]
            doh = do[place, cols]
            pick = lambda t: (
                t[:, h : h + 1] + t[:, heads + h : heads + h + 1]
            ) + t[:, 2 * heads + h : 2 * heads + h + 1]
            lse, delta = pick(tail_q), pick(tail_do)
            keys = slice(0, (jq + 1) * rows)
            weight = jnp.exp(dot(qh, kv[keys, cols], (1, 1)) - lse)
            weight = mask_last(weight, allowed, 0.0)
            pulled = dot(doh, kv[keys, vcols], (1, 1))
            low = (weight * (pulled - delta)).astype(BF16)
            if g_q is not None:
                grad = dot(low, kv[keys, cols], (1, 0))
                if q_in is not None:
                    grad = grad + q_in[place, cols]
            if g_kv is not None:
                g_kv[keys, cols] += dot(low, qh, (0, 0))
                g_kv[keys, vcols] += dot(weight.astype(BF16), doh, (0, 0))
            if g_q is not None:
                g_q[place, cols] = grad


def ahead_of(rows):
    return lax.broadcasted_iota(jnp.int32, (rows, rows), 1) - lax.broadcasted_iota(
        jnp.int32, (rows, rows), 0
    )


def back_first(sc, q, do, kv, g_q, g_kv):
    g_kv[...] = jnp.zeros_like(g_kv)
    pair_back(q, do, kv, ahead_of(kv.shape[0] // WAYS) <= 0, g_q, g_kv)


def back_queries(sc, step, q, do, kv_other, q_in, g_q):
    limit = jnp.where((sc[2] ^ step) < sc[2], 1, -1)
    rows = kv_other.shape[0] // WAYS
    pair_back(q, do, kv_other, jnp.zeros((rows, rows), jnp.int32) <= limit, g_q=g_q, q_in=q_in)


def back_keys(sc, step, last, refs):
    q_other, do_other, kv, kv_in = refs[:4]
    if last:
        q_in, full, scales, g_proj, own, far, sent, sent_own, sums, g_kv, scratch = refs[4:]
    else:
        (g_kv,) = refs[4:]
    width = kv.shape[1] // 2
    rows = kv.shape[0] // WAYS
    limit = jnp.where(sc[2] < (sc[2] ^ step), 1, -1)
    g_kv[...] = kv_in[...]
    pair_back(q_other, do_other, kv, jnp.zeros((rows, rows), jnp.int32) <= limit, g_kv=g_kv)
    if last:
        g_proj[:, :width] = (q_in[...] * 0.125).astype(BF16)
        g_proj[:, width:] = g_kv[...].astype(BF16)
        scratch[...] = dot(g_proj[...], full[...], (1, 1))
        emit_partials(sc, rows, scratch, own, far, sent, sent_own)
        sums[0:1, :] = jnp.sum(scratch[...] * scales[...].astype(F32), axis=0, keepdims=True)
        sums[1:2, :] = jnp.sum(scratch[...], axis=0, keepdims=True)


def out_grad_kernel(bits, sc, attended, g_branch, slots, scratch):
    scratch[...] = dot(attended[...], g_branch[...], (0, 0)).astype(BF16)
    rows, cols = scratch.shape[0] // WAYS, scratch.shape[1] // 2
    tall, rest = 2 * rows // 3, rows // 3
    for slot in range(PIECES):
        piece = piece_of(sc, bits, slot)
        block = scratch[block_rows(piece >> 1, rows), block_rows(piece & 1, cols)]
        slots[slot, :, :cols] = block[:tall]
        slots[slot, :rest, cols:] = block[tall:, : cols // 2]
        slots[slot, rest:, cols:] = block[tall:, cols // 2 :]


def qkv_grad_kernel(
    near_bits, far_bits, sc, normed, g_proj, out, two, proj, fc, one, nk, ns, vec, wk, ws, scratch, rows_out
):
    half = PIECES // 2
    step = scratch.shape[0] // WAYS // PIECES
    width = nk.shape[1] // 3
    scratch[...] = dot(normed[...], g_proj[...], (0, 0))
    for base, bits, keep, send in ((2, far_bits, wk, ws), (0, near_bits, nk, ns)):
        size = keep.shape[0] // half
        for slot in range(PIECES):
            ref, at = (keep, slot) if slot < half else (send, slot - half)
            piece = piece_of(sc, bits, slot)
            for i in range(2):
                start = (sc[0] ^ (base + i)) * PIECES + piece
                ref[at * size + i * step : at * size + (i + 1) * step, :] = scratch[
                    block_rows(start, step), :
                ].astype(BF16)
            if base == 2:
                ref[at * size + 2 * step : (at + 1) * size, :] = out[slot]
    rows_out[0:2, :] = one[...]
    rows_out[2:3, :] = two[2:3, :]
    rows_out[3:5, :] = two[0:2, :]
    rows_out[5:6, :] = proj[...]
    rows_out[6:8, :] = jnp.zeros_like(rows_out[6:8, :])
    rows_out[8:12, :] = jnp.zeros_like(rows_out[8:12, :])
    total = jnp.sum(g_proj[...].astype(F32), axis=0, keepdims=True)
    for block in range(WAYS):

        @pl.when(sc[0] == block)
        def _(block=block):
            place = slice(block * width, (block + 1) * width)
            rows_out[6:7, place] = total[:, :width]
            rows_out[7:8, place] = total[:, 2 * width :]
            rows_out[8 + block : 9 + block, :] = fc[...]

    for row in range(VECTOR_ROWS):
        for block in range(WAYS):
            vec[vector_place(row, block, width)] = rows_out[
                row : row + 1, block * width : (block + 1) * width
            ].astype(BF16)
    ns[nk.shape[0] :, :] = vec[...]


def first_back_kernel(sc, own, got, far, x, table, g_residual, input_grad):
    upstream = own[...] + got[...].astype(F32) + far[...].astype(F32)
    scaled, inverse = normalise(x[...].astype(F32))
    through = norm_back(upstream, scaled, inverse, table[0:1, :])
    input_grad[0] = (g_residual[...] + through).astype(BF16)


def output_kernel(sc, own, got, far, residual, table, out):
    value = (
        residual[...] + own[...] + got[...].astype(F32) + far[...].astype(F32) + table[5:6, :]
    )
    out[0] = jnp.where(valid_rows(sc, table, sc[0], out.shape[1]), value, 0.0).astype(BF16)


def slots_in(near, far):
    half = near.shape[0]
    return [(slot, near if slot < half else far, slot % half) for slot in range(2 * half)]


def proj_final_kernel(bits, sc, near, far, out):
    rows, cols = near.shape[1:]
    for slot, ref, at in slots_in(near, far):
        piece = piece_of(sc, bits, slot)
        out[block_rows(piece >> 1, rows), block_rows(piece & 1, cols)] = ref[at].astype(F32)


def fc_final_kernel(bits, sc, near, far, out):
    quarter, step_cols = near.shape[1] // WAYS, near.shape[2]
    for slot, ref, at in slots_in(near, far):
        piece = piece_of(sc, bits, slot)
        for k in range(WAYS):
            wide = block_rows((sc[0] ^ k) * 2 + (piece & 1), step_cols)
            out[block_rows(piece >> 1, quarter), wide] = ref[
                at, k * quarter : (k + 1) * quarter
            ].astype(F32)


def qkv_final_kernel(near_bits, far_bits, sc, nn, nf, wn, wf, out, out_out):
    step, width = nn.shape[1] // 2, nn.shape[2] // 3
    cols = out_out.shape[1] // 2
    rows = out_out.shape[0] // WAYS
    tall, rest = 2 * rows // 3, rows // 3
    for slot, ref, at in slots_in(wn, wf):
        piece = piece_of(sc, far_bits, slot)
        block = ref[at, 2 * step :].astype(F32)
        start = (piece >> 1) * rows
        left = pl.ds(pl.multiple_of((piece & 1) * cols, cols), cols)
        low = pl.ds(pl.multiple_of(start, 8), tall)
        out_out[low, left] = block[:, :cols]
        high = pl.ds(pl.multiple_of(start + tall, 8), rest)
        out_out[high, left] = jnp.concatenate([block[:rest, cols:], block[rest:, cols:]], axis=1)
    for member in range(WAYS):

        @pl.when(sc[0] == member)
        def _(member=member):
            for base, bits, near, far in ((0, near_bits, nn, nf), (2, far_bits, wn, wf)):
                for slot, ref, at in slots_in(near, far):
                    place = block_rows(piece_of(sc, bits, slot), step)
                    for i in range(2):
                        piece = ref[at, i * step : (i + 1) * step].astype(F32)
                        for part in range(3):
                            start = (part * WAYS + (member ^ (base + i))) * width
                            out[place, start : start + width] = piece[
                                :, part * width : (part + 1) * width
                            ]


def body(
    inputs, lengths, ln1_gain, ln1_bias, qkv_weight, qv_bias, out_weight, out_bias,
    ln2_gain, ln2_bias, fc_weight, fc_bias, proj_weight, proj_bias, cotangent,
):
    group = lax.axis_size("ctx")
    members = group // WAYS
    assert lax.axis_size("fsdp") == WAYS and inputs.shape[0] == 1
    assert group % PIECES == 0 and group & (group - 1) == 0
    f, c = lax.axis_index("fsdp"), lax.axis_index("ctx")
    rows, width = inputs.shape[1:]
    head_width = width // WAYS
    hidden_width = fc_bias.shape[0]
    total = rows * WAYS
    half = PIECES // 2
    scalars = jnp.stack(
        [f, c, c % members, jnp.asarray(members), lengths[0], turned(c // members)]
    ).astype(jnp.int32)
    order = Order(scalars)

    vectors = [ln1_gain, ln1_bias, out_bias, ln2_gain, ln2_bias, proj_bias, qv_bias, fc_bias]
    w_qkv = order.call(
        qkv_columns_kernel,
        [shape((head_width // (1 + i // 2), 3 * head_width), BF16) for i in range(WAYS)],
        [qkv_weight],
        name="qkv_columns",
    )
    small, fc_row = order.call(
        small_kernel,
        [shape((16, head_width), BF16), shape((1, hidden_width), F32)],
        [jnp.concatenate(vectors)],
        name="small",
    )
    small_all = [small, f_xor(small, 1), f_xor(small, 2), f_xor(small, 3)]
    x_own = swap_layout(inputs[0])
    w_qkv = fetched(*w_qkv)
    x_far = f_xor(after(x_own, w_qkv[2], w_qkv[4], small), 2)
    x_all = [x_own, f_xor(x_own, 1), x_far, f_xor(x_far, 1)]
    cot_own = swap_layout(after(cotangent[0], x_far))
    table, qkv_bias = order.call(
        table_kernel,
        [shape((8, width), F32), shape((1, 3 * head_width), F32)],
        small_all,
        flops=4 * 10**9,
        name="table",
        late=[x_own, w_qkv[3], w_qkv[5]],
    )
    w_fc = order.call(
        fc_columns_kernel,
        [shape((head_width, hidden_width), BF16)] * WAYS,
        [fc_weight],
        name="fc_columns",
    )
    w_fc = [w_fc[0]] + [f_xor(w_fc[k], k) for k in range(1, WAYS)]

    normed_one, scales_one, qkv_full, q, kv = order.call(
        qkv_kernel,
        [
            shape((total, width), BF16),
            shape((total, width), BF16),
            shape((width, 3 * head_width), BF16),
            shape((total, head_width), BF16),
            shape((total, 2 * head_width), BF16),
        ],
        [*x_all, *w_qkv, table, qkv_bias],
        flops=2 * total * width * 3 * head_width,
        name="qkv",
    )
    kv_other = [kv] + [c_xor(kv, r) for r in range(1, members)]

    partials = [shape((rows, width), F32)] * 2 + [shape((rows, width), BF16)] * 2
    state = []
    for r in range(members):
        first, last = r == 0, r == members - 1
        if r == 1:
            cot_all = gather_f(after(cot_own, state[1]))
        if last:
            outs = [
                shape((total, head_width), F32),
                shape((total, head_width), BF16),
                shape((total, head_width + 64), BF16),
                *partials,
            ]
            scratch = [pltpu.VMEM((total, width), F32)]
            extra = [out_weight]
        else:
            outs = [shape((total, head_width), F32), shape((total, 128), F32)]
            scratch, extra = [], []

        def kernel(sc_ref, *refs, r=r, first=first, last=last):
            attend(sc_ref, r, first, last, refs)

        state = order.call(
            kernel,
            outs,
            [q, kv_other[r], *state, *extra],
            scratch,
            flops=4 * total * total * head_width,
            name=f"attend{min(r, 1)}",
        )
    attended, attended_low, q_ext, *branch = state
    branch = order.scatter_f(*branch)
    q_other = [q_ext] + [c_xor(q_ext, r) for r in range(1, members)]
    (fc_full,) = order.call(
        assemble_kernel,
        [shape((width, hidden_width), BF16)],
        w_fc,
        name="fc_assemble",
    )
    branch = order.scatter_f_far(branch)
    residual, normed_two = order.call(
        second_norm_kernel,
        [shape((rows, width), F32), shape((rows, width), BF16)],
        [*branch, x_own, table],
        name="norm2",
        late=[cot_all[2]],
    )
    normed_two_all = gather_f(normed_two)
    g_out, pulled, proj_row = order.call(
        cot_kernel,
        [
            shape((total, width), BF16),
            shape((total, hidden_width), F32),
            shape((1, width), F32),
        ],
        [*cot_all, proj_weight, table],
        flops=2 * total * width * hidden_width,
        name="cot",
    )
    normed_two_full, active, g_hidden, fc_rows, *g_two = order.call(
        feed_kernel,
        [
            shape((total, width), BF16),
            shape((total, hidden_width), BF16),
            shape((total, hidden_width), BF16),
            shape((1, hidden_width), F32),
            *partials,
        ],
        [*normed_two_all, fc_full, fc_row, pulled],
        [pltpu.VMEM((total, width), F32)],
        flops=4 * total * width * hidden_width,
        name="feed",
        late=q_other[1:],
    )
    g_two = order.scatter_f(*g_two)
    slots = [shape((half, head_width, width // 2), BF16)] * 2
    proj_keep, send = order.call(
        functools.partial(tile_grad_kernel, OTHER),
        slots,
        [active, g_out],
        [pltpu.VMEM((width, width), BF16)],
        flops=2 * total * width * hidden_width,
        name="proj_grad",
    )
    proj_got = c_xor(send, 1 << OTHER[0])
    g_two = order.scatter_f_far(g_two)
    fc_keep, send = order.call(
        functools.partial(fc_grad_kernel, ONE),
        slots,
        [normed_two_full, g_hidden],
        [pltpu.VMEM((width, width), BF16)],
        flops=2 * total * width * hidden_width,
        name="fc_grad",
    )
    fc_got = c_xor(send, 1 << ONE[0])
    result = order.call(
        result_kernel,
        partials,
        [active, proj_weight],
        [pltpu.VMEM((total, width), F32)],
        flops=2 * total * width * hidden_width,
        name="result",
    )
    result = order.scatter_f(*result)
    g_residual, g_branch, two_rows = order.call(
        second_back_kernel,
        [shape((rows, width), F32), shape((rows, width), BF16), shape((3, width), F32)],
        [*g_two, residual, cot_own, table],
        name="norm2_back",
    )
    g_branch_all = gather_f(g_branch)
    result = order.scatter_f_far(result)
    g_branch_full, do_ext = order.call(
        pull_kernel,
        [shape((total, width), BF16), shape((total, head_width + 64), BF16)],
        [*g_branch_all, out_weight, attended],
        flops=2 * total * width * head_width,
        name="pull",
    )
    do_other = [do_ext] + [c_xor(do_ext, r) for r in range(1, members)]
    step = head_width // PIECES
    out_rows = head_width // 6
    (out_slots,) = order.call(
        functools.partial(out_grad_kernel, ONE),
        [shape((PIECES, out_rows, 3 * head_width), BF16)],
        [attended_low, g_branch_full],
        [pltpu.VMEM((head_width, width), BF16)],
        flops=2 * total * width * head_width,
        name="out_grad",
    )
    tile = (head_width, width // 2)
    proj_keep, proj_send, fc_keep, fc_send = order.call(
        mlp_fold_kernel,
        [shape((2, *tile), BF16)] * 4,
        [proj_keep, proj_got, fc_keep, fc_got],
        name="mlp_fold",
    )
    proj_got, fc_got = c_xor(proj_send, 1 << OTHER[1]), c_xor(fc_send, 1 << ONE[1])
    (outputs,) = order.call(
        output_kernel, [shape((1, rows, width), BF16)], [*result, residual, table], name="output"
    )
    outputs = swap_layout(outputs)
    g_q, g_kv = order.call(
        back_first,
        [shape((total, head_width), F32), shape((total, 2 * head_width), F32)],
        [q_ext, do_ext, kv],
        flops=10 * total * total * head_width,
        name="back0",
    )
    mlp_keep, mlp_send = order.call(
        mlp_meet_kernel,
        [shape((2, *tile), BF16)] * 2,
        [proj_keep, proj_got, fc_keep, fc_got],
        name="mlp_meet",
        late=[outputs],
    )
    mlp_got = c_xor(mlp_send, 1 << Z2)
    for r in range(1, members):

        def kernel(sc_ref, *refs, r=r):
            back_queries(sc_ref, r, *refs)

        (g_q,) = order.call(
            kernel,
            [shape(g_q.shape, F32)],
            [q_ext, do_ext, kv_other[r], g_q],
            flops=6 * total * total * head_width,
            name="back_q",
        )
    for r in range(1, members):
        last = r == members - 1
        outs, scratch, extra = [shape(g_kv.shape, F32)], [], []
        if last:
            scratch = [pltpu.VMEM(g_kv.shape, F32), pltpu.VMEM((total, width), F32)]
            outs = [shape((total, 3 * head_width), BF16), *partials, shape((2, width), F32)]
            extra = [g_q, qkv_full, scales_one]

        def kernel(sc_ref, *refs, r=r, last=last):
            back_keys(sc_ref, r, last, refs)

        grads = order.call(
            kernel,
            outs,
            [q_other[r], do_other[r], kv, g_kv, *extra],
            scratch,
            flops=8 * total * total * head_width,
            name="back_kv",
        )
        g_kv = grads[0]
    g_proj, *g_one, one_rows = grads
    g_one = order.scatter_f(*g_one)
    near_rows, far_rows, vec_rows, cols = 2 * step, 2 * step + out_rows, 16, 3 * head_width
    near_keep, near_send, vec, far_keep, far_send = order.call(
        functools.partial(qkv_grad_kernel, OTHER, ONE),
        [
            shape((half * near_rows, cols), BF16),
            shape((half * near_rows + vec_rows, cols), BF16),
            shape((vec_rows, cols), BF16),
            shape((half * far_rows, cols), BF16),
            shape((half * far_rows, cols), BF16),
        ],
        [normed_one, g_proj, out_slots, two_rows, proj_row, fc_rows, one_rows],
        [pltpu.VMEM((width, cols), F32), pltpu.VMEM((VECTOR_ROWS, width), F32)],
        flops=2 * total * width * cols,
        name="qkv_grad",
    )
    near_got, far_got = c_xor(near_send, 1 << OTHER[0]), c_xor(far_send, 1 << ONE[0])
    quarter = head_width // WAYS
    pieces = order.call(
        mlp_last_kernel,
        [shape(tile, BF16)] + [shape((quarter, tile[1]), BF16)] * WAYS,
        [mlp_keep, mlp_got],
        name="mlp_last",
    )
    proj_piece, *fc_pieces = [others(piece) for piece in pieces]
    proj_got = c_xor(proj_piece, 1 << Z2)
    fc_pieces = [fc_pieces[0]] + [f_xor(fc_pieces[k], k) for k in range(1, WAYS)]
    g_one = order.scatter_f_far(g_one)
    (fc_piece,) = order.call(
        mlp_join_kernel, [shape(tile, BF16)], fc_pieces, name="mlp_join"
    )
    fc_got = c_xor(fc_piece, 1 << Z2)
    near_keep, vec, near_send, far_keep, far_send = order.call(
        qkv_fold_kernel,
        [
            shape((2 * near_rows, cols), BF16),
            shape((vec_rows, cols), BF16),
            shape((2 * near_rows + vec_rows, cols), BF16),
            shape((2 * far_rows, cols), BF16),
            shape((2 * far_rows, cols), BF16),
        ],
        [near_keep, vec, near_got, far_keep, far_got],
        name="qkv_fold",
        late=[proj_got],
    )
    near_got, far_got = c_xor(near_send, 1 << OTHER[1]), c_xor(far_send, 1 << ONE[1])
    (input_grad,) = order.call(
        first_back_kernel,
        [shape((1, rows, width), BF16)],
        [*g_one, x_own, table, g_residual],
        name="norm1_back",
    )
    input_grad = swap_layout(input_grad)
    keep, vec, send = order.call(
        qkv_meet_kernel,
        [
            shape((near_rows + far_rows, cols), BF16),
            shape((vec_rows, cols), BF16),
            shape((near_rows + far_rows + vec_rows, cols), BF16),
        ],
        [near_keep, vec, near_got, far_keep, far_got],
        name="qkv_meet",
    )
    got = c_xor(send, 1 << Z2)
    proj_own, fc_own = order.call(
        mlp_part_kernel,
        [shape((2, *tile), BF16)] * 2,
        [proj_piece, proj_got, fc_piece, fc_got],
        name="mlp_part",
    )
    proj_got, fc_got = c_xor(proj_own, 1 << OTHER[1]), c_xor(fc_own, 1 << ONE[1])
    proj_own, fc_own = order.call(
        grow_kernel,
        [shape((half, *tile), BF16)] * 2,
        [proj_own, proj_got, fc_own, fc_got],
        name="mlp_grow",
        late=[got],
    )
    proj_got, fc_got = c_xor(proj_own, 1 << OTHER[0]), c_xor(fc_own, 1 << ONE[0])
    piece, vec = order.call(
        qkv_last_kernel,
        [shape((near_rows + far_rows, cols), BF16), shape((vec_rows, cols), BF16)],
        [keep, vec, got],
        name="qkv_last",
    )
    piece, vec = others(piece), others(vec)
    s1, s2, s3 = order.call(
        exchange_kernel, [shape((step + vec_rows, cols), BF16)] * 3, [piece, vec], name="exchange"
    )
    r2, r3, r1 = f_xor(s2, 2), f_xor(s3, 3), f_xor(s1, 1)
    joined, *mine, grad_qv, grad_fc_bias = order.call(
        join_kernel,
        [
            shape((near_rows + far_rows, cols), BF16),
            *[shape((head_width,), F32)] * 6,
            shape((2 * head_width,), F32),
            shape((hidden_width,), F32),
        ],
        [piece, vec, r1, r2, r3],
        [pltpu.VMEM((vec_rows, cols), F32)],
        name="join",
    )
    got = c_xor(joined, 1 << Z2)
    near_own, far_own = order.call(
        qkv_part_kernel,
        [shape((2, near_rows, cols), BF16), shape((2, far_rows, cols), BF16)],
        [joined, got],
        name="qkv_part",
    )
    near_got, far_got = c_xor(near_own, 1 << OTHER[1]), c_xor(far_own, 1 << ONE[1])
    def finish(kernel, dims, arrays, name):
        late = [input_grad] if name == "qkv_final" else []
        return order.call(
            kernel, [shape(d, F32) for d in dims], arrays, name=name, direct=True, late=late
        )

    (grad_fc,) = finish(
        functools.partial(fc_final_kernel, ONE),
        [(head_width, WAYS * hidden_width)],
        [fc_own, fc_got],
        "fc_final",
    )
    (grad_proj,) = finish(
        functools.partial(proj_final_kernel, OTHER),
        [(hidden_width, width)],
        [proj_own, proj_got],
        "proj_final",
    )
    near_own, far_own = order.call(
        grow_kernel,
        [shape((half, near_rows, cols), BF16), shape((half, far_rows, cols), BF16)],
        [near_own, near_got, far_own, far_got],
        name="qkv_grow",
    )
    near_got, far_got = c_xor(near_own, 1 << OTHER[0]), c_xor(far_own, 1 << ONE[0])

    grad_qkv, grad_out = finish(
        functools.partial(qkv_final_kernel, OTHER, ONE),
        [(head_width, 3 * width), (head_width, width)],
        [near_own, near_got, far_own, far_got],
        "qkv_final",
    )
    return (
        outputs,
        input_grad,
        mine[0],
        mine[1],
        grad_qkv,
        grad_qv,
        grad_out,
        mine[2],
        mine[3],
        mine[4],
        grad_fc,
        grad_fc_bias,
        grad_proj,
        mine[5],
    )


def solution(mesh):
    tokens, rows, vector = P("fsdp", "ctx", None), P("fsdp", None), P("fsdp")
    in_specs = (
        tokens, vector, vector, vector, rows, vector, rows, vector,
        vector, vector, rows, vector, rows, vector, tokens,
    )
    out_specs = (
        tokens, tokens, vector, vector, rows, vector, rows, vector,
        vector, vector, rows, vector, rows, vector,
    )
    return jax.shard_map(body, mesh=mesh, in_specs=in_specs, out_specs=out_specs, check_vma=False)
```

```python
import functools

import jax
import jax.numpy as jnp
from jax import lax
from jax.experimental import pallas as pl
from jax.experimental.pallas import tpu as pltpu
from jax.sharding import PartitionSpec as P

HD = 64
EPSILON = 1e-05
NEGATIVE = -1e30
GELU_COEF = 0.7978845608028654
CUBE = 0.044715
F32 = jnp.float32
BF16 = jnp.bfloat16
WAYS = 4
PIECES = 8
VMEM_LIMIT = 24 * 1024 * 1024


def f_xor(x, k):
    n = lax.axis_size("fsdp")
    return lax.ppermute(x, "fsdp", [(i, i ^ k) for i in range(n)])


def c_xor(x, k):
    n = lax.axis_size("ctx")
    return lax.ppermute(x, "ctx", [(i, i ^ k) for i in range(n)])


def turned(index):
    return ((index & 1) << 1) | (index >> 1)


def swap_layout(x):
    group = lax.axis_size("ctx")
    members = group // WAYS
    perm = []
    for f in range(WAYS):
        for c in range(group):
            j, m = divmod(c, members)
            perm.append((f * group + c, turned(j) * group + turned(f) * members + m))
    return lax.ppermute(x, ("fsdp", "ctx"), perm)


def after(value, *others):
    return lax.optimization_barrier((value, *others))[0]


def gather_f(x, until=lambda far: far):
    far = f_xor(x, 2)
    near = f_xor(x, 1)
    return [x, near, far, f_xor(until(far), 1)]


class Order:
    def __init__(self, scalars):
        self.scalars = scalars
        self.token = None

    def tie(self, value):
        if self.token is None:
            return value
        return lax.optimization_barrier((value, self.token))[0]

    def mark(self, value):
        self.token = value
        return value

    def call(self, kernel, outs, args, scratch=(), flops=0, name=None, direct=False, late=()):
        scalars = after(self.tie(self.scalars), *late)
        got = call(kernel, outs, [scalars, *args], scratch, flops, name, direct)
        self.mark(min(got, key=lambda value: value.size))
        return got

    def scatter_f(self, kept_own, kept_far, sent_far, sent_own):
        return kept_own, kept_far, f_xor(sent_far, 1), f_xor(sent_own, 1)

    def scatter_f_far(self, state, late=()):
        kept_own, kept_far, got_far, got_own = state
        (far,) = self.call(
            far_kernel, [shape(kept_own.shape, BF16)], [kept_far, got_far], name="far", late=late
        )
        return kept_own, got_own, f_xor(far, 2)


X, Z1, Z2 = 0, 1, 2
ONE, OTHER = (X, Z1, Z2), (Z1, X, Z2)


def others(value):
    bit = 3
    while (1 << bit) < lax.axis_size("ctx"):
        value = (value.astype(F32) + c_xor(value, 1 << bit).astype(F32)).astype(BF16)
        bit += 1
    return value


def call(kernel, outs, args, scratch=(), flops=0, name=None, direct=False):
    vmem = pl.BlockSpec(memory_space=pltpu.VMEM)
    moved = sum(a.size * a.dtype.itemsize for a in args) + sum(
        o.size * o.dtype.itemsize for o in outs
    )
    return pl.pallas_call(
        kernel,
        out_shape=tuple(outs),
        in_specs=[pl.BlockSpec(memory_space=pltpu.SMEM)] + [vmem] * (len(args) - 1),
        out_specs=tuple([pl.BlockSpec() if direct else vmem] * len(outs)),
        scratch_shapes=list(scratch),
        cost_estimate=pl.CostEstimate(flops=flops, bytes_accessed=moved, transcendentals=0),
        compiler_params=pltpu.CompilerParams(vmem_limit_bytes=VMEM_LIMIT),
        name=name,
    )(*args)


def shape(dims, dtype):
    return jax.ShapeDtypeStruct(dims, dtype)


def dot(a, b, contract):
    return lax.dot_general(a, b, ((contract[0:1], contract[1:2]), ((), ())), preferred_element_type=F32)


def block_rows(index, size):
    return pl.ds(pl.multiple_of(index * size, size), size)


def member_rows(member, size):
    return block_rows(turned(member), size)


def normalise(values):
    centred = values - jnp.mean(values, axis=-1, keepdims=True)
    inverse = lax.rsqrt(jnp.mean(centred * centred, axis=-1, keepdims=True) + EPSILON)
    return centred * inverse, inverse


def norm_back(upstream, scaled, inverse, gain):
    weighted = upstream * gain
    return inverse * (
        weighted
        - jnp.mean(weighted, axis=-1, keepdims=True)
        - scaled * jnp.mean(weighted * scaled, axis=-1, keepdims=True)
    )


def valid_rows(sc, table, chunk, rows):
    place = (turned(chunk) * sc[3] + sc[2]) * rows + lax.broadcasted_iota(jnp.int32, (rows, 1), 0)
    return place.astype(F32) < table[6:7, 0:1]


def emit_partials(sc, rows, value_ref, own_ref, far_ref, sent_far, sent_own):
    f = sc[0]
    own_ref[...] = value_ref[member_rows(f, rows), :]
    far_ref[...] = value_ref[member_rows(f ^ 2, rows), :]
    sent_own[...] = value_ref[member_rows(f ^ 1, rows), :].astype(BF16)
    sent_far[...] = value_ref[member_rows(f ^ 3, rows), :].astype(BF16)


def far_kernel(sc, kept, got, out):
    out[...] = (kept[...] + got[...].astype(F32)).astype(BF16)


def added(a, b):
    return (a.astype(F32) + b.astype(F32)).astype(BF16)


def fold_into(keep, got, kept, sent):
    half = keep.shape[0] // 2
    sent[:half] = added(keep[half:], got[half : 2 * half])
    kept[...] = added(keep[:half], got[:half])


def mlp_fold_kernel(sc, proj, proj_got, fc, fc_got, proj_kept, proj_sent, fc_kept, fc_sent):
    fold_into(proj, proj_got, proj_kept, proj_sent)
    fold_into(fc, fc_got, fc_kept, fc_sent)


def mlp_meet_kernel(sc, proj, proj_got, fc, fc_got, kept, sent):
    for i, (keep, got) in enumerate(((proj, proj_got), (fc, fc_got))):
        kept[i] = added(keep[0], got[0])
        sent[i] = added(keep[1], got[1])


def mlp_last_kernel(sc, keep, got, proj, *pieces):
    proj[...] = added(keep[0], got[0])
    rows = pieces[0].shape[0]
    for i, piece in enumerate(pieces):
        place = slice(i * rows, (i + 1) * rows)
        piece[...] = added(keep[1, place], got[1, place])


def mlp_join_kernel(sc, p0, p1, p2, p3, out):
    rows = p0.shape[0]
    for i, piece in enumerate((p0, p1, p2, p3)):
        out[i * rows : (i + 1) * rows] = piece[...]


def mlp_part_kernel(sc, proj_own, proj_got, fc_own, fc_got, proj, fc):
    for out, own, got in ((proj, proj_own, proj_got), (fc, fc_own, fc_got)):
        out[0] = own[...]
        out[1] = got[...]


def grow_kernel(sc, a, a_got, b, b_got, a_out, b_out):
    for own, got, out in ((a, a_got, a_out), (b, b_got, b_out)):
        count = own.shape[0]
        out[:count] = own[...]
        out[count:] = got[...]


def qkv_fold_kernel(sc, near, vec, near_got, far, far_got, near_kept, vec_out, near_sent, far_kept, far_sent):
    fold_into(near, near_got, near_kept, near_sent)
    both = added(vec[...], near_got[near.shape[0] :])
    near_sent[near.shape[0] // 2 :] = both
    vec_out[...] = both
    fold_into(far, far_got, far_kept, far_sent)


def qkv_meet_kernel(sc, near, vec, near_got, far, far_got, kept, vec_out, sent):
    rows, more = near.shape[0] // 2, far.shape[0] // 2
    kept[:rows] = added(near[:rows], near_got[:rows])
    sent[:rows] = added(near[rows:], near_got[rows : 2 * rows])
    kept[rows:] = added(far[:more], far_got[:more])
    sent[rows : rows + more] = added(far[more:], far_got[more:])
    both = added(vec[...], near_got[2 * rows :])
    sent[rows + more :] = both
    vec_out[...] = both


def qkv_last_kernel(sc, keep, vec, got, piece, vec_out):
    count = keep.shape[0]
    piece[...] = added(keep[...], got[:count])
    vec_out[...] = added(vec[...], got[count:])


def exchange_kernel(sc, piece, vec, s1, s2, s3):
    rows = s1.shape[0] - vec.shape[0]
    for k, sent in ((2, s2), (3, s3), (1, s1)):
        sent[:rows] = piece[k * rows : (k + 1) * rows]
        sent[rows:] = vec[...]


def qkv_part_kernel(sc, own, got, near, far):
    rows = near.shape[1]
    for i, ref in enumerate((own, got)):
        near[i] = ref[:rows]
        far[i] = ref[rows:]


VECTOR_ROWS = 12


def vector_place(row, block, width):
    at = row * WAYS + block
    return slice(at // 3, at // 3 + 1), slice((at % 3) * width, (at % 3 + 1) * width)


def join_kernel(sc, piece, vec, r1, r2, r3, joined, *rest):
    *mine, qv, fc, scratch = rest
    rows, width = r1.shape[0] - vec.shape[0], piece.shape[1] // 3
    joined[:rows] = piece[:rows]
    for i, got in ((1, r1), (2, r2), (3, r3)):
        joined[i * rows : (i + 1) * rows] = got[:rows]
    joined[WAYS * rows :] = piece[WAYS * rows :]
    scratch[...] = (
        vec[...].astype(F32)
        + r1[rows:].astype(F32)
        + r2[rows:].astype(F32)
        + r3[rows:].astype(F32)
    )
    for block in range(WAYS):

        @pl.when(sc[0] == block)
        def _(block=block):
            for row in range(6):
                mine[row][...] = scratch[vector_place(row, block, width)].reshape(width)
            for i in range(2):
                at = 2 * block + i
                qv[i * width : (i + 1) * width] = scratch[
                    vector_place(6 + at // WAYS, at % WAYS, width)
                ].reshape(width)
            for i in range(WAYS):
                fc[i * width : (i + 1) * width] = scratch[
                    vector_place(8 + block, i, width)
                ].reshape(width)


def small_kernel(sc, vectors, out, bias):
    width = out.shape[1]
    out[...] = jnp.zeros_like(out)
    length = sc[4]
    out[8:9, :] = jnp.full((1, width), length >> 6, jnp.int32).astype(BF16)
    out[9:10, :] = jnp.full((1, width), length & 63, jnp.int32).astype(BF16)
    for i in range(8):
        out[i : i + 1, :] = vectors[i * width : (i + 1) * width].reshape(1, width)
    bias[...] = vectors[8 * width :].reshape(bias.shape).astype(F32)


def table_kernel(sc, s0, s1, s2, s3, table, bias):
    width = s0.shape[1]
    table[7:8, :] = jnp.zeros((1, table.shape[1]), F32)
    bias[...] = jnp.zeros_like(bias)
    odd = (sc[0] & 1) == 1
    for k, ref in enumerate((s0, s1, s2, s3)):
        values = ref[...].astype(F32)
        j = sc[0] ^ k
        pair = jnp.where(odd, values[7:8], values[6:7])
        for block in range(WAYS):

            @pl.when(j == block)
            def _(values=values, block=block):
                table[0:6, block * width : (block + 1) * width] = values[0:6]

        @pl.when(j == (sc[0] >> 1))
        def _(pair=pair):
            bias[:, :width] = pair

        @pl.when(j == 2 + (sc[0] >> 1))
        def _(pair=pair):
            bias[:, 2 * width :] = pair

        @pl.when(j == sc[5])
        def _(values=values):
            row = values[8:9] * 64.0 + values[9:10]
            for block in range(WAYS):
                table[6:7, block * width : (block + 1) * width] = row


def half_of(sc, rows):
    return block_rows(sc[1] & 1, rows)


def qkv_columns_kernel(sc, weight, w0, w1, w2, w3):
    width = w0.shape[1] // 3
    half = half_of(sc, w2.shape[0])
    for k, ref in ((2, w2), (3, w3), (1, w1), (0, w0)):
        for block in range(WAYS):

            @pl.when((sc[0] ^ k) == block)
            def _(k=k, ref=ref, block=block):
                for part in range(3):
                    base = part * WAYS * width + block * width
                    source = weight[half if k > 1 else slice(None), base : base + width]
                    ref[:, part * width : (part + 1) * width] = source


def fc_columns_kernel(sc, weight, w0, w1, w2, w3):
    for k, ref in ((2, w2), (3, w3), (1, w1), (0, w0)):
        ref[...] = weight[:, block_rows(sc[0] ^ k, ref.shape[1])]


def assemble(sc, near, far, full):
    for k, ref in enumerate(near):
        full[block_rows(sc[0] ^ k, ref.shape[0]), :] = ref[...]
    mine = sc[1] & 1
    for k, halves in ((2, far[:2]), (3, far[2:])):
        for i, ref in enumerate(halves):
            full[block_rows((sc[0] ^ k) * 2 + (mine ^ i), ref.shape[0]), :] = ref[...]


def fetched(w0, w1, w2, w3):
    far2, far3 = f_xor(w2, 2), f_xor(w3, 3)
    return [w0, f_xor(w1, 1), far2, c_xor(far2, 1 << X), far3, c_xor(far3, 1 << X)]


def cot_kernel(sc, c0, c1, c2, c3, proj, table, g_out, pulled, bias_row):
    rows = c0.shape[0]
    for k, ref in enumerate((c0, c1, c2, c3)):
        j = sc[0] ^ k
        kept = jnp.where(valid_rows(sc, table, j, rows), ref[...].astype(F32), 0.0)
        if k == 0:
            bias_row[...] = jnp.sum(kept, axis=0, keepdims=True)
        low = kept.astype(BF16)
        g_out[member_rows(j, rows), :] = low
        pulled[member_rows(j, rows), :] = dot(low, proj[...], (1, 1))


def qkv_kernel(sc, x0, x1, x2, x3, w0, w1, w2, w2_x, w3, w3_x, table, bias, normed, scales, full, q, kv):
    rows = x0.shape[0]
    assemble(sc, (w0, w1), (w2, w2_x, w3, w3_x), full)
    for k, ref in enumerate((x0, x1, x2, x3)):
        place = member_rows(sc[0] ^ k, rows)
        scaled, _ = normalise(ref[...].astype(F32))
        low = (scaled * table[0:1, :] + table[1:2, :]).astype(BF16)
        normed[place, :] = low
        scales[place, :] = scaled.astype(BF16)
        got = (dot(low, full[...], (1, 0)) + bias[...]).astype(BF16)
        width = q.shape[1]
        q[place, :] = got[:, :width] * jnp.asarray(0.125, BF16)
        kv[place, :] = got[:, width:]


def in_parts(columns, rows, width):
    heads = len(columns)
    lane = lax.broadcasted_iota(jnp.int32, (rows, width), 1)
    value = jnp.zeros((rows, width), F32)
    for h, column in enumerate(columns):
        here = (lane == h) | (lane == heads + h) | (lane == 2 * heads + h)
        value = jnp.where(here, column, value)
    high = value.astype(BF16).astype(F32)
    rest = value - high
    mid = rest.astype(BF16).astype(F32)
    parts = jnp.where(lane < heads, high, jnp.where(lane < 2 * heads, mid, rest - mid))
    return parts.astype(BF16)


def from_parts(tail, heads):
    tail = tail.astype(F32)
    return (tail[:, :heads] + tail[:, heads : 2 * heads]) + tail[:, 2 * heads : 3 * heads]


def lanes(columns, rows, width, dtype):
    lane = lax.broadcasted_iota(jnp.int32, (rows, width), 1)
    out = jnp.zeros((rows, width), F32)
    for i, column in enumerate(columns):
        out = jnp.where(lane == i, column.astype(F32), out)
    return out.astype(dtype)


def threshold(sc, other):
    return jnp.where(other == sc[2], 0, jnp.where(other < sc[2], 1 << 20, -(1 << 20)))


def mask_last(values, allowed, other):
    rows = allowed.shape[1]
    masked = jnp.where(allowed, values[:, values.shape[1] - rows :], other)
    if values.shape[1] == rows:
        return masked
    return jnp.concatenate([values[:, : values.shape[1] - rows], masked], axis=1)


def attend(sc, step, first, last, refs):
    if first:
        q, kv = refs[:2]
        state_in = None
        rest = refs[2:]
    else:
        q, kv, acc_in, stat_in = refs[:4]
        rest = refs[4:]
    if last:
        out_w, attended, low, q_ext, own, far, sent, sent_own, scratch = rest
    else:
        acc_out, stat_out = rest
    total, width = q.shape
    rows = total // WAYS
    heads = width // HD
    limit = threshold(sc, sc[2] ^ step)
    ahead = lax.broadcasted_iota(jnp.int32, (rows, rows), 1) - lax.broadcasted_iota(
        jnp.int32, (rows, rows), 0
    )
    allowed = ahead <= limit
    for jq in range(WAYS):
        place = slice(jq * rows, (jq + 1) * rows)
        parts, tops, sums = [], [], []
        for h in range(heads):
            cols = slice(h * HD, (h + 1) * HD)
            vcols = slice(width + h * HD, width + (h + 1) * HD)
            qh = q[place, cols]
            keys = slice(0, (jq + 1) * rows)
            scores = dot(qh, kv[keys, cols], (1, 1))
            scores = mask_last(scores, allowed, NEGATIVE)
            top = jnp.max(scores, axis=-1, keepdims=True)
            if not first:
                old = stat_in[place, h : h + 1]
                top = jnp.maximum(top, old)
            weight = jnp.exp(scores - top)
            count = jnp.sum(weight, axis=-1, keepdims=True)
            acc = dot(weight.astype(BF16), kv[keys, vcols], (1, 0))
            if not first:
                shrink = jnp.exp(old - top)
                count = count + shrink * stat_in[place, heads + h : heads + h + 1]
                acc = acc + shrink * acc_in[place, cols]
            if last:
                acc = acc / count
                tops.append(top + jnp.log(count))
            else:
                tops.append(top)
                sums.append(count)
            parts.append(acc)
        joined_parts = jnp.concatenate(parts, axis=1)
        if last:
            attended[place, :] = joined_parts
            low_part = joined_parts.astype(BF16)
            low[place, :] = low_part
            scratch[place, :] = dot(low_part, out_w[...], (1, 0))
            q_ext[place, :width] = q[place, :]
            q_ext[place, width:] = in_parts(tops, rows, q_ext.shape[1] - width)
        else:
            acc_out[place, :] = joined_parts
            stat_out[place, :] = lanes(tops + sums, rows, stat_out.shape[1], F32)
    if last:
        emit_partials(sc, rows, scratch, own, far, sent, sent_own)


def second_norm_kernel(sc, own, got, far, x, table, residual, normed):
    value = (
        x[...].astype(F32)
        + own[...]
        + got[...].astype(F32)
        + far[...].astype(F32)
        + table[2:3, :]
    )
    residual[...] = value
    scaled, _ = normalise(value)
    normed[...] = (scaled * table[3:4, :] + table[4:5, :]).astype(BF16)


def assemble_kernel(sc, w0, w1, w2, w3, full):
    for k, ref in enumerate((w0, w1, w2, w3)):
        full[block_rows(sc[0] ^ k, ref.shape[0]), :] = ref[...]


def feed_kernel(
    sc, n0, n1, n2, n3, full, bias, pulled,
    normed, active, g_hidden, bias_row, own, far, sent, sent_own, scratch,
):
    rows = n0.shape[0]
    total = jnp.zeros_like(bias_row)
    for k, ref in enumerate((n0, n1, n2, n3)):
        place = member_rows(sc[0] ^ k, rows)
        normed[place, :] = ref[...]
        hidden = dot(ref[...], full[...], (1, 0)) + bias[...]
        square = hidden * hidden
        bend = jnp.tanh(GELU_COEF * (hidden + CUBE * hidden * square))
        active[place, :] = (0.5 * hidden * (1.0 + bend)).astype(BF16)
        slope = 0.5 * (1.0 + bend) + 0.5 * hidden * (1.0 - bend * bend) * (
            GELU_COEF * (1.0 + 3.0 * CUBE * square)
        )
        low = (pulled[place, :] * slope).astype(BF16)
        g_hidden[place, :] = low
        total = total + jnp.sum(low.astype(F32), axis=0, keepdims=True)
        scratch[place, :] = dot(low, full[...], (1, 1))
    bias_row[...] = total
    emit_partials(sc, rows, scratch, own, far, sent, sent_own)


def result_kernel(sc, active, proj, own, far, sent, sent_own, scratch):
    rows = active.shape[0] // WAYS
    scratch[...] = dot(active[...], proj[...], (1, 0))
    emit_partials(sc, rows, scratch, own, far, sent, sent_own)


def piece_of(sc, bits, slot):
    r = 0
    for i, bit in enumerate(bits):
        r |= ((slot >> (2 - i)) & 1) << bit
    return (sc[1] ^ r) & 7


def place_halves(keep, send):
    half = keep.shape[0]
    return [(slot, keep if slot < half else send, slot % half) for slot in range(2 * half)]


def tile_grad_kernel(bits, sc, active, g_out, keep, send, scratch):
    step_rows, step_cols = keep.shape[1], keep.shape[2]
    scratch[...] = dot(active[...], g_out[...], (0, 0)).astype(BF16)
    for slot, ref, at in place_halves(keep, send):
        piece = piece_of(sc, bits, slot)
        ref[at] = scratch[block_rows(piece >> 1, step_rows), block_rows(piece & 1, step_cols)]


def fc_grad_kernel(bits, sc, normed, g_hidden, keep, send, scratch):
    step_rows, step_cols = keep.shape[1], keep.shape[2]
    quarter = step_rows // WAYS
    scratch[...] = dot(normed[...], g_hidden[...], (0, 0)).astype(BF16)
    for slot, ref, at in place_halves(keep, send):
        piece = piece_of(sc, bits, slot)
        for k in range(WAYS):
            start = (sc[0] ^ k) * WAYS + (piece >> 1)
            ref[at, k * quarter : (k + 1) * quarter, :] = scratch[
                block_rows(start, quarter), block_rows(piece & 1, step_cols)
            ]


def second_back_kernel(sc, own, got, far, residual, cot, table, g_residual, g_branch, rows_out):
    upstream = own[...] + got[...].astype(F32) + far[...].astype(F32)
    scaled, inverse = normalise(residual[...])
    through = norm_back(upstream, scaled, inverse, table[3:4, :])
    g_out = jnp.where(valid_rows(sc, table, sc[0], cot.shape[0]), cot[...].astype(F32), 0.0)
    value = g_out + through
    g_residual[...] = value
    low = value.astype(BF16)
    g_branch[...] = low
    rows_out[0:1, :] = jnp.sum(upstream * scaled, axis=0, keepdims=True)
    rows_out[1:2, :] = jnp.sum(upstream, axis=0, keepdims=True)
    rows_out[2:3, :] = jnp.sum(low.astype(F32), axis=0, keepdims=True)


def pull_kernel(sc, b0, b1, b2, b3, out_w, attended, g_branch, do_ext):
    rows = b0.shape[0]
    width = attended.shape[1]
    heads = width // HD
    for k, ref in enumerate((b0, b1, b2, b3)):
        place = member_rows(sc[0] ^ k, rows)
        g_branch[place, :] = ref[...]
        low = dot(ref[...], out_w[...], (1, 1)).astype(BF16)
        product = low.astype(F32) * attended[place, :]
        sums = [
            jnp.sum(product[:, h * HD : (h + 1) * HD], axis=-1, keepdims=True) for h in range(heads)
        ]
        do_ext[place, :width] = low
        do_ext[place, width:] = in_parts(sums, rows, do_ext.shape[1] - width)


def pair_back(q, do, kv, allowed, g_q=None, g_kv=None, q_in=None):
    total = kv.shape[0]
    width = kv.shape[1] // 2
    rows = total // WAYS
    heads = width // HD
    for jq in range(WAYS):
        place = slice(jq * rows, (jq + 1) * rows)
        tops = from_parts(q[place, width:], heads)
        deltas = from_parts(do[place, width:], heads)
        for h in range(heads):
            cols = slice(h * HD, (h + 1) * HD)
            vcols = slice(width + h * HD, width + (h + 1) * HD)
            qh = q[place, cols]
            doh = do[place, cols]
            lse, delta = tops[:, h : h + 1], deltas[:, h : h + 1]
            keys = slice(0, (jq + 1) * rows)
            weight = jnp.exp(dot(qh, kv[keys, cols], (1, 1)) - lse)
            weight = mask_last(weight, allowed, 0.0)
            pulled = dot(doh, kv[keys, vcols], (1, 1))
            low = (weight * (pulled - delta)).astype(BF16)
            if g_q is not None:
                grad = dot(low, kv[keys, cols], (1, 0))
                if q_in is not None:
                    grad = grad + q_in[place, cols]
            if g_kv is not None:
                g_kv[keys, cols] += dot(low, qh, (0, 0))
                g_kv[keys, vcols] += dot(weight.astype(BF16), doh, (0, 0))
            if g_q is not None:
                g_q[place, cols] = grad


def ahead_of(rows):
    return lax.broadcasted_iota(jnp.int32, (rows, rows), 1) - lax.broadcasted_iota(
        jnp.int32, (rows, rows), 0
    )


def back_first(sc, q, do, kv, g_q, g_kv):
    g_kv[...] = jnp.zeros_like(g_kv)
    pair_back(q, do, kv, ahead_of(kv.shape[0] // WAYS) <= 0, g_q, g_kv)


def back_queries(sc, step, q, do, kv_other, q_in, g_q):
    limit = jnp.where((sc[2] ^ step) < sc[2], 1, -1)
    rows = kv_other.shape[0] // WAYS
    pair_back(q, do, kv_other, jnp.zeros((rows, rows), jnp.int32) <= limit, g_q=g_q, q_in=q_in)


def back_keys(sc, step, last, refs):
    q_other, do_other, kv, kv_in = refs[:4]
    if last:
        q_in, full, scales, g_proj, own, far, sent, sent_own, sums, g_kv, scratch = refs[4:]
    else:
        (g_kv,) = refs[4:]
    width = kv.shape[1] // 2
    rows = kv.shape[0] // WAYS
    limit = jnp.where(sc[2] < (sc[2] ^ step), 1, -1)
    g_kv[...] = kv_in[...]
    pair_back(q_other, do_other, kv, jnp.zeros((rows, rows), jnp.int32) <= limit, g_kv=g_kv)
    if last:
        g_proj[:, :width] = (q_in[...] * 0.125).astype(BF16)
        g_proj[:, width:] = g_kv[...].astype(BF16)
        scratch[...] = dot(g_proj[...], full[...], (1, 1))
        emit_partials(sc, rows, scratch, own, far, sent, sent_own)
        sums[0:1, :] = jnp.sum(scratch[...] * scales[...].astype(F32), axis=0, keepdims=True)
        sums[1:2, :] = jnp.sum(scratch[...], axis=0, keepdims=True)


def out_grad_kernel(bits, sc, attended, g_branch, slots, scratch):
    scratch[...] = dot(attended[...], g_branch[...], (0, 0)).astype(BF16)
    rows, cols = scratch.shape[0] // WAYS, scratch.shape[1] // 2
    tall, rest = 2 * rows // 3, rows // 3
    for slot in range(PIECES):
        piece = piece_of(sc, bits, slot)
        block = scratch[block_rows(piece >> 1, rows), block_rows(piece & 1, cols)]
        slots[slot, :, :cols] = block[:tall]
        slots[slot, :rest, cols:] = block[tall:, : cols // 2]
        slots[slot, rest:, cols:] = block[tall:, cols // 2 :]


def qkv_grad_kernel(
    near_bits, far_bits, sc, normed, g_proj, out, two, proj, fc, one, nk, ns, vec, wk, ws, scratch, rows_out
):
    half = PIECES // 2
    step = scratch.shape[0] // WAYS // PIECES
    width = nk.shape[1] // 3
    scratch[...] = dot(normed[...], g_proj[...], (0, 0))
    for base, bits, keep, send in ((2, far_bits, wk, ws), (0, near_bits, nk, ns)):
        size = keep.shape[0] // half
        for slot in range(PIECES):
            ref, at = (keep, slot) if slot < half else (send, slot - half)
            piece = piece_of(sc, bits, slot)
            for i in range(2):
                start = (sc[0] ^ (base + i)) * PIECES + piece
                ref[at * size + i * step : at * size + (i + 1) * step, :] = scratch[
                    block_rows(start, step), :
                ].astype(BF16)
            if base == 2:
                ref[at * size + 2 * step : (at + 1) * size, :] = out[slot]
    rows_out[0:2, :] = one[...]
    rows_out[2:3, :] = two[2:3, :]
    rows_out[3:5, :] = two[0:2, :]
    rows_out[5:6, :] = proj[...]
    rows_out[6:8, :] = jnp.zeros_like(rows_out[6:8, :])
    rows_out[8:12, :] = jnp.zeros_like(rows_out[8:12, :])
    total = jnp.sum(g_proj[...].astype(F32), axis=0, keepdims=True)
    for block in range(WAYS):

        @pl.when(sc[0] == block)
        def _(block=block):
            place = slice(block * width, (block + 1) * width)
            rows_out[6:7, place] = total[:, :width]
            rows_out[7:8, place] = total[:, 2 * width :]
            rows_out[8 + block : 9 + block, :] = fc[...]

    for row in range(VECTOR_ROWS):
        for block in range(WAYS):
            vec[vector_place(row, block, width)] = rows_out[
                row : row + 1, block * width : (block + 1) * width
            ].astype(BF16)
    ns[nk.shape[0] :, :] = vec[...]


def first_back_kernel(sc, own, got, far, x, table, g_residual, input_grad):
    upstream = own[...] + got[...].astype(F32) + far[...].astype(F32)
    scaled, inverse = normalise(x[...].astype(F32))
    through = norm_back(upstream, scaled, inverse, table[0:1, :])
    input_grad[0] = (g_residual[...] + through).astype(BF16)


def output_kernel(sc, own, got, far, residual, table, out):
    value = (
        residual[...] + own[...] + got[...].astype(F32) + far[...].astype(F32) + table[5:6, :]
    )
    out[0] = jnp.where(valid_rows(sc, table, sc[0], out.shape[1]), value, 0.0).astype(BF16)


def slots_in(near, far):
    half = near.shape[0]
    return [(slot, near if slot < half else far, slot % half) for slot in range(2 * half)]


def proj_final_kernel(bits, sc, near, far, out):
    rows, cols = near.shape[1:]
    for slot, ref, at in slots_in(near, far):
        piece = piece_of(sc, bits, slot)
        out[block_rows(piece >> 1, rows), block_rows(piece & 1, cols)] = ref[at].astype(F32)


def fc_final_kernel(bits, sc, near, far, tokens, out, tokens_out):
    tokens_out[...] = tokens[...]
    quarter, step_cols = near.shape[1] // WAYS, near.shape[2]
    for slot, ref, at in slots_in(near, far):
        piece = piece_of(sc, bits, slot)
        for k in range(WAYS):
            wide = block_rows((sc[0] ^ k) * 2 + (piece & 1), step_cols)
            out[block_rows(piece >> 1, quarter), wide] = ref[
                at, k * quarter : (k + 1) * quarter
            ].astype(F32)


def qkv_final_kernel(near_bits, far_bits, sc, nn, nf, wn, wf, tokens, out, out_out, tokens_out):
    tokens_out[...] = tokens[...]
    step, width = nn.shape[1] // 2, nn.shape[2] // 3
    cols = out_out.shape[1] // 2
    rows = out_out.shape[0] // WAYS
    tall, rest = 2 * rows // 3, rows // 3
    for slot, ref, at in slots_in(wn, wf):
        piece = piece_of(sc, far_bits, slot)
        block = ref[at, 2 * step :].astype(F32)
        start = (piece >> 1) * rows
        left = pl.ds(pl.multiple_of((piece & 1) * cols, cols), cols)
        low = pl.ds(pl.multiple_of(start, 8), tall)
        out_out[low, left] = block[:, :cols]
        high = pl.ds(pl.multiple_of(start + tall, 8), rest)
        out_out[high, left] = jnp.concatenate([block[:rest, cols:], block[rest:, cols:]], axis=1)
    for member in range(WAYS):

        @pl.when(sc[0] == member)
        def _(member=member):
            for base, bits, near, far in ((0, near_bits, nn, nf), (2, far_bits, wn, wf)):
                for slot, ref, at in slots_in(near, far):
                    place = block_rows(piece_of(sc, bits, slot), step)
                    for i in range(2):
                        piece = ref[at, i * step : (i + 1) * step].astype(F32)
                        for part in range(3):
                            start = (part * WAYS + (member ^ (base + i))) * width
                            out[place, start : start + width] = piece[
                                :, part * width : (part + 1) * width
                            ]


def body(
    inputs, lengths, ln1_gain, ln1_bias, qkv_weight, qv_bias, out_weight, out_bias,
    ln2_gain, ln2_bias, fc_weight, fc_bias, proj_weight, proj_bias, cotangent,
):
    group = lax.axis_size("ctx")
    members = group // WAYS
    assert lax.axis_size("fsdp") == WAYS and inputs.shape[0] == 1
    assert group % PIECES == 0 and group & (group - 1) == 0
    f, c = lax.axis_index("fsdp"), lax.axis_index("ctx")
    rows, width = inputs.shape[1:]
    head_width = width // WAYS
    hidden_width = fc_bias.shape[0]
    total = rows * WAYS
    half = PIECES // 2
    scalars = jnp.stack(
        [f, c, c % members, jnp.asarray(members), lengths[0], turned(c // members)]
    ).astype(jnp.int32)
    order = Order(scalars)

    vectors = [ln1_gain, ln1_bias, out_bias, ln2_gain, ln2_bias, proj_bias, qv_bias, fc_bias]
    w_qkv = order.call(
        qkv_columns_kernel,
        [shape((head_width // (1 + i // 2), 3 * head_width), BF16) for i in range(WAYS)],
        [qkv_weight],
        name="qkv_columns",
    )
    small, fc_row = order.call(
        small_kernel,
        [shape((16, head_width), BF16), shape((1, hidden_width), F32)],
        [jnp.concatenate(vectors)],
        name="small",
    )
    small_all = [small, f_xor(small, 1), f_xor(small, 2), f_xor(small, 3)]
    x_own = swap_layout(inputs[0])
    w_qkv = fetched(*w_qkv)
    x_far = f_xor(after(x_own, w_qkv[2], w_qkv[4], small), 2)
    x_all = [x_own, f_xor(x_own, 1), x_far, f_xor(x_far, 1)]
    cot_own = swap_layout(after(cotangent[0], x_far))
    table, qkv_bias = order.call(
        table_kernel,
        [shape((8, width), F32), shape((1, 3 * head_width), F32)],
        small_all,
        flops=4 * 10**9,
        name="table",
        late=[x_own, w_qkv[3], w_qkv[5]],
    )
    w_fc = order.call(
        fc_columns_kernel,
        [shape((head_width, hidden_width), BF16)] * WAYS,
        [fc_weight],
        name="fc_columns",
    )
    w_fc = [w_fc[0]] + [f_xor(w_fc[k], k) for k in range(1, WAYS)]

    normed_one, scales_one, qkv_full, q, kv = order.call(
        qkv_kernel,
        [
            shape((total, width), BF16),
            shape((total, width), BF16),
            shape((width, 3 * head_width), BF16),
            shape((total, head_width), BF16),
            shape((total, 2 * head_width), BF16),
        ],
        [*x_all, *w_qkv, table, qkv_bias],
        flops=2 * total * width * 3 * head_width,
        name="qkv",
    )
    kv_other = [kv] + [c_xor(kv, r) for r in range(1, members)]

    partials = [shape((rows, width), F32)] * 2 + [shape((rows, width), BF16)] * 2
    state = []
    for r in range(members):
        first, last = r == 0, r == members - 1
        if r == 1:
            cot_all = gather_f(after(cot_own, state[1]))
        if last:
            outs = [
                shape((total, head_width), F32),
                shape((total, head_width), BF16),
                shape((total, head_width + 64), BF16),
                *partials,
            ]
            scratch = [pltpu.VMEM((total, width), F32)]
            extra = [out_weight]
        else:
            outs = [shape((total, head_width), F32), shape((total, 128), F32)]
            scratch, extra = [], []

        def kernel(sc_ref, *refs, r=r, first=first, last=last):
            attend(sc_ref, r, first, last, refs)

        state = order.call(
            kernel,
            outs,
            [q, kv_other[r], *state, *extra],
            scratch,
            flops=4 * total * total * head_width,
            name=f"attend{min(r, 1)}",
        )
    attended, attended_low, q_ext, *branch = state
    branch = order.scatter_f(*branch)
    q_other = [q_ext] + [c_xor(q_ext, r) for r in range(1, members)]
    (fc_full,) = order.call(
        assemble_kernel,
        [shape((width, hidden_width), BF16)],
        w_fc,
        name="fc_assemble",
    )
    branch = order.scatter_f_far(branch)
    residual, normed_two = order.call(
        second_norm_kernel,
        [shape((rows, width), F32), shape((rows, width), BF16)],
        [*branch, x_own, table],
        name="norm2",
        late=[cot_all[2]],
    )
    normed_two_all = gather_f(normed_two)
    g_out, pulled, proj_row = order.call(
        cot_kernel,
        [
            shape((total, width), BF16),
            shape((total, hidden_width), F32),
            shape((1, width), F32),
        ],
        [*cot_all, proj_weight, table],
        flops=2 * total * width * hidden_width,
        name="cot",
    )
    normed_two_full, active, g_hidden, fc_rows, *g_two = order.call(
        feed_kernel,
        [
            shape((total, width), BF16),
            shape((total, hidden_width), BF16),
            shape((total, hidden_width), BF16),
            shape((1, hidden_width), F32),
            *partials,
        ],
        [*normed_two_all, fc_full, fc_row, pulled],
        [pltpu.VMEM((total, width), F32)],
        flops=4 * total * width * hidden_width,
        name="feed",
        late=q_other[1:],
    )
    g_two = order.scatter_f(*g_two)
    slots = [shape((half, head_width, width // 2), BF16)] * 2
    proj_keep, send = order.call(
        functools.partial(tile_grad_kernel, OTHER),
        slots,
        [active, g_out],
        [pltpu.VMEM((width, width), BF16)],
        flops=2 * total * width * hidden_width,
        name="proj_grad",
    )
    proj_got = c_xor(send, 1 << OTHER[0])
    g_two = order.scatter_f_far(g_two)
    fc_keep, send = order.call(
        functools.partial(fc_grad_kernel, ONE),
        slots,
        [normed_two_full, g_hidden],
        [pltpu.VMEM((width, width), BF16)],
        flops=2 * total * width * hidden_width,
        name="fc_grad",
    )
    fc_got = c_xor(send, 1 << ONE[0])
    result = order.call(
        result_kernel,
        partials,
        [active, proj_weight],
        [pltpu.VMEM((total, width), F32)],
        flops=2 * total * width * hidden_width,
        name="result",
    )
    result = order.scatter_f(*result)
    g_residual, g_branch, two_rows = order.call(
        second_back_kernel,
        [shape((rows, width), F32), shape((rows, width), BF16), shape((3, width), F32)],
        [*g_two, residual, cot_own, table],
        name="norm2_back",
    )
    g_branch_all = gather_f(g_branch)
    result = order.scatter_f_far(result)
    g_branch_full, do_ext = order.call(
        pull_kernel,
        [shape((total, width), BF16), shape((total, head_width + 64), BF16)],
        [*g_branch_all, out_weight, attended],
        flops=2 * total * width * head_width,
        name="pull",
    )
    do_other = [do_ext] + [c_xor(do_ext, r) for r in range(1, members)]
    step = head_width // PIECES
    out_rows = head_width // 6
    (out_slots,) = order.call(
        functools.partial(out_grad_kernel, ONE),
        [shape((PIECES, out_rows, 3 * head_width), BF16)],
        [attended_low, g_branch_full],
        [pltpu.VMEM((head_width, width), BF16)],
        flops=2 * total * width * head_width,
        name="out_grad",
    )
    tile = (head_width, width // 2)
    proj_keep, proj_send, fc_keep, fc_send = order.call(
        mlp_fold_kernel,
        [shape((2, *tile), BF16)] * 4,
        [proj_keep, proj_got, fc_keep, fc_got],
        name="mlp_fold",
    )
    proj_got, fc_got = c_xor(proj_send, 1 << OTHER[1]), c_xor(fc_send, 1 << ONE[1])
    (outputs,) = order.call(
        output_kernel, [shape((1, rows, width), BF16)], [*result, residual, table], name="output"
    )
    outputs = swap_layout(outputs)
    g_q, g_kv = order.call(
        back_first,
        [shape((total, head_width), F32), shape((total, 2 * head_width), F32)],
        [q_ext, do_ext, kv],
        flops=10 * total * total * head_width,
        name="back0",
    )
    mlp_keep, mlp_send = order.call(
        mlp_meet_kernel,
        [shape((2, *tile), BF16)] * 2,
        [proj_keep, proj_got, fc_keep, fc_got],
        name="mlp_meet",
        late=[outputs],
    )
    mlp_got = c_xor(mlp_send, 1 << Z2)
    for r in range(1, members):

        def kernel(sc_ref, *refs, r=r):
            back_queries(sc_ref, r, *refs)

        (g_q,) = order.call(
            kernel,
            [shape(g_q.shape, F32)],
            [q_ext, do_ext, kv_other[r], g_q],
            flops=6 * total * total * head_width,
            name="back_q",
        )
    for r in range(1, members):
        last = r == members - 1
        outs, scratch, extra = [shape(g_kv.shape, F32)], [], []
        if last:
            scratch = [pltpu.VMEM(g_kv.shape, F32), pltpu.VMEM((total, width), F32)]
            outs = [shape((total, 3 * head_width), BF16), *partials, shape((2, width), F32)]
            extra = [g_q, qkv_full, scales_one]

        def kernel(sc_ref, *refs, r=r, last=last):
            back_keys(sc_ref, r, last, refs)

        grads = order.call(
            kernel,
            outs,
            [q_other[r], do_other[r], kv, g_kv, *extra],
            scratch,
            flops=8 * total * total * head_width,
            name="back_kv",
        )
        g_kv = grads[0]
    g_proj, *g_one, one_rows = grads
    g_one = order.scatter_f(*g_one)
    near_rows, far_rows, vec_rows, cols = 2 * step, 2 * step + out_rows, 16, 3 * head_width
    near_keep, near_send, vec, far_keep, far_send = order.call(
        functools.partial(qkv_grad_kernel, OTHER, ONE),
        [
            shape((half * near_rows, cols), BF16),
            shape((half * near_rows + vec_rows, cols), BF16),
            shape((vec_rows, cols), BF16),
            shape((half * far_rows, cols), BF16),
            shape((half * far_rows, cols), BF16),
        ],
        [normed_one, g_proj, out_slots, two_rows, proj_row, fc_rows, one_rows],
        [pltpu.VMEM((width, cols), F32), pltpu.VMEM((VECTOR_ROWS, width), F32)],
        flops=2 * total * width * cols,
        name="qkv_grad",
    )
    near_got, far_got = c_xor(near_send, 1 << OTHER[0]), c_xor(far_send, 1 << ONE[0])
    quarter = head_width // WAYS
    pieces = order.call(
        mlp_last_kernel,
        [shape(tile, BF16)] + [shape((quarter, tile[1]), BF16)] * WAYS,
        [mlp_keep, mlp_got],
        name="mlp_last",
    )
    proj_piece, *fc_pieces = [others(piece) for piece in pieces]
    proj_got = c_xor(proj_piece, 1 << Z2)
    fc_pieces = [fc_pieces[0]] + [f_xor(fc_pieces[k], k) for k in range(1, WAYS)]
    g_one = order.scatter_f_far(g_one)
    (fc_piece,) = order.call(
        mlp_join_kernel, [shape(tile, BF16)], fc_pieces, name="mlp_join"
    )
    fc_got = c_xor(fc_piece, 1 << Z2)
    near_keep, vec, near_send, far_keep, far_send = order.call(
        qkv_fold_kernel,
        [
            shape((2 * near_rows, cols), BF16),
            shape((vec_rows, cols), BF16),
            shape((2 * near_rows + vec_rows, cols), BF16),
            shape((2 * far_rows, cols), BF16),
            shape((2 * far_rows, cols), BF16),
        ],
        [near_keep, vec, near_got, far_keep, far_got],
        name="qkv_fold",
        late=[proj_got],
    )
    near_got, far_got = c_xor(near_send, 1 << OTHER[1]), c_xor(far_send, 1 << ONE[1])
    (input_grad,) = order.call(
        first_back_kernel,
        [shape((1, rows, width), BF16)],
        [*g_one, x_own, table, g_residual],
        name="norm1_back",
    )
    input_grad = swap_layout(input_grad)
    keep, vec, send = order.call(
        qkv_meet_kernel,
        [
            shape((near_rows + far_rows, cols), BF16),
            shape((vec_rows, cols), BF16),
            shape((near_rows + far_rows + vec_rows, cols), BF16),
        ],
        [near_keep, vec, near_got, far_keep, far_got],
        name="qkv_meet",
        late=[fc_got],
    )
    got = c_xor(send, 1 << Z2)
    proj_own, fc_own = order.call(
        mlp_part_kernel,
        [shape((2, *tile), BF16)] * 2,
        [proj_piece, proj_got, fc_piece, fc_got],
        name="mlp_part",
    )
    proj_got, fc_got = c_xor(proj_own, 1 << OTHER[1]), c_xor(fc_own, 1 << ONE[1])
    piece, vec = order.call(
        qkv_last_kernel,
        [shape((near_rows + far_rows, cols), BF16), shape((vec_rows, cols), BF16)],
        [keep, vec, got],
        flops=4 * 10**9,
        name="qkv_last",
    )
    piece, vec = others(piece), others(vec)
    s1, s2, s3 = order.call(
        exchange_kernel,
        [shape((step + vec_rows, cols), BF16)] * 3,
        [piece, vec],
        flops=4 * 10**9,
        name="exchange",
    )
    r2, r3, r1 = f_xor(s2, 2), f_xor(s3, 3), f_xor(s1, 1)
    proj_own, fc_own = order.call(
        grow_kernel,
        [shape((half, *tile), BF16)] * 2,
        [proj_own, proj_got, fc_own, fc_got],
        name="mlp_grow",
    )
    proj_got, fc_got = c_xor(proj_own, 1 << OTHER[0]), c_xor(fc_own, 1 << ONE[0])
    joined, *mine, grad_qv, grad_fc_bias = order.call(
        join_kernel,
        [
            shape((near_rows + far_rows, cols), BF16),
            *[shape((head_width,), F32)] * 6,
            shape((2 * head_width,), F32),
            shape((hidden_width,), F32),
        ],
        [piece, vec, r1, r2, r3],
        [pltpu.VMEM((vec_rows, cols), F32)],
        name="join",
    )
    got = c_xor(joined, 1 << Z2)
    near_own, far_own = order.call(
        qkv_part_kernel,
        [shape((2, near_rows, cols), BF16), shape((2, far_rows, cols), BF16)],
        [joined, got],
        name="qkv_part",
    )
    near_got, far_got = c_xor(near_own, 1 << OTHER[1]), c_xor(far_own, 1 << ONE[1])
    def finish(kernel, dims, arrays, name, tokens=None):
        outs = [shape(d, F32) for d in dims]
        if tokens is not None:
            outs.append(shape(tokens.shape, BF16))
            arrays = [*arrays, tokens]
        return order.call(kernel, outs, arrays, name=name, direct=True)

    grad_fc, outputs = finish(
        functools.partial(fc_final_kernel, ONE),
        [(head_width, WAYS * hidden_width)],
        [fc_own, fc_got],
        "fc_final",
        outputs,
    )
    (grad_proj,) = finish(
        functools.partial(proj_final_kernel, OTHER),
        [(hidden_width, width)],
        [proj_own, proj_got],
        "proj_final",
    )
    near_own, far_own = order.call(
        grow_kernel,
        [shape((half, near_rows, cols), BF16), shape((half, far_rows, cols), BF16)],
        [near_own, near_got, far_own, far_got],
        name="qkv_grow",
    )
    near_got, far_got = c_xor(near_own, 1 << OTHER[0]), c_xor(far_own, 1 << ONE[0])

    grad_qkv, grad_out, input_grad = finish(
        functools.partial(qkv_final_kernel, OTHER, ONE),
        [(head_width, 3 * width), (head_width, width)],
        [near_own, near_got, far_own, far_got],
        "qkv_final",
        input_grad,
    )
    return (
        outputs,
        input_grad,
        mine[0],
        mine[1],
        grad_qkv,
        grad_qv,
        grad_out,
        mine[2],
        mine[3],
        mine[4],
        grad_fc,
        grad_fc_bias,
        grad_proj,
        mine[5],
    )


def solution(mesh):
    tokens, rows, vector = P("fsdp", "ctx", None), P("fsdp", None), P("fsdp")
    in_specs = (
        tokens, vector, vector, vector, rows, vector, rows, vector,
        vector, vector, rows, vector, rows, vector, tokens,
    )
    out_specs = (
        tokens, tokens, vector, vector, rows, vector, rows, vector,
        vector, vector, rows, vector, rows, vector,
    )
    return jax.shard_map(body, mesh=mesh, in_specs=in_specs, out_specs=out_specs, check_vma=False)
```

```python
import functools

import jax
import jax.numpy as jnp
from jax import lax
from jax.experimental import pallas as pl
from jax.experimental.pallas import tpu as pltpu
from jax.sharding import PartitionSpec as P

HD = 64
EPSILON = 1e-05
NEGATIVE = -1e30
GELU_COEF = 0.7978845608028654
CUBE = 0.044715
F32 = jnp.float32
BF16 = jnp.bfloat16
WAYS = 4
PIECES = 8
VMEM_LIMIT = 24 * 1024 * 1024


def f_xor(x, k):
    n = lax.axis_size("fsdp")
    return lax.ppermute(x, "fsdp", [(i, i ^ k) for i in range(n)])


def c_xor(x, k):
    n = lax.axis_size("ctx")
    return lax.ppermute(x, "ctx", [(i, i ^ k) for i in range(n)])


def turned(index):
    return ((index & 1) << 1) | (index >> 1)


def swap_layout(x):
    group = lax.axis_size("ctx")
    members = group // WAYS
    perm = []
    for f in range(WAYS):
        for c in range(group):
            j, m = divmod(c, members)
            perm.append((f * group + c, turned(j) * group + turned(f) * members + m))
    return lax.ppermute(x, ("fsdp", "ctx"), perm)


def after(value, *others):
    return lax.optimization_barrier((value, *others))[0]


def gather_f(x, until=lambda far: far):
    far = f_xor(x, 2)
    near = f_xor(x, 1)
    return [x, near, far, f_xor(until(far), 1)]


class Order:
    def __init__(self, scalars):
        self.scalars = scalars
        self.token = None

    def tie(self, value):
        if self.token is None:
            return value
        return lax.optimization_barrier((value, self.token))[0]

    def mark(self, value):
        self.token = value
        return value

    def call(self, kernel, outs, args, scratch=(), flops=0, name=None, direct=False, late=()):
        scalars = after(self.tie(self.scalars), *late)
        got = call(kernel, outs, [scalars, *args], scratch, flops, name, direct)
        self.mark(min(got, key=lambda value: value.size))
        return got

    def scatter_f(self, kept_own, kept_far, sent_far, sent_own):
        return kept_own, kept_far, f_xor(sent_far, 1), f_xor(sent_own, 1)

    def scatter_f_far(self, state, late=()):
        kept_own, kept_far, got_far, got_own = state
        (far,) = self.call(
            far_kernel, [shape(kept_own.shape, BF16)], [kept_far, got_far], name="far", late=late
        )
        return kept_own, got_own, f_xor(far, 2)


X, Z1, Z2 = 0, 1, 2
ONE, OTHER = (X, Z1, Z2), (Z1, X, Z2)


def others(value):
    bit = 3
    while (1 << bit) < lax.axis_size("ctx"):
        value = (value.astype(F32) + c_xor(value, 1 << bit).astype(F32)).astype(BF16)
        bit += 1
    return value


def call(kernel, outs, args, scratch=(), flops=0, name=None, direct=False):
    vmem = pl.BlockSpec(memory_space=pltpu.VMEM)
    moved = sum(a.size * a.dtype.itemsize for a in args) + sum(
        o.size * o.dtype.itemsize for o in outs
    )
    return pl.pallas_call(
        kernel,
        out_shape=tuple(outs),
        in_specs=[pl.BlockSpec(memory_space=pltpu.SMEM)] + [vmem] * (len(args) - 1),
        out_specs=tuple([pl.BlockSpec() if direct else vmem] * len(outs)),
        scratch_shapes=list(scratch),
        cost_estimate=pl.CostEstimate(flops=flops, bytes_accessed=moved, transcendentals=0),
        compiler_params=pltpu.CompilerParams(vmem_limit_bytes=VMEM_LIMIT),
        name=name,
    )(*args)


def shape(dims, dtype):
    return jax.ShapeDtypeStruct(dims, dtype)


def dot(a, b, contract):
    return lax.dot_general(a, b, ((contract[0:1], contract[1:2]), ((), ())), preferred_element_type=F32)


def block_rows(index, size):
    return pl.ds(pl.multiple_of(index * size, size), size)


def member_rows(member, size):
    return block_rows(turned(member), size)


def normalise(values):
    centred = values - jnp.mean(values, axis=-1, keepdims=True)
    inverse = lax.rsqrt(jnp.mean(centred * centred, axis=-1, keepdims=True) + EPSILON)
    return centred * inverse, inverse


def norm_back(upstream, scaled, inverse, gain):
    weighted = upstream * gain
    return inverse * (
        weighted
        - jnp.mean(weighted, axis=-1, keepdims=True)
        - scaled * jnp.mean(weighted * scaled, axis=-1, keepdims=True)
    )


def valid_rows(sc, table, chunk, rows):
    place = (turned(chunk) * sc[3] + sc[2]) * rows + lax.broadcasted_iota(jnp.int32, (rows, 1), 0)
    return place.astype(F32) < table[6:7, 0:1]


def emit_partials(sc, rows, value_ref, own_ref, far_ref, sent_far, sent_own):
    f = sc[0]
    own_ref[...] = value_ref[member_rows(f, rows), :]
    far_ref[...] = value_ref[member_rows(f ^ 2, rows), :]
    sent_own[...] = value_ref[member_rows(f ^ 1, rows), :].astype(BF16)
    sent_far[...] = value_ref[member_rows(f ^ 3, rows), :].astype(BF16)


def far_kernel(sc, kept, got, out):
    out[...] = (kept[...] + got[...].astype(F32)).astype(BF16)


def added(a, b):
    return (a.astype(F32) + b.astype(F32)).astype(BF16)


def fold_into(keep, got, kept, sent):
    half = keep.shape[0] // 2
    sent[:half] = added(keep[half:], got[half : 2 * half])
    kept[...] = added(keep[:half], got[:half])


def mlp_fold_kernel(sc, proj, proj_got, fc, fc_got, proj_kept, proj_sent, fc_kept, fc_sent):
    fold_into(proj, proj_got, proj_kept, proj_sent)
    fold_into(fc, fc_got, fc_kept, fc_sent)


def mlp_meet_kernel(sc, proj, proj_got, fc, fc_got, kept, sent):
    for i, (keep, got) in enumerate(((proj, proj_got), (fc, fc_got))):
        kept[i] = added(keep[0], got[0])
        sent[i] = added(keep[1], got[1])


def mlp_last_kernel(sc, keep, got, proj, *pieces):
    proj[...] = added(keep[0], got[0])
    rows = pieces[0].shape[0]
    for i, piece in enumerate(pieces):
        place = slice(i * rows, (i + 1) * rows)
        piece[...] = added(keep[1, place], got[1, place])


def mlp_join_kernel(sc, p0, p1, p2, p3, out):
    rows = p0.shape[0]
    for i, piece in enumerate((p0, p1, p2, p3)):
        out[i * rows : (i + 1) * rows] = piece[...]


def mlp_part_kernel(sc, proj_own, proj_got, fc_own, fc_got, proj, fc):
    for out, own, got in ((proj, proj_own, proj_got), (fc, fc_own, fc_got)):
        out[0] = own[...]
        out[1] = got[...]


def grow_kernel(sc, a, a_got, b, b_got, a_out, b_out):
    for own, got, out in ((a, a_got, a_out), (b, b_got, b_out)):
        count = own.shape[0]
        out[:count] = own[...]
        out[count:] = got[...]


def qkv_fold_kernel(sc, near, vec, near_got, far, far_got, near_kept, vec_out, near_sent, far_kept, far_sent):
    fold_into(near, near_got, near_kept, near_sent)
    both = added(vec[...], near_got[near.shape[0] :])
    near_sent[near.shape[0] // 2 :] = both
    vec_out[...] = both
    fold_into(far, far_got, far_kept, far_sent)


def qkv_meet_kernel(sc, near, vec, near_got, far, far_got, kept, vec_out, sent):
    rows, more = near.shape[0] // 2, far.shape[0] // 2
    kept[:rows] = added(near[:rows], near_got[:rows])
    sent[:rows] = added(near[rows:], near_got[rows : 2 * rows])
    kept[rows:] = added(far[:more], far_got[:more])
    sent[rows : rows + more] = added(far[more:], far_got[more:])
    both = added(vec[...], near_got[2 * rows :])
    sent[rows + more :] = both
    vec_out[...] = both


def qkv_last_kernel(sc, keep, vec, got, piece, vec_out):
    count = keep.shape[0]
    piece[...] = added(keep[...], got[:count])
    vec_out[...] = added(vec[...], got[count:])


def exchange_kernel(sc, piece, vec, s1, s2, s3):
    rows = s1.shape[0] - vec.shape[0]
    for k, sent in ((2, s2), (3, s3), (1, s1)):
        sent[:rows] = piece[k * rows : (k + 1) * rows]
        sent[rows:] = vec[...]


def qkv_part_kernel(sc, own, got, near, far):
    rows = near.shape[1]
    for i, ref in enumerate((own, got)):
        near[i] = ref[:rows]
        far[i] = ref[rows:]


VECTOR_ROWS = 12


def vector_place(row, block, width):
    at = row * WAYS + block
    return slice(at // 3, at // 3 + 1), slice((at % 3) * width, (at % 3 + 1) * width)


def join_kernel(sc, piece, vec, r1, r2, r3, joined, *rest):
    *mine, qv, fc, scratch = rest
    rows, width = r1.shape[0] - vec.shape[0], piece.shape[1] // 3
    joined[:rows] = piece[:rows]
    for i, got in ((1, r1), (2, r2), (3, r3)):
        joined[i * rows : (i + 1) * rows] = got[:rows]
    joined[WAYS * rows :] = piece[WAYS * rows :]
    scratch[...] = (
        vec[...].astype(F32)
        + r1[rows:].astype(F32)
        + r2[rows:].astype(F32)
        + r3[rows:].astype(F32)
    )
    for block in range(WAYS):

        @pl.when(sc[0] == block)
        def _(block=block):
            for row in range(6):
                mine[row][...] = scratch[vector_place(row, block, width)].reshape(width)
            for i in range(2):
                at = 2 * block + i
                qv[i * width : (i + 1) * width] = scratch[
                    vector_place(6 + at // WAYS, at % WAYS, width)
                ].reshape(width)
            for i in range(WAYS):
                fc[i * width : (i + 1) * width] = scratch[
                    vector_place(8 + block, i, width)
                ].reshape(width)


def small_kernel(sc, vectors, out, bias):
    width = out.shape[1]
    out[...] = jnp.zeros_like(out)
    length = sc[4]
    out[8:9, :] = jnp.full((1, width), length >> 6, jnp.int32).astype(BF16)
    out[9:10, :] = jnp.full((1, width), length & 63, jnp.int32).astype(BF16)
    for i in range(8):
        out[i : i + 1, :] = vectors[i * width : (i + 1) * width].reshape(1, width)
    bias[...] = vectors[8 * width :].reshape(bias.shape).astype(F32)


def table_kernel(sc, s0, s1, s2, s3, table, bias):
    width = s0.shape[1]
    table[7:8, :] = jnp.zeros((1, table.shape[1]), F32)
    bias[...] = jnp.zeros_like(bias)
    odd = (sc[0] & 1) == 1
    for k, ref in enumerate((s0, s1, s2, s3)):
        values = ref[...].astype(F32)
        j = sc[0] ^ k
        pair = jnp.where(odd, values[7:8], values[6:7])
        for block in range(WAYS):

            @pl.when(j == block)
            def _(values=values, block=block):
                table[0:6, block * width : (block + 1) * width] = values[0:6]

        @pl.when(j == (sc[0] >> 1))
        def _(pair=pair):
            bias[:, :width] = pair

        @pl.when(j == 2 + (sc[0] >> 1))
        def _(pair=pair):
            bias[:, 2 * width :] = pair

        @pl.when(j == sc[5])
        def _(values=values):
            row = values[8:9] * 64.0 + values[9:10]
            for block in range(WAYS):
                table[6:7, block * width : (block + 1) * width] = row


def half_of(sc, rows):
    return block_rows(sc[1] & 1, rows)


def qkv_columns_kernel(sc, weight, w0, w1, w2, w3):
    width = w0.shape[1] // 3
    half = half_of(sc, w2.shape[0])
    for k, ref in ((2, w2), (3, w3), (1, w1), (0, w0)):
        for block in range(WAYS):

            @pl.when((sc[0] ^ k) == block)
            def _(k=k, ref=ref, block=block):
                for part in range(3):
                    base = part * WAYS * width + block * width
                    source = weight[half if k > 1 else slice(None), base : base + width]
                    ref[:, part * width : (part + 1) * width] = source


def fc_columns_kernel(sc, weight, w0, w1, w2, w3):
    for k, ref in ((2, w2), (3, w3), (1, w1), (0, w0)):
        ref[...] = weight[:, block_rows(sc[0] ^ k, ref.shape[1])]


def assemble(sc, near, far, full):
    for k, ref in enumerate(near):
        full[block_rows(sc[0] ^ k, ref.shape[0]), :] = ref[...]
    mine = sc[1] & 1
    for k, halves in ((2, far[:2]), (3, far[2:])):
        for i, ref in enumerate(halves):
            full[block_rows((sc[0] ^ k) * 2 + (mine ^ i), ref.shape[0]), :] = ref[...]


def fetched(w0, w1, w2, w3):
    far2, far3 = f_xor(w2, 2), f_xor(w3, 3)
    return [w0, f_xor(w1, 1), far2, c_xor(far2, 1 << X), far3, c_xor(far3, 1 << X)]


def cot_kernel(sc, c0, c1, c2, c3, proj, table, g_out, pulled, bias_row):
    rows = c0.shape[0]
    for k, ref in enumerate((c0, c1, c2, c3)):
        j = sc[0] ^ k
        kept = jnp.where(valid_rows(sc, table, j, rows), ref[...].astype(F32), 0.0)
        if k == 0:
            bias_row[...] = jnp.sum(kept, axis=0, keepdims=True)
        low = kept.astype(BF16)
        g_out[member_rows(j, rows), :] = low
        pulled[member_rows(j, rows), :] = dot(low, proj[...], (1, 1))


def qkv_kernel(sc, x0, x1, x2, x3, w0, w1, w2, w2_x, w3, w3_x, table, bias, normed, scales, full, q, kv):
    rows = x0.shape[0]
    assemble(sc, (w0, w1), (w2, w2_x, w3, w3_x), full)
    for k, ref in enumerate((x0, x1, x2, x3)):
        place = member_rows(sc[0] ^ k, rows)
        scaled, _ = normalise(ref[...].astype(F32))
        low = (scaled * table[0:1, :] + table[1:2, :]).astype(BF16)
        normed[place, :] = low
        scales[place, :] = scaled.astype(BF16)
        got = (dot(low, full[...], (1, 0)) + bias[...]).astype(BF16)
        width = q.shape[1]
        q[place, :] = got[:, :width] * jnp.asarray(0.125, BF16)
        kv[place, :] = got[:, width:]


def in_parts(columns, rows, width):
    heads = len(columns)
    lane = lax.broadcasted_iota(jnp.int32, (rows, width), 1)
    value = jnp.zeros((rows, width), F32)
    for h, column in enumerate(columns):
        here = (lane == h) | (lane == heads + h) | (lane == 2 * heads + h)
        value = jnp.where(here, column, value)
    high = value.astype(BF16).astype(F32)
    rest = value - high
    mid = rest.astype(BF16).astype(F32)
    parts = jnp.where(lane < heads, high, jnp.where(lane < 2 * heads, mid, rest - mid))
    return parts.astype(BF16)


def from_parts(tail, heads):
    tail = tail.astype(F32)
    return (tail[:, :heads] + tail[:, heads : 2 * heads]) + tail[:, 2 * heads : 3 * heads]


def lanes(columns, rows, width, dtype):
    lane = lax.broadcasted_iota(jnp.int32, (rows, width), 1)
    out = jnp.zeros((rows, width), F32)
    for i, column in enumerate(columns):
        out = jnp.where(lane == i, column.astype(F32), out)
    return out.astype(dtype)


def threshold(sc, other):
    return jnp.where(other == sc[2], 0, jnp.where(other < sc[2], 1 << 20, -(1 << 20)))


def mask_last(values, allowed, other):
    rows = allowed.shape[1]
    masked = jnp.where(allowed, values[:, values.shape[1] - rows :], other)
    if values.shape[1] == rows:
        return masked
    return jnp.concatenate([values[:, : values.shape[1] - rows], masked], axis=1)


def attend(sc, step, first, last, refs):
    if first:
        q, kv = refs[:2]
        state_in = None
        rest = refs[2:]
    else:
        q, kv, acc_in, stat_in = refs[:4]
        rest = refs[4:]
    if last:
        out_w, attended, low, q_ext, own, far, sent, sent_own, scratch = rest
    else:
        acc_out, stat_out = rest
    total, width = q.shape
    rows = total // WAYS
    heads = width // HD
    limit = threshold(sc, sc[2] ^ step)
    ahead = lax.broadcasted_iota(jnp.int32, (rows, rows), 1) - lax.broadcasted_iota(
        jnp.int32, (rows, rows), 0
    )
    allowed = ahead <= limit
    for jq in range(WAYS):
        place = slice(jq * rows, (jq + 1) * rows)
        parts, tops, sums = [], [], []
        for h in range(heads):
            cols = slice(h * HD, (h + 1) * HD)
            vcols = slice(width + h * HD, width + (h + 1) * HD)
            qh = q[place, cols]
            keys = slice(0, (jq + 1) * rows)
            scores = dot(qh, kv[keys, cols], (1, 1))
            scores = mask_last(scores, allowed, NEGATIVE)
            top = jnp.max(scores, axis=-1, keepdims=True)
            if not first:
                old = stat_in[place, h : h + 1]
                top = jnp.maximum(top, old)
            weight = jnp.exp(scores - top)
            count = jnp.sum(weight, axis=-1, keepdims=True)
            acc = dot(weight.astype(BF16), kv[keys, vcols], (1, 0))
            if not first:
                shrink = jnp.exp(old - top)
                count = count + shrink * stat_in[place, heads + h : heads + h + 1]
                acc = acc + shrink * acc_in[place, cols]
            if last:
                acc = acc / count
                tops.append(top + jnp.log(count))
            else:
                tops.append(top)
                sums.append(count)
            parts.append(acc)
        joined_parts = jnp.concatenate(parts, axis=1)
        if last:
            attended[place, :] = joined_parts
            low_part = joined_parts.astype(BF16)
            low[place, :] = low_part
            scratch[place, :] = dot(low_part, out_w[...], (1, 0))
            q_ext[place, :width] = q[place, :]
            q_ext[place, width:] = in_parts(tops, rows, q_ext.shape[1] - width)
        else:
            acc_out[place, :] = joined_parts
            stat_out[place, :] = lanes(tops + sums, rows, stat_out.shape[1], F32)
    if last:
        emit_partials(sc, rows, scratch, own, far, sent, sent_own)


def second_norm_kernel(sc, own, got, far, x, table, residual, normed):
    value = (
        x[...].astype(F32)
        + own[...]
        + got[...].astype(F32)
        + far[...].astype(F32)
        + table[2:3, :]
    )
    residual[...] = value
    scaled, _ = normalise(value)
    normed[...] = (scaled * table[3:4, :] + table[4:5, :]).astype(BF16)


def assemble_kernel(sc, w0, w1, w2, w3, full):
    for k, ref in enumerate((w0, w1, w2, w3)):
        full[block_rows(sc[0] ^ k, ref.shape[0]), :] = ref[...]


def feed_kernel(
    sc, n0, n1, n2, n3, full, bias, pulled,
    normed, active, g_hidden, bias_row, own, far, sent, sent_own, scratch,
):
    rows = n0.shape[0]
    total = jnp.zeros_like(bias_row)
    for k, ref in enumerate((n0, n1, n2, n3)):
        place = member_rows(sc[0] ^ k, rows)
        normed[place, :] = ref[...]
        hidden = dot(ref[...], full[...], (1, 0)) + bias[...]
        square = hidden * hidden
        bend = jnp.tanh(GELU_COEF * (hidden + CUBE * hidden * square))
        active[place, :] = (0.5 * hidden * (1.0 + bend)).astype(BF16)
        slope = 0.5 * (1.0 + bend) + 0.5 * hidden * (1.0 - bend * bend) * (
            GELU_COEF * (1.0 + 3.0 * CUBE * square)
        )
        low = (pulled[place, :] * slope).astype(BF16)
        g_hidden[place, :] = low
        total = total + jnp.sum(low.astype(F32), axis=0, keepdims=True)
        scratch[place, :] = dot(low, full[...], (1, 1))
    bias_row[...] = total
    emit_partials(sc, rows, scratch, own, far, sent, sent_own)


def result_kernel(sc, active, proj, own, far, sent, sent_own, scratch):
    rows = active.shape[0] // WAYS
    scratch[...] = dot(active[...], proj[...], (1, 0))
    emit_partials(sc, rows, scratch, own, far, sent, sent_own)


def piece_of(sc, bits, slot):
    r = 0
    for i, bit in enumerate(bits):
        r |= ((slot >> (2 - i)) & 1) << bit
    return (sc[1] ^ r) & 7


def place_halves(keep, send):
    half = keep.shape[0]
    return [(slot, keep if slot < half else send, slot % half) for slot in range(2 * half)]


def tile_grad_kernel(bits, sc, active, g_out, keep, send, scratch):
    step_rows, step_cols = keep.shape[1], keep.shape[2]
    scratch[...] = dot(active[...], g_out[...], (0, 0)).astype(BF16)
    for slot, ref, at in place_halves(keep, send):
        piece = piece_of(sc, bits, slot)
        ref[at] = scratch[block_rows(piece >> 1, step_rows), block_rows(piece & 1, step_cols)]


def fc_grad_kernel(bits, sc, normed, g_hidden, keep, send, scratch):
    step_rows, step_cols = keep.shape[1], keep.shape[2]
    quarter = step_rows // WAYS
    scratch[...] = dot(normed[...], g_hidden[...], (0, 0)).astype(BF16)
    for slot, ref, at in place_halves(keep, send):
        piece = piece_of(sc, bits, slot)
        for k in range(WAYS):
            start = (sc[0] ^ k) * WAYS + (piece >> 1)
            ref[at, k * quarter : (k + 1) * quarter, :] = scratch[
                block_rows(start, quarter), block_rows(piece & 1, step_cols)
            ]


def second_back_kernel(sc, own, got, far, residual, cot, table, g_residual, g_branch, rows_out):
    upstream = own[...] + got[...].astype(F32) + far[...].astype(F32)
    scaled, inverse = normalise(residual[...])
    through = norm_back(upstream, scaled, inverse, table[3:4, :])
    g_out = jnp.where(valid_rows(sc, table, sc[0], cot.shape[0]), cot[...].astype(F32), 0.0)
    value = g_out + through
    g_residual[...] = value
    low = value.astype(BF16)
    g_branch[...] = low
    rows_out[0:1, :] = jnp.sum(upstream * scaled, axis=0, keepdims=True)
    rows_out[1:2, :] = jnp.sum(upstream, axis=0, keepdims=True)
    rows_out[2:3, :] = jnp.sum(low.astype(F32), axis=0, keepdims=True)


def pull_kernel(sc, b0, b1, b2, b3, out_w, attended, g_branch, do_ext):
    rows = b0.shape[0]
    width = attended.shape[1]
    heads = width // HD
    for k, ref in enumerate((b0, b1, b2, b3)):
        place = member_rows(sc[0] ^ k, rows)
        g_branch[place, :] = ref[...]
        low = dot(ref[...], out_w[...], (1, 1)).astype(BF16)
        product = low.astype(F32) * attended[place, :]
        sums = [
            jnp.sum(product[:, h * HD : (h + 1) * HD], axis=-1, keepdims=True) for h in range(heads)
        ]
        do_ext[place, :width] = low
        do_ext[place, width:] = in_parts(sums, rows, do_ext.shape[1] - width)


def pair_back(q, do, kv, allowed, g_q=None, g_kv=None, q_in=None):
    total = kv.shape[0]
    width = kv.shape[1] // 2
    rows = total // WAYS
    heads = width // HD
    for jq in range(WAYS):
        place = slice(jq * rows, (jq + 1) * rows)
        tops = from_parts(q[place, width:], heads)
        deltas = from_parts(do[place, width:], heads)
        for h in range(heads):
            cols = slice(h * HD, (h + 1) * HD)
            vcols = slice(width + h * HD, width + (h + 1) * HD)
            qh = q[place, cols]
            doh = do[place, cols]
            lse, delta = tops[:, h : h + 1], deltas[:, h : h + 1]
            keys = slice(0, (jq + 1) * rows)
            weight = jnp.exp(dot(qh, kv[keys, cols], (1, 1)) - lse)
            weight = mask_last(weight, allowed, 0.0)
            pulled = dot(doh, kv[keys, vcols], (1, 1))
            low = (weight * (pulled - delta)).astype(BF16)
            if g_q is not None:
                grad = dot(low, kv[keys, cols], (1, 0))
                if q_in is not None:
                    grad = grad + q_in[place, cols]
            if g_kv is not None:
                g_kv[keys, cols] += dot(low, qh, (0, 0))
                g_kv[keys, vcols] += dot(weight.astype(BF16), doh, (0, 0))
            if g_q is not None:
                g_q[place, cols] = grad


def ahead_of(rows):
    return lax.broadcasted_iota(jnp.int32, (rows, rows), 1) - lax.broadcasted_iota(
        jnp.int32, (rows, rows), 0
    )


def back_first(sc, q, do, kv, g_q, g_kv):
    g_kv[...] = jnp.zeros_like(g_kv)
    pair_back(q, do, kv, ahead_of(kv.shape[0] // WAYS) <= 0, g_q, g_kv)


def back_queries(sc, step, q, do, kv_other, q_in, g_q):
    limit = jnp.where((sc[2] ^ step) < sc[2], 1, -1)
    rows = kv_other.shape[0] // WAYS
    pair_back(q, do, kv_other, jnp.zeros((rows, rows), jnp.int32) <= limit, g_q=g_q, q_in=q_in)


def back_keys(sc, step, last, refs):
    q_other, do_other, kv, kv_in = refs[:4]
    if last:
        q_in, full, scales, g_proj, own, far, sent, sent_own, sums, g_kv, scratch = refs[4:]
    else:
        (g_kv,) = refs[4:]
    width = kv.shape[1] // 2
    rows = kv.shape[0] // WAYS
    limit = jnp.where(sc[2] < (sc[2] ^ step), 1, -1)
    g_kv[...] = kv_in[...]
    pair_back(q_other, do_other, kv, jnp.zeros((rows, rows), jnp.int32) <= limit, g_kv=g_kv)
    if last:
        g_proj[:, :width] = (q_in[...] * 0.125).astype(BF16)
        g_proj[:, width:] = g_kv[...].astype(BF16)
        scratch[...] = dot(g_proj[...], full[...], (1, 1))
        emit_partials(sc, rows, scratch, own, far, sent, sent_own)
        sums[0:1, :] = jnp.sum(scratch[...] * scales[...].astype(F32), axis=0, keepdims=True)
        sums[1:2, :] = jnp.sum(scratch[...], axis=0, keepdims=True)


def out_grad_kernel(bits, sc, attended, g_branch, slots, scratch):
    scratch[...] = dot(attended[...], g_branch[...], (0, 0)).astype(BF16)
    rows, cols = scratch.shape[0] // WAYS, scratch.shape[1] // 2
    tall, rest = 2 * rows // 3, rows // 3
    for slot in range(PIECES):
        piece = piece_of(sc, bits, slot)
        block = scratch[block_rows(piece >> 1, rows), block_rows(piece & 1, cols)]
        slots[slot, :, :cols] = block[:tall]
        slots[slot, :rest, cols:] = block[tall:, : cols // 2]
        slots[slot, rest:, cols:] = block[tall:, cols // 2 :]


def qkv_grad_kernel(
    near_bits, far_bits, sc, normed, g_proj, out, two, proj, fc, one, nk, ns, vec, wk, ws, scratch, rows_out
):
    half = PIECES // 2
    step = scratch.shape[0] // WAYS // PIECES
    width = nk.shape[1] // 3
    scratch[...] = dot(normed[...], g_proj[...], (0, 0))
    for base, bits, keep, send in ((2, far_bits, wk, ws), (0, near_bits, nk, ns)):
        size = keep.shape[0] // half
        for slot in range(PIECES):
            ref, at = (keep, slot) if slot < half else (send, slot - half)
            piece = piece_of(sc, bits, slot)
            for i in range(2):
                start = (sc[0] ^ (base + i)) * PIECES + piece
                ref[at * size + i * step : at * size + (i + 1) * step, :] = scratch[
                    block_rows(start, step), :
                ].astype(BF16)
            if base == 2:
                ref[at * size + 2 * step : (at + 1) * size, :] = out[slot]
    rows_out[0:2, :] = one[...]
    rows_out[2:3, :] = two[2:3, :]
    rows_out[3:5, :] = two[0:2, :]
    rows_out[5:6, :] = proj[...]
    rows_out[6:8, :] = jnp.zeros_like(rows_out[6:8, :])
    rows_out[8:12, :] = jnp.zeros_like(rows_out[8:12, :])
    total = jnp.sum(g_proj[...].astype(F32), axis=0, keepdims=True)
    for block in range(WAYS):

        @pl.when(sc[0] == block)
        def _(block=block):
            place = slice(block * width, (block + 1) * width)
            rows_out[6:7, place] = total[:, :width]
            rows_out[7:8, place] = total[:, 2 * width :]
            rows_out[8 + block : 9 + block, :] = fc[...]

    for row in range(VECTOR_ROWS):
        for block in range(WAYS):
            vec[vector_place(row, block, width)] = rows_out[
                row : row + 1, block * width : (block + 1) * width
            ].astype(BF16)
    ns[nk.shape[0] :, :] = vec[...]


def first_back_kernel(sc, own, got, far, x, table, g_residual, input_grad):
    upstream = own[...] + got[...].astype(F32) + far[...].astype(F32)
    scaled, inverse = normalise(x[...].astype(F32))
    through = norm_back(upstream, scaled, inverse, table[0:1, :])
    input_grad[0] = (g_residual[...] + through).astype(BF16)


def output_kernel(sc, own, got, far, residual, table, out):
    value = (
        residual[...] + own[...] + got[...].astype(F32) + far[...].astype(F32) + table[5:6, :]
    )
    out[0] = jnp.where(valid_rows(sc, table, sc[0], out.shape[1]), value, 0.0).astype(BF16)


def slots_in(near, far):
    half = near.shape[0]
    return [(slot, near if slot < half else far, slot % half) for slot in range(2 * half)]


def proj_final_kernel(bits, sc, near, far, out):
    rows, cols = near.shape[1:]
    for slot, ref, at in slots_in(near, far):
        piece = piece_of(sc, bits, slot)
        out[block_rows(piece >> 1, rows), block_rows(piece & 1, cols)] = ref[at].astype(F32)


def fc_final_kernel(bits, sc, near, far, tokens, out, tokens_out):
    tokens_out[...] = tokens[...]
    quarter, step_cols = near.shape[1] // WAYS, near.shape[2]
    for slot, ref, at in slots_in(near, far):
        piece = piece_of(sc, bits, slot)
        for k in range(WAYS):
            wide = block_rows((sc[0] ^ k) * 2 + (piece & 1), step_cols)
            out[block_rows(piece >> 1, quarter), wide] = ref[
                at, k * quarter : (k + 1) * quarter
            ].astype(F32)


def qkv_final_kernel(near_bits, far_bits, sc, nn, nf, wn, wf, tokens, out, out_out, tokens_out):
    tokens_out[...] = tokens[...]
    step, width = nn.shape[1] // 2, nn.shape[2] // 3
    cols = out_out.shape[1] // 2
    rows = out_out.shape[0] // WAYS
    tall, rest = 2 * rows // 3, rows // 3
    for slot, ref, at in slots_in(wn, wf):
        piece = piece_of(sc, far_bits, slot)
        block = ref[at, 2 * step :].astype(F32)
        start = (piece >> 1) * rows
        left = pl.ds(pl.multiple_of((piece & 1) * cols, cols), cols)
        low = pl.ds(pl.multiple_of(start, 8), tall)
        out_out[low, left] = block[:, :cols]
        high = pl.ds(pl.multiple_of(start + tall, 8), rest)
        out_out[high, left] = jnp.concatenate([block[:rest, cols:], block[rest:, cols:]], axis=1)
    for member in range(WAYS):

        @pl.when(sc[0] == member)
        def _(member=member):
            for base, bits, near, far in ((0, near_bits, nn, nf), (2, far_bits, wn, wf)):
                for slot, ref, at in slots_in(near, far):
                    place = block_rows(piece_of(sc, bits, slot), step)
                    for i in range(2):
                        piece = ref[at, i * step : (i + 1) * step].astype(F32)
                        for part in range(3):
                            start = (part * WAYS + (member ^ (base + i))) * width
                            out[place, start : start + width] = piece[
                                :, part * width : (part + 1) * width
                            ]


def body(
    inputs, lengths, ln1_gain, ln1_bias, qkv_weight, qv_bias, out_weight, out_bias,
    ln2_gain, ln2_bias, fc_weight, fc_bias, proj_weight, proj_bias, cotangent,
):
    group = lax.axis_size("ctx")
    members = group // WAYS
    assert lax.axis_size("fsdp") == WAYS and inputs.shape[0] == 1
    assert group % PIECES == 0 and group & (group - 1) == 0
    f, c = lax.axis_index("fsdp"), lax.axis_index("ctx")
    rows, width = inputs.shape[1:]
    head_width = width // WAYS
    hidden_width = fc_bias.shape[0]
    total = rows * WAYS
    half = PIECES // 2
    scalars = jnp.stack(
        [f, c, c % members, jnp.asarray(members), lengths[0], turned(c // members)]
    ).astype(jnp.int32)
    order = Order(scalars)

    vectors = [ln1_gain, ln1_bias, out_bias, ln2_gain, ln2_bias, proj_bias, qv_bias, fc_bias]
    w_qkv = order.call(
        qkv_columns_kernel,
        [shape((head_width // (1 + i // 2), 3 * head_width), BF16) for i in range(WAYS)],
        [qkv_weight],
        name="qkv_columns",
    )
    small, fc_row = order.call(
        small_kernel,
        [shape((16, head_width), BF16), shape((1, hidden_width), F32)],
        [jnp.concatenate(vectors)],
        name="small",
    )
    small_all = [small, f_xor(small, 1), f_xor(small, 2), f_xor(small, 3)]
    x_own = swap_layout(inputs[0])
    w_qkv = fetched(*w_qkv)
    x_far = f_xor(after(x_own, w_qkv[2], w_qkv[4], small), 2)
    x_all = [x_own, f_xor(x_own, 1), x_far, f_xor(x_far, 1)]
    cot_own = swap_layout(after(cotangent[0], x_far))
    table, qkv_bias = order.call(
        table_kernel,
        [shape((8, width), F32), shape((1, 3 * head_width), F32)],
        small_all,
        flops=4 * 10**9,
        name="table",
        late=[x_own, w_qkv[3], w_qkv[5]],
    )
    w_fc = order.call(
        fc_columns_kernel,
        [shape((head_width, hidden_width), BF16)] * WAYS,
        [fc_weight],
        name="fc_columns",
    )
    w_fc = [w_fc[0]] + [f_xor(w_fc[k], k) for k in range(1, WAYS)]

    normed_one, scales_one, qkv_full, q, kv = order.call(
        qkv_kernel,
        [
            shape((total, width), BF16),
            shape((total, width), BF16),
            shape((width, 3 * head_width), BF16),
            shape((total, head_width), BF16),
            shape((total, 2 * head_width), BF16),
        ],
        [*x_all, *w_qkv, table, qkv_bias],
        flops=2 * total * width * 3 * head_width,
        name="qkv",
    )
    kv_other = [kv] + [c_xor(kv, r) for r in range(1, members)]

    partials = [shape((rows, width), F32)] * 2 + [shape((rows, width), BF16)] * 2
    state = []
    for r in range(members):
        first, last = r == 0, r == members - 1
        if r == 1:
            cot_all = gather_f(after(cot_own, state[1]))
        if last:
            outs = [
                shape((total, head_width), F32),
                shape((total, head_width), BF16),
                shape((total, head_width + 64), BF16),
                *partials,
            ]
            scratch = [pltpu.VMEM((total, width), F32)]
            extra = [out_weight]
        else:
            outs = [shape((total, head_width), F32), shape((total, 128), F32)]
            scratch, extra = [], []

        def kernel(sc_ref, *refs, r=r, first=first, last=last):
            attend(sc_ref, r, first, last, refs)

        state = order.call(
            kernel,
            outs,
            [q, kv_other[r], *state, *extra],
            scratch,
            flops=4 * total * total * head_width,
            name=f"attend{min(r, 1)}",
        )
    attended, attended_low, q_ext, *branch = state
    branch = order.scatter_f(*branch)
    q_other = [q_ext] + [c_xor(q_ext, r) for r in range(1, members)]
    (fc_full,) = order.call(
        assemble_kernel,
        [shape((width, hidden_width), BF16)],
        w_fc,
        name="fc_assemble",
    )
    branch = order.scatter_f_far(branch)
    residual, normed_two = order.call(
        second_norm_kernel,
        [shape((rows, width), F32), shape((rows, width), BF16)],
        [*branch, x_own, table],
        name="norm2",
        late=[cot_all[2]],
    )
    normed_two_all = gather_f(normed_two)
    g_out, pulled, proj_row = order.call(
        cot_kernel,
        [
            shape((total, width), BF16),
            shape((total, hidden_width), F32),
            shape((1, width), F32),
        ],
        [*cot_all, proj_weight, table],
        flops=2 * total * width * hidden_width,
        name="cot",
    )
    normed_two_full, active, g_hidden, fc_rows, *g_two = order.call(
        feed_kernel,
        [
            shape((total, width), BF16),
            shape((total, hidden_width), BF16),
            shape((total, hidden_width), BF16),
            shape((1, hidden_width), F32),
            *partials,
        ],
        [*normed_two_all, fc_full, fc_row, pulled],
        [pltpu.VMEM((total, width), F32)],
        flops=4 * total * width * hidden_width,
        name="feed",
        late=q_other[1:],
    )
    g_two = order.scatter_f(*g_two)
    slots = [shape((half, head_width, width // 2), BF16)] * 2
    proj_keep, send = order.call(
        functools.partial(tile_grad_kernel, OTHER),
        slots,
        [active, g_out],
        [pltpu.VMEM((width, width), BF16)],
        flops=2 * total * width * hidden_width,
        name="proj_grad",
    )
    proj_got = c_xor(send, 1 << OTHER[0])
    g_two = order.scatter_f_far(g_two)
    fc_keep, send = order.call(
        functools.partial(fc_grad_kernel, ONE),
        slots,
        [normed_two_full, g_hidden],
        [pltpu.VMEM((width, width), BF16)],
        flops=2 * total * width * hidden_width,
        name="fc_grad",
    )
    fc_got = c_xor(send, 1 << ONE[0])
    result = order.call(
        result_kernel,
        partials,
        [active, proj_weight],
        [pltpu.VMEM((total, width), F32)],
        flops=2 * total * width * hidden_width,
        name="result",
    )
    result = order.scatter_f(*result)
    g_residual, g_branch, two_rows = order.call(
        second_back_kernel,
        [shape((rows, width), F32), shape((rows, width), BF16), shape((3, width), F32)],
        [*g_two, residual, cot_own, table],
        name="norm2_back",
    )
    g_branch_all = gather_f(g_branch)
    result = order.scatter_f_far(result)
    g_branch_full, do_ext = order.call(
        pull_kernel,
        [shape((total, width), BF16), shape((total, head_width + 64), BF16)],
        [*g_branch_all, out_weight, attended],
        flops=2 * total * width * head_width,
        name="pull",
    )
    do_other = [do_ext] + [c_xor(do_ext, r) for r in range(1, members)]
    step = head_width // PIECES
    out_rows = head_width // 6
    (out_slots,) = order.call(
        functools.partial(out_grad_kernel, ONE),
        [shape((PIECES, out_rows, 3 * head_width), BF16)],
        [attended_low, g_branch_full],
        [pltpu.VMEM((head_width, width), BF16)],
        flops=2 * total * width * head_width,
        name="out_grad",
    )
    tile = (head_width, width // 2)
    proj_keep, proj_send, fc_keep, fc_send = order.call(
        mlp_fold_kernel,
        [shape((2, *tile), BF16)] * 4,
        [proj_keep, proj_got, fc_keep, fc_got],
        name="mlp_fold",
    )
    proj_got, fc_got = c_xor(proj_send, 1 << OTHER[1]), c_xor(fc_send, 1 << ONE[1])
    (outputs,) = order.call(
        output_kernel, [shape((1, rows, width), BF16)], [*result, residual, table], name="output"
    )
    outputs = swap_layout(outputs)
    g_q, g_kv = order.call(
        back_first,
        [shape((total, head_width), F32), shape((total, 2 * head_width), F32)],
        [q_ext, do_ext, kv],
        flops=10 * total * total * head_width,
        name="back0",
    )
    mlp_keep, mlp_send = order.call(
        mlp_meet_kernel,
        [shape((2, *tile), BF16)] * 2,
        [proj_keep, proj_got, fc_keep, fc_got],
        name="mlp_meet",
        late=[outputs],
    )
    mlp_got = c_xor(mlp_send, 1 << Z2)
    for r in range(1, members):

        def kernel(sc_ref, *refs, r=r):
            back_queries(sc_ref, r, *refs)

        (g_q,) = order.call(
            kernel,
            [shape(g_q.shape, F32)],
            [q_ext, do_ext, kv_other[r], g_q],
            flops=6 * total * total * head_width,
            name="back_q",
        )
    for r in range(1, members):
        last = r == members - 1
        outs, scratch, extra = [shape(g_kv.shape, F32)], [], []
        if last:
            scratch = [pltpu.VMEM(g_kv.shape, F32), pltpu.VMEM((total, width), F32)]
            outs = [shape((total, 3 * head_width), BF16), *partials, shape((2, width), F32)]
            extra = [g_q, qkv_full, scales_one]

        def kernel(sc_ref, *refs, r=r, last=last):
            back_keys(sc_ref, r, last, refs)

        grads = order.call(
            kernel,
            outs,
            [q_other[r], do_other[r], kv, g_kv, *extra],
            scratch,
            flops=8 * total * total * head_width,
            name="back_kv",
        )
        g_kv = grads[0]
    g_proj, *g_one, one_rows = grads
    g_one = order.scatter_f(*g_one)
    near_rows, far_rows, vec_rows, cols = 2 * step, 2 * step + out_rows, 16, 3 * head_width
    near_keep, near_send, vec, far_keep, far_send = order.call(
        functools.partial(qkv_grad_kernel, OTHER, ONE),
        [
            shape((half * near_rows, cols), BF16),
            shape((half * near_rows + vec_rows, cols), BF16),
            shape((vec_rows, cols), BF16),
            shape((half * far_rows, cols), BF16),
            shape((half * far_rows, cols), BF16),
        ],
        [normed_one, g_proj, out_slots, two_rows, proj_row, fc_rows, one_rows],
        [pltpu.VMEM((width, cols), F32), pltpu.VMEM((VECTOR_ROWS, width), F32)],
        flops=2 * total * width * cols,
        name="qkv_grad",
    )
    near_got, far_got = c_xor(near_send, 1 << OTHER[0]), c_xor(far_send, 1 << ONE[0])
    quarter = head_width // WAYS
    pieces = order.call(
        mlp_last_kernel,
        [shape(tile, BF16)] + [shape((quarter, tile[1]), BF16)] * WAYS,
        [mlp_keep, mlp_got],
        name="mlp_last",
    )
    proj_piece, *fc_pieces = [others(piece) for piece in pieces]
    proj_got = c_xor(proj_piece, 1 << Z2)
    fc_pieces = [fc_pieces[0]] + [f_xor(fc_pieces[k], k) for k in range(1, WAYS)]
    g_one = order.scatter_f_far(g_one)
    (fc_piece,) = order.call(
        mlp_join_kernel, [shape(tile, BF16)], fc_pieces, name="mlp_join"
    )
    fc_got = c_xor(fc_piece, 1 << Z2)
    near_keep, vec, near_send, far_keep, far_send = order.call(
        qkv_fold_kernel,
        [
            shape((2 * near_rows, cols), BF16),
            shape((vec_rows, cols), BF16),
            shape((2 * near_rows + vec_rows, cols), BF16),
            shape((2 * far_rows, cols), BF16),
            shape((2 * far_rows, cols), BF16),
        ],
        [near_keep, vec, near_got, far_keep, far_got],
        name="qkv_fold",
        late=[proj_got],
    )
    near_got, far_got = c_xor(near_send, 1 << OTHER[1]), c_xor(far_send, 1 << ONE[1])
    (input_grad,) = order.call(
        first_back_kernel,
        [shape((1, rows, width), BF16)],
        [*g_one, x_own, table, g_residual],
        name="norm1_back",
    )
    input_grad = swap_layout(input_grad)
    keep, vec, send = order.call(
        qkv_meet_kernel,
        [
            shape((near_rows + far_rows, cols), BF16),
            shape((vec_rows, cols), BF16),
            shape((near_rows + far_rows + vec_rows, cols), BF16),
        ],
        [near_keep, vec, near_got, far_keep, far_got],
        name="qkv_meet",
        late=[fc_got],
    )
    got = c_xor(send, 1 << Z2)
    proj_own, fc_own = order.call(
        mlp_part_kernel,
        [shape((2, *tile), BF16)] * 2,
        [proj_piece, proj_got, fc_piece, fc_got],
        name="mlp_part",
    )
    proj_got, fc_got = c_xor(proj_own, 1 << OTHER[1]), c_xor(fc_own, 1 << ONE[1])
    piece, vec = order.call(
        qkv_last_kernel,
        [shape((near_rows + far_rows, cols), BF16), shape((vec_rows, cols), BF16)],
        [keep, vec, got],
        flops=4 * 10**9,
        name="qkv_last",
    )
    piece, vec = others(piece), others(vec)
    s1, s2, s3 = order.call(
        exchange_kernel,
        [shape((step + vec_rows, cols), BF16)] * 3,
        [piece, vec],
        flops=4 * 10**9,
        name="exchange",
    )
    r2, r3, r1 = f_xor(s2, 2), f_xor(s3, 3), f_xor(s1, 1)
    proj_own, fc_own = order.call(
        grow_kernel,
        [shape((half, *tile), BF16)] * 2,
        [proj_own, proj_got, fc_own, fc_got],
        name="mlp_grow",
    )
    proj_got, fc_got = c_xor(proj_own, 1 << OTHER[0]), c_xor(fc_own, 1 << ONE[0])
    joined, *mine, grad_qv, grad_fc_bias = order.call(
        join_kernel,
        [
            shape((near_rows + far_rows, cols), BF16),
            *[shape((head_width,), F32)] * 6,
            shape((2 * head_width,), F32),
            shape((hidden_width,), F32),
        ],
        [piece, vec, r1, r2, r3],
        [pltpu.VMEM((vec_rows, cols), F32)],
        name="join",
    )
    got = c_xor(joined, 1 << Z2)
    near_own, far_own = order.call(
        qkv_part_kernel,
        [shape((2, near_rows, cols), BF16), shape((2, far_rows, cols), BF16)],
        [joined, got],
        name="qkv_part",
    )
    near_got, far_got = c_xor(near_own, 1 << OTHER[1]), c_xor(far_own, 1 << ONE[1])
    def finish(kernel, dims, arrays, name, tokens=None):
        outs = [shape(d, F32) for d in dims]
        if tokens is not None:
            outs.append(shape(tokens.shape, BF16))
            arrays = [*arrays, tokens]
        return order.call(kernel, outs, arrays, name=name, direct=True)

    grad_fc, outputs = finish(
        functools.partial(fc_final_kernel, ONE),
        [(head_width, WAYS * hidden_width)],
        [fc_own, fc_got],
        "fc_final",
        outputs,
    )
    near_own, far_own = order.call(
        grow_kernel,
        [shape((half, near_rows, cols), BF16), shape((half, far_rows, cols), BF16)],
        [near_own, near_got, far_own, far_got],
        name="qkv_grow",
    )
    near_got, far_got = c_xor(near_own, 1 << OTHER[0]), c_xor(far_own, 1 << ONE[0])

    (grad_proj,) = finish(
        functools.partial(proj_final_kernel, OTHER),
        [(hidden_width, width)],
        [proj_own, proj_got],
        "proj_final",
    )
    grad_qkv, grad_out, input_grad = finish(
        functools.partial(qkv_final_kernel, OTHER, ONE),
        [(head_width, 3 * width), (head_width, width)],
        [near_own, near_got, far_own, far_got],
        "qkv_final",
        input_grad,
    )
    return (
        outputs,
        input_grad,
        mine[0],
        mine[1],
        grad_qkv,
        grad_qv,
        grad_out,
        mine[2],
        mine[3],
        mine[4],
        grad_fc,
        grad_fc_bias,
        grad_proj,
        mine[5],
    )


def solution(mesh):
    tokens, rows, vector = P("fsdp", "ctx", None), P("fsdp", None), P("fsdp")
    in_specs = (
        tokens, vector, vector, vector, rows, vector, rows, vector,
        vector, vector, rows, vector, rows, vector, tokens,
    )
    out_specs = (
        tokens, tokens, vector, vector, rows, vector, rows, vector,
        vector, vector, rows, vector, rows, vector,
    )
    return jax.shard_map(body, mesh=mesh, in_specs=in_specs, out_specs=out_specs, check_vma=False)
```
